512 devices in a mesh: rot: 4 (over y), tile: 64 (over x_lo, z, core), nar: 2 (over x_hi).
Axes of the slice: x: 4 (x_hi: 2, x_lo: 2; x = x_hi * 2 + x_lo), y: 4, z: 16, core: 2. Of those that a mesh axis runs over, the one named last changes fastest.
Arguments:
- interp_index: int32 [8, 8, 2, 192, 384], P(None, 'rot', 'nar', 'tile'), may hold values from 0 to 4095
- interp_weight: bfloat16 [8, 8, 2, 192, 384], P(None, 'rot', 'nar', 'tile'), may hold values from 0 to 0.25
- volume: bfloat16 [2, 2, 64, 4096], P(None, 'nar', 'tile'), may hold values from -6 to 6
- spectrum: bfloat16 [2, 64, 2, 192, 384], P(None, 'tile', 'nar'), may hold values from -6 to 6
- ctf_filter: bfloat16 [64, 2, 192, 384], P('tile', 'nar'), may hold values from -1 to 1
- peak_count: int32 [4, 64], P('rot', 'tile'), may hold values from 1 to 4, 129 in all within a row
- peak_orient: int32 [1024], P(('rot', 'tile')), may hold values from 0 to 1
- peak_row: int32 [1024], P(('rot', 'tile')), may hold values from 0 to 383
- peak_col: int32 [1024], P(('rot', 'tile')), may hold values from 0 to 383
- ctf_grid: bfloat16 [512, 2, 18432], P('tile', 'nar'), may hold values from -1 to 1
Outputs:
- peak_max: float32 [64, 2, 73728], P('tile', 'nar')
- peak_mean: float32 [64, 2, 73728], P('tile', 'nar')
- refined: float32 [4, 256, 512], P('rot', None, 'tile')
- best: float32 [4, 256], P('rot')
The draws below stay inside these ranges and needn't reach their ends.
Inputs may be any that keep to these rules, and one draw needn't show every extreme that they name: `peak_count`: in each orientation group the counts over all tiles sum to 129, and some tile has exactly 4.
All inputs are finite; a program needn't handle non-finite values.
Results may differ from the reference program's by a relative error of at most 0.013.
Values may be sent and summed in bfloat16 or wider, within the bound.
No kernel may reach another device: no remote copies, remote signals or barrier semaphores. Data moves between devices by JAX's collectives and lax.ppermute only.
A program may use at most 64 MiB of HBM per device.

```python
import math
import jax
import jax.numpy as jnp
import numpy as np
from jax import lax

TL = 384
K = 8
VOX = 4096
ORI = 2
MOST = 4
HALF = 192
SROWS = 3
BINS = 18432
ORIENTS = 8
PTOTAL = 129
PEAKS = 1024
DEFOCI = 512
N_ROT = 4
N_TILE = 64
N_NAR = 2


def set_ends(entries, stream_key, low, largest):
    place = [jax.random.randint(jax.random.fold_in(stream_key, axis), (), 0, length) for axis, length in enumerate(entries.shape)]
    main_axis = entries.shape.index(max(entries.shape))
    next_to = place[:main_axis] + [(place[main_axis] + 1) % entries.shape[main_axis]] + place[main_axis + 1:]
    return entries.at[tuple(place)].set(low).at[tuple(next_to)].set(largest)


def levels(own_key, extent, pieces, low, largest):
    gain, own = 1.0, jax.random.fold_in(own_key, 6)
    for position, blocks in pieces:
        steps = jnp.exp(jax.random.uniform(jax.random.fold_in(own, position), (blocks,), jnp.float32, low / len(pieces), largest / len(pieces)))
        gain = gain * jnp.repeat(steps, extent[position] // blocks).reshape([-1 if axis == position else 1 for axis in range(len(extent))])
    return gain


def length_profile(amount, total, bound, lean):
    weights = [(1 << 20) // math.isqrt(rank ** lean) + 1 for rank in range(2, amount + 1)]
    rest, counts = total - bound - (amount - 1), [1] * (amount - 1)
    while rest > 0:
        free = [i for i in range(amount - 1) if counts[i] < bound]
        pool, budget = sum([weights[i] for i in free]), rest
        for i in free:
            addition = min(bound - counts[i], max(1, budget * weights[i] // pool), rest)
            counts[i] = counts[i] + addition
            rest = rest - addition
    return np.array([bound] + counts)


def ragged_sizes(key, amount, total, reach, skew):
    if amount == 2:
        one = jax.random.randint(key, (), max(1, total - reach), min(reach, total - 1) + 1)
        return jnp.stack([one, total - one])
    lengths = jnp.asarray(length_profile(amount, total, reach, skew), jnp.int32)
    pairs = (amount - 1) // 2
    source_of, receiver = lengths[1:1 + 2 * pairs:2], lengths[2:2 + 2 * pairs:2]
    margin = jnp.minimum(source_of - 1, reach - receiver)
    passed = jax.random.randint(jax.random.fold_in(key, 1), (pairs,), 0, 1 << 20) % (margin + 1)
    lengths = lengths.at[1:1 + 2 * pairs:2].set(source_of - passed).at[2:2 + 2 * pairs:2].set(receiver + passed)
    return lengths[jax.random.permutation(jax.random.fold_in(key, 2), amount)]


def gaussian(stream_key, extent, width, most, pieces=(), kind=jnp.bfloat16):
    entries = width * jax.random.normal(stream_key, extent, jnp.float32)
    if pieces:
        entries = entries * levels(stream_key, extent, pieces, -0.22, 0.18)
    return jnp.clip(entries, -most, most).astype(kind)


def setup_inputs(seed: int = 0) -> dict:
    key_list = jax.random.split(jax.random.key(seed), 11)
    interp_index = set_ends(jax.random.randint(key_list[0], (K, ORIENTS, N_NAR, HALF, TL), 0, VOX), jax.random.fold_in(key_list[0], 1), 0, VOX - 1).astype(jnp.int32)
    interp_weight = jnp.clip(0.25 * jax.random.uniform(key_list[1], (K, ORIENTS, N_NAR, HALF, TL), jnp.float32) ** levels(key_list[1], (K, ORIENTS, N_NAR, HALF, TL), ((1, 4), (2, 2), (3, 64)), -0.2, 0.2), 0.0, 0.25).astype(jnp.bfloat16)
    volume = gaussian(key_list[2], (2, N_NAR, N_TILE, VOX), 1.0, 6.0, ((1, 2), (2, 64)))
    spectrum = gaussian(key_list[3], (2, N_TILE, N_NAR, HALF, TL), 1.0, 6.0, ((1, 64), (2, 2)))
    ctf_filter = jnp.clip(jax.random.uniform(key_list[4], (N_TILE, N_NAR, HALF, TL), jnp.float32, -1.0, 1.0) * levels(key_list[4], (N_TILE, N_NAR, HALF, TL), ((0, 64), (1, 2)), -0.4, 0.0), -1.0, 1.0).astype(jnp.bfloat16)
    peak_count = jax.vmap(lambda own: ragged_sizes(own, N_TILE, PTOTAL, MOST, 2))(jax.random.split(key_list[5], N_ROT)).reshape((N_ROT, N_TILE)).astype(jnp.int32)
    peak_orient = set_ends(jax.random.randint(key_list[6], (PEAKS,), 0, ORI), jax.random.fold_in(key_list[6], 1), 0, ORI - 1).astype(jnp.int32)
    peak_row = set_ends(jax.random.randint(key_list[7], (PEAKS,), 0, TL), jax.random.fold_in(key_list[7], 1), 0, TL - 1).astype(jnp.int32)
    peak_col = set_ends(jax.random.randint(key_list[8], (PEAKS,), 0, TL), jax.random.fold_in(key_list[8], 1), 0, TL - 1).astype(jnp.int32)
    ctf_grid = jnp.clip(jax.random.uniform(key_list[9], (DEFOCI, N_NAR, BINS), jnp.float32, -1.0, 1.0) * levels(key_list[9], (DEFOCI, N_NAR, BINS), ((0, 64), (1, 2)), -0.4, 0.0), -1.0, 1.0).astype(jnp.bfloat16)
    return dict(interp_index=interp_index, interp_weight=interp_weight, volume=volume, spectrum=spectrum, ctf_filter=ctf_filter, peak_count=peak_count, peak_orient=peak_orient, peak_row=peak_row, peak_col=peak_col, ctf_grid=ctf_grid)


def dft_tables(length):
    steps = jnp.arange(length, dtype=jnp.int32)
    phase = ((steps[:, None] * steps[None, :]) % length).astype(jnp.float32) * (2.0 * jnp.pi / length)
    cosv = jnp.cos(phase).astype(jnp.bfloat16)
    sinv = jnp.sin(phase).astype(jnp.bfloat16)
    wide = jnp.concatenate([jnp.concatenate([cosv, sinv], 1), jnp.concatenate([-sinv, cosv], 1)], 0)
    back = jnp.stack([cosv, -sinv], axis=1)
    return wide, back


def reference(interp_index, interp_weight, volume, spectrum, ctf_filter, peak_count, peak_orient, peak_row, peak_col, ctf_grid):
    vol_rows = jnp.repeat(volume, SROWS, axis=2)
    narrow = jnp.arange(N_NAR, dtype=jnp.int32)[None, :, None, None]
    rowpos = jnp.arange(HALF, dtype=jnp.int32)[None, None, :, None]

    def project(pair):
        index_o, weight_o = pair
        values = vol_rows[:, narrow, rowpos, index_o]
        return jnp.sum(weight_o.astype(jnp.float32)[None] * values.astype(jnp.float32), axis=1).astype(jnp.bfloat16)

    slices = lax.map(project, (jnp.moveaxis(interp_index, 1, 0), jnp.moveaxis(interp_weight, 1, 0)))
    slices = slices.reshape(ORIENTS, 2, TL, TL)
    wide, back = dft_tables(TL)
    back_f = back.astype(jnp.float32)

    def per_tile(t):
        spec = spectrum[:, t].reshape(2, TL, TL).astype(jnp.float32)
        filt = ctf_filter[t].reshape(TL, TL).astype(jnp.float32)
        sr = slices[:, 0].astype(jnp.float32)
        si = slices[:, 1].astype(jnp.float32)
        cr = filt * sr
        ci = filt * si
        xr = spec[0] * cr + spec[1] * ci
        xi = spec[1] * cr - spec[0] * ci
        cross = jnp.stack([xr, xi], axis=2).astype(jnp.bfloat16)
        halfimg = jnp.dot(cross.reshape(ORIENTS * TL, 2 * TL), wide, preferred_element_type=jnp.float32)
        halfimg = halfimg.astype(jnp.bfloat16).reshape(ORIENTS, TL, 2, TL)
        corr = jnp.einsum('yck,okcx->oyx', back_f, halfimg.astype(jnp.float32)) * (1.0 / TL)
        top = jnp.max(corr, axis=0)
        mean = jnp.sum(corr, axis=0) / ORIENTS
        return top, mean

    peak_max, peak_mean = lax.map(per_tile, jnp.arange(N_TILE, dtype=jnp.int32))
    peak_max = peak_max.reshape(N_TILE, TL, N_NAR, HALF).transpose(0, 2, 1, 3).reshape(N_TILE, N_NAR, TL * HALF)
    peak_mean = peak_mean.reshape(N_TILE, TL, N_NAR, HALF).transpose(0, 2, 1, 3).reshape(N_TILE, N_NAR, TL * HALF)

    freq = jnp.arange(TL, dtype=jnp.int32)
    slot = jnp.arange(MOST, dtype=jnp.int32)

    def per_list(index):
        r = index // N_TILE
        t = index % N_TILE
        rows = index * MOST + slot
        orient = (r * ORI + peak_orient[rows]).astype(jnp.int32)
        y0 = peak_row[rows].astype(jnp.int32)
        x0 = peak_col[rows].astype(jnp.int32)
        spec = spectrum[:, t].reshape(2, TL, TL).astype(jnp.float32)
        chosen = slices[orient].astype(jnp.float32)
        pr = (spec[0][None] * chosen[:, 0] + spec[1][None] * chosen[:, 1]).astype(jnp.bfloat16).astype(jnp.float32)
        pi = (spec[1][None] * chosen[:, 0] - spec[0][None] * chosen[:, 1]).astype(jnp.bfloat16).astype(jnp.float32)
        turns = (freq[None, :, None] * y0[:, None, None] + freq[None, None, :] * x0[:, None, None]) % TL
        phase = turns.astype(jnp.float32) * (2.0 * jnp.pi / TL)
        shifted = pr * jnp.cos(phase) - pi * jnp.sin(phase)
        binned = jnp.sum(shifted.reshape(MOST, TL, TL // 4, 4), axis=3).astype(jnp.bfloat16)
        valid = slot < peak_count[r, t]
        binned = jnp.where(valid[:, None, None], binned, jnp.zeros_like(binned))
        return binned.reshape(MOST, N_NAR, BINS)

    binned_all = lax.map(per_list, jnp.arange(N_ROT * N_TILE, dtype=jnp.int32))
    binned_all = binned_all.reshape(N_ROT, N_TILE * MOST, N_NAR, BINS)
    refined = jnp.einsum('rpnb,qnb->rpq', binned_all.astype(jnp.float32), ctf_grid.astype(jnp.float32)) * (1.0 / TL)
    best = jnp.max(refined, axis=2)
    return peak_max, peak_mean, refined, best
```

```python
import jax
import jax.numpy as jnp
import numpy as np
from jax import lax
from jax.experimental import pallas as pl
from jax.experimental.pallas import tpu as pltpu
from jax.sharding import PartitionSpec as P

BF = jnp.bfloat16
F32 = jnp.float32
I32 = jnp.int32
LANES = 128
DFT = 384
HALF = 192
ROWS = 3
TILES = 64
SLOTS = 4
WIDE = ROWS * DFT
BINS = 288
GRID = 8
BASE = 16
VMEM_LIMIT = 48 * 1024 * 1024

VM = pl.BlockSpec(memory_space=pltpu.VMEM)
SM = pl.BlockSpec(memory_space=pltpu.SMEM)
NN = (((1,), (0,)), ((), ()))
NT = (((1,), (1,)), ((), ()))


def bf(x):
    return np.asarray(x, np.float32).astype(jnp.bfloat16)


def split(x):
    high = bf(x)
    return high, bf(np.asarray(x, np.float64) - high.astype(np.float64))


def tables():
    steps = np.arange(DFT)
    phase = (steps[:, None] * steps[None, :] % DFT) * (2.0 * np.pi / DFT)
    cosv, sinv = np.cos(phase), np.sin(phase)
    back = np.zeros((2, DFT, 2 * HALF), np.float32)
    order = np.array([ROWS * t + j for j in range(ROWS) for t in range(TILES)])
    for n in range(2):
        back[n, :, :HALF] = cosv[:, n * HALF + order]
        back[n, :, HALF:] = -sinv[:, n * HALF + order]
    ch, cl = split(cosv)
    sh, sl = split(sinv)
    tabx = np.concatenate([ch, cl, sh, sl], 1)
    return bf(back), tabx


def interpolate(index, weight, table):
    blocks = index.shape[0] // 8
    kept = index.shape[0] // 8

    def kernel(index_ref, weight_ref, table_ref, out_ref, value_ref):
        def step(v, carry):
            rows = pl.ds(pl.multiple_of(v * 8, 8), 8)
            entry = index_ref[rows, :]
            low = entry & (LANES - 1)
            high = lax.shift_right_logical(entry, 7)
            bits = [(lax.shift_right_logical(high, b) & 1) == 1 for b in range(5)]
            weights = weight_ref[rows, :]

            def pick(c, level, first):
                if level < 0:
                    row = jnp.broadcast_to(table_ref[c, first : first + 1, :], (8, LANES))
                    return jnp.take_along_axis(row, low, axis=1)
                return jnp.where(
                    bits[level],
                    pick(c, level - 1, first + (1 << level)),
                    pick(c, level - 1, first),
                )

            for c in range(2):
                value_ref[c, rows, :] = pick(c, 4, 0) * weights
            return carry

        lax.fori_loop(0, blocks, step, 0)
        for c in range(2):
            total = value_ref[c, 0:kept, :]
            for k in range(1, 8):
                total = total + value_ref[c, k * kept : (k + 1) * kept, :]
            out_ref[c] = total

    return pl.pallas_call(
        kernel,
        out_shape=jax.ShapeDtypeStruct((2, kept, LANES), F32),
        in_specs=[VM] * 3,
        out_specs=VM,
        scratch_shapes=[pltpu.VMEM((2, index.shape[0], LANES), F32)],
        name="interpolate",
    )(index, weight, table)


def correlate(nar, own, other, spec, filt, tabx, back):
    def kernel(at_ref, own_ref, other_ref, spec_ref, filt_ref, tabx_ref, back_ref, keep_ref, send_ref):
        first = at_ref[1] == 0
        mine = own_ref[...].astype(F32)
        theirs = other_ref[...].astype(F32)
        sr = jnp.where(first, mine, theirs)
        si = jnp.where(first, theirs, mine)
        parts = []
        for o in range(2):
            for j in range(ROWS):
                at = slice(j * DFT, (j + 1) * DFT)
                so = slice(o * WIDE + j * DFT, o * WIDE + (j + 1) * DFT)
                c = filt_ref[:, at].astype(F32)
                mr = spec_ref[:, at].astype(F32)
                mi = spec_ref[:, WIDE + j * DFT : WIDE + (j + 1) * DFT].astype(F32)
                cr = c * sr[:, so]
                ci = c * si[:, so]
                xr = mr * cr + mi * ci
                xi = mi * cr - mr * ci
                parts.append(jnp.concatenate([xr.astype(BF), xi.astype(BF)], axis=1))
        cross = jnp.concatenate(parts, axis=0)
        cosv, sinv = tabx_ref[:, :DFT], tabx_ref[:, 2 * DFT : 3 * DFT]
        wide = jnp.concatenate(
            [jnp.concatenate([cosv, sinv], axis=1), jnp.concatenate([-sinv, cosv], axis=1)], axis=0
        )
        halfimg = lax.dot_general(cross, wide, NN, preferred_element_type=F32).astype(BF)
        table = back_ref[at_ref[0]]
        low = at_ref[0] == 0
        for o in range(2):
            rows = halfimg[o * HALF : (o + 1) * HALF]
            both = jnp.concatenate([rows[:, :DFT], rows[:, DFT:]], axis=0)
            sums = lax.dot_general(table, both, NN, preferred_element_type=F32)
            left, right = sums[:, :HALF], sums[:, HALF:]
            keep_ref[o] = jnp.where(low, left, right).astype(BF)
            send_ref[o] = jnp.where(low, right, left).astype(BF)

    shape = jax.ShapeDtypeStruct((2, DFT, HALF), BF)
    return pl.pallas_call(
        kernel,
        out_shape=(shape, shape),
        in_specs=[SM] + [VM] * 6,
        out_specs=(VM, VM),
        compiler_params=pltpu.CompilerParams(vmem_limit_bytes=VMEM_LIMIT),
        name="correlate",
    )(nar, own, other, spec, filt, tabx, back)


def score(spec, grid, slices, meta, tabx, taby):
    def kernel(spec_ref, grid_ref, slice_ref, meta_ref, tabx_ref, taby_ref, out_ref, place_ref):
        meta = meta_ref[...].astype(F32)
        lane = lax.broadcasted_iota(I32, (TILES, DFT), 1).astype(F32)
        count = meta[:, 20:21]
        tri_r = lax.broadcasted_iota(I32, (TILES, TILES), 0)
        tri_c = lax.broadcasted_iota(I32, (TILES, TILES), 1)
        before = jnp.where(tri_c < tri_r, 1.0, 0.0).astype(BF)
        spread = jnp.broadcast_to(count, (TILES, LANES)).astype(BF)
        offset = lax.dot_general(before, spread, NN, preferred_element_type=F32)[:, 0:1]
        hot_x, hot_y, place, listed = [], [], [], []
        for i in range(SLOTS):
            y0 = meta[:, 5 * i + 1 : 5 * i + 2] * BASE + meta[:, 5 * i + 2 : 5 * i + 3]
            x0 = meta[:, 5 * i + 3 : 5 * i + 4] * BASE + meta[:, 5 * i + 4 : 5 * i + 5]
            hot_x.append(jnp.where(lane == x0, 1.0, 0.0).astype(BF))
            hot_y.append(jnp.where(lane == y0, 1.0, 0.0).astype(BF))
            valid = count > float(i)
            seat = jnp.where(valid, offset + float(i), -1.0)
            hot = jnp.where(lane[:, :256] == seat, 1.0, 0.0)
            for h in range(2):
                place_ref[h, pl.ds(i, TILES, stride=SLOTS), :] = hot[:, h * LANES : (h + 1) * LANES]
            place.append(hot.astype(BF))
        hot_x = jnp.concatenate(hot_x, axis=0)
        hot_y = jnp.concatenate(hot_y, axis=0)
        place = jnp.concatenate(place, axis=0)
        wave = lax.dot_general(hot_x, tabx_ref[...], NN, preferred_element_type=F32)
        cx = wave[:, :DFT] + wave[:, DFT : 2 * DFT]
        sx = wave[:, 2 * DFT : 3 * DFT] + wave[:, 3 * DFT :]
        tilt = lax.dot_general(hot_y, taby_ref[...], NT, preferred_element_type=F32)
        rows = []
        for i in range(SLOTS):
            at = slice(i * TILES, (i + 1) * TILES)
            second = meta[:, 5 * i : 5 * i + 1] > 0.5
            pieces = []
            for j in range(ROWS):
                cols = slice(j * DFT, (j + 1) * DFT)
                mr = spec_ref[:, cols].astype(F32)
                mi = spec_ref[:, WIDE + j * DFT : WIDE + (j + 1) * DFT].astype(F32)

                def chosen(c):
                    part = [
                        slice_ref[:, (c * 2 + o) * WIDE + j * DFT : (c * 2 + o) * WIDE + (j + 1) * DFT]
                        for o in range(2)
                    ]
                    return jnp.where(second, part[1], part[0])

                sr, si = chosen(0), chosen(1)
                pr = (mr * sr + mi * si).astype(BF).astype(F32)
                pi = (mi * sr - mr * si).astype(BF).astype(F32)
                cy = tilt[at, j : j + 1] + tilt[at, 3 + j : 4 + j]
                sy = tilt[at, 6 + j : 7 + j] + tilt[at, 9 + j : 10 + j]
                pieces.append(
                    cy * (pr * cx[at] - pi * sx[at]) - sy * (pr * sx[at] + pi * cx[at])
                )
            rows.append(jnp.concatenate(pieces, axis=1))
        shifted = jnp.concatenate(rows, axis=0)
        high = shifted.astype(BF)
        bin_of = lax.shift_right_logical(lax.broadcasted_iota(I32, (WIDE, DFT), 0), 2)
        group = jnp.where(bin_of == lax.broadcasted_iota(I32, (WIDE, DFT), 1), 1.0, 0.0).astype(BF)
        low = (shifted - high.astype(F32)).astype(BF)
        binned = lax.dot_general(high, group, NN, preferred_element_type=F32)
        binned = binned + lax.dot_general(low, group, NN, preferred_element_type=F32)
        binned = binned.astype(BF)[:, :BINS]
        values = jnp.concatenate([grid_ref[:, q * BINS : (q + 1) * BINS] for q in range(GRID)], axis=0)
        scores = lax.dot_general(values, binned, NT, preferred_element_type=F32).astype(BF)
        packed = lax.dot_general(scores, place, NN, preferred_element_type=F32)
        lanes = lax.broadcasted_iota(I32, (TILES, LANES), 1)
        extra = jnp.zeros((TILES, LANES), F32)
        for q in range(GRID):
            block = packed[q * TILES : (q + 1) * TILES]
            out_ref[:, q * LANES : (q + 1) * LANES] = block[:, :LANES].astype(BF)
            extra = jnp.where(lanes == q, block[:, LANES : LANES + 1], extra)
        out_ref[:, GRID * LANES :] = extra.astype(BF)

    return pl.pallas_call(
        kernel,
        out_shape=(
            jax.ShapeDtypeStruct((TILES, (GRID + 1) * LANES), BF),
            jax.ShapeDtypeStruct((2, SLOTS * TILES, LANES), F32),
        ),
        in_specs=[VM] * 6,
        out_specs=(VM, VM),
        compiler_params=pltpu.CompilerParams(vmem_limit_bytes=VMEM_LIMIT),
        name="score",
    )(spec, grid, slices, meta, tabx, taby)


def expand(place, values, tops):
    def kernel(place_ref, value_ref, top_ref, refined_ref, best_ref):
        exact = dict(preferred_element_type=F32, precision=lax.Precision.HIGHEST)
        place = jnp.concatenate([place_ref[0], place_ref[1]], axis=1)
        refined_ref[...] = lax.dot_general(place, value_ref[...], NT, **exact)
        top = jnp.max(top_ref[...], axis=0, keepdims=True)
        top = jnp.broadcast_to(top, (8, top.shape[1]))
        best_ref[...] = lax.dot_general(top, place, NT, **exact)[0:1]

    return pl.pallas_call(
        kernel,
        out_shape=(
            jax.ShapeDtypeStruct((SLOTS * TILES, GRID), F32),
            jax.ShapeDtypeStruct((1, SLOTS * TILES), F32),
        ),
        in_specs=[VM] * 3,
        out_specs=(VM, VM),
        name="expand",
    )(place, values, tops)


def exchange(x, axis, bit):
    size = lax.axis_size(axis)
    return lax.ppermute(x, axis, [(k, k ^ bit) for k in range(size)])


def shards(
    interp_index,
    interp_weight,
    volume,
    spectrum,
    ctf_filter,
    peak_count,
    peak_orient,
    peak_row,
    peak_col,
    ctf_grid,
):
    back, tabx = [jnp.asarray(t) for t in tables()]
    nar = lax.axis_index("nar")
    tile = lax.axis_index("tile")

    taby = lax.dynamic_slice_in_dim(tabx, (nar * TILES + tile) * ROWS, ROWS, 0)
    taby = taby.reshape(ROWS, 4, DFT).transpose(1, 0, 2).reshape(4 * ROWS, DFT)
    taby = jnp.pad(taby, ((0, 16 - 4 * ROWS), (0, 0)))

    slices = interpolate(
        interp_index.reshape(-1, LANES),
        interp_weight.reshape(-1, LANES).astype(F32),
        volume.reshape(2, -1, LANES).astype(F32),
    ).astype(BF)

    spec = spectrum.reshape(2, TILES, WIDE).transpose(1, 0, 2).reshape(TILES, 2 * WIDE)
    filt = ctf_filter.reshape(TILES, WIDE)
    grid = ctf_grid.reshape(GRID, TILES, BINS).transpose(1, 0, 2).reshape(TILES, GRID * BINS)
    fields = jnp.stack(
        [peak_orient, peak_row // BASE, peak_row % BASE, peak_col // BASE, peak_col % BASE], axis=1
    ).reshape(-1)
    fields = jnp.pad(jnp.concatenate([fields, peak_count.reshape(1)]), (0, LANES - 5 * SLOTS - 1)).astype(BF)
    core = (jnp.arange(TILES, dtype=I32) % 2)[:, None]
    flat = slices.reshape(2, 1, 2 * WIDE)
    payload = jnp.concatenate(
        [
            jnp.where(core == 0, flat[0], flat[1]),
            spec,
            grid,
            jnp.broadcast_to(fields[None], (TILES, LANES)),
        ],
        axis=1,
    )
    got = lax.all_to_all(payload, "tile", 0, 0, tiled=True)
    mine = got[:, : 2 * WIDE]
    other = exchange(mine, "tile", 1)
    packed, place = score(
        got[:, 2 * WIDE : 4 * WIDE],
        got[:, 4 * WIDE : 4 * WIDE + GRID * BINS],
        slices.reshape(1, 4 * WIDE).astype(F32),
        got[:, 4 * WIDE + GRID * BINS :],
        tabx,
        taby,
    )
    keep, send = correlate(jnp.stack([nar, tile % 2]), mine, other, spec, filt, tabx, back)
    extra_rows = exchange(send, "nar", 1)

    sums = lax.all_to_all(packed, "tile", 0, 0, tiled=True)
    sums = jnp.sum(sums.astype(F32), axis=0)
    sums = lax.psum(sums, "nar") * (1.0 / DFT)
    last = jnp.zeros((GRID, LANES), F32).at[:, 0].set(sums[GRID * LANES : GRID * LANES + GRID])
    values = jnp.concatenate([sums[: GRID * LANES].reshape(GRID, LANES), last], axis=1)
    top = jnp.max(values, axis=0)

    corr = (keep.astype(F32) + extra_rows.astype(F32)) * (1.0 / DFT)
    stats = jnp.stack([jnp.maximum(corr[0], corr[1]), corr[0] + corr[1]]).astype(BF)
    others = [exchange(stats, "rot", bit) for bit in (1, 2, 3)]

    tops = lax.all_to_all(jnp.broadcast_to(top[None], (TILES, 2 * LANES)), "tile", 0, 0, tiled=True)
    refined, best = expand(place, values, tops)

    everything = [x.astype(F32) for x in [stats] + others]
    peak = jnp.maximum(
        jnp.maximum(everything[0][0], everything[1][0]), jnp.maximum(everything[2][0], everything[3][0])
    )
    total = (everything[0][1] + everything[1][1]) + (everything[2][1] + everything[3][1])
    return (
        peak.reshape(1, 1, -1),
        (total * (1.0 / 8)).reshape(1, 1, -1),
        refined.reshape(1, SLOTS * TILES, GRID),
        best,
    )


def solution(mesh):
    return jax.shard_map(
        shards,
        mesh=mesh,
        in_specs=(
            P(None, "rot", "nar", "tile", None),
            P(None, "rot", "nar", "tile", None),
            P(None, "nar", "tile", None),
            P(None, "tile", "nar", None, None),
            P("tile", "nar", None, None),
            P("rot", "tile"),
            P(("rot", "tile")),
            P(("rot", "tile")),
            P(("rot", "tile")),
            P("tile", "nar", None),
        ),
        out_specs=(
            P("tile", "nar", None),
            P("tile", "nar", None),
            P("rot", None, "tile"),
            P("rot", None),
        ),
        check_vma=False,
    )
```

```python
import jax
import jax.numpy as jnp
import numpy as np
from jax import lax
from jax.experimental import pallas as pl
from jax.experimental.pallas import tpu as pltpu
from jax.sharding import PartitionSpec as P

BF = jnp.bfloat16
F32 = jnp.float32
I32 = jnp.int32
LANES = 128
DFT = 384
HALF = 192
ROWS = 3
TILES = 64
SLOTS = 4
WIDE = ROWS * DFT
BINS = 288
GRID = 8
BASE = 16
BLOCKS = 9
XROWS = 40
SROWS = 24
ORIENTS = 8
VMEM_LIMIT = 48 * 1024 * 1024

VM = pl.BlockSpec(memory_space=pltpu.VMEM)
SM = pl.BlockSpec(memory_space=pltpu.SMEM)
NN = (((1,), (0,)), ((), ()))
NT = (((1,), (1,)), ((), ()))


def bf(x):
    return np.asarray(x, np.float32).astype(jnp.bfloat16)


def split(x):
    high = bf(x)
    return high, bf(np.asarray(x, np.float64) - high.astype(np.float64))


def tables():
    steps = np.arange(DFT)
    phase = (steps[:, None] * steps[None, :] % DFT) * (2.0 * np.pi / DFT)
    cosv, sinv = np.cos(phase), np.sin(phase)
    rows = np.concatenate([steps[0::2], steps[1::2]])
    order = np.array([ROWS * t + j for j in range(ROWS) for t in range(TILES)])
    back = np.zeros((2, DFT, 2 * HALF), np.float32)
    for n in range(2):
        back[n, :, :HALF] = cosv[rows][:, n * HALF + order]
        back[n, :, HALF:] = -sinv[rows][:, n * HALF + order]
    ch, cl = split(cosv)
    sh, sl = split(sinv)
    return bf(back), np.concatenate([ch, cl, sh, sl], 1)


def every(ref, row, step):
    return ref[pl.ds(row, TILES, stride=step), :]


def prepare(spectrum, grid, meta):
    def kernel(spec_ref, grid_ref, meta_ref, out_ref, spec_s, out_s):
        for c in range(2):
            for b in range(ROWS):
                spec_s[c * ROWS + b] = spec_ref[c, :, b * LANES : (b + 1) * LANES].astype(F32)
        for c in range(2):
            for j in range(ROWS):
                for b in range(ROWS):
                    row = c * BLOCKS + j * ROWS + b
                    out_s[pl.ds(row, TILES, stride=XROWS), :] = spec_s[c * ROWS + b, pl.ds(j, TILES, stride=ROWS), :]
        for r in range(2 * BLOCKS):
            block = grid_ref[:, r * LANES : (r + 1) * LANES].astype(F32)
            out_s[pl.ds(2 * BLOCKS + r, TILES, stride=XROWS), :] = block
        fields = jnp.broadcast_to(meta_ref[...], (TILES, LANES))
        for r in range(4 * BLOCKS, XROWS):
            out_s[pl.ds(r, TILES, stride=XROWS), :] = fields
        out_ref[...] = out_s[...].astype(BF).reshape(out_ref.shape)

    return pl.pallas_call(
        kernel,
        out_shape=jax.ShapeDtypeStruct((TILES, XROWS, LANES), BF),
        in_specs=[VM] * 3,
        out_specs=VM,
        scratch_shapes=[
            pltpu.VMEM((2 * ROWS, HALF, LANES), F32),
            pltpu.VMEM((TILES * XROWS, LANES), F32),
        ],
        compiler_params=pltpu.CompilerParams(vmem_limit_bytes=VMEM_LIMIT),
        name="prepare",
    )(spectrum, grid, meta)


def interpolate(index, weight, table):
    steps = index.shape[0] // 16
    kept = index.shape[0] // 8

    def kernel(index_ref, weight_ref, table_ref, out_ref, own_ref, value_ref):
        def step(v, carry):
            pair = pl.ds(pl.multiple_of(v * 16, 16), 16)
            weights = weight_ref[pair, :].astype(F32)
            for s in range(2):
                rows = pl.ds(pl.multiple_of(v * 16 + s * 8, 8), 8)
                entry = index_ref[rows, :]
                low = entry & (LANES - 1)
                high = lax.shift_right_logical(entry, 7)
                bits = [(lax.shift_right_logical(high, b) & 1) == 1 for b in range(5)]

                def pick(c, level, first):
                    if level < 0:
                        row = jnp.broadcast_to(table_ref[c, first : first + 1, :], (8, LANES))
                        return jnp.take_along_axis(row, low, axis=1)
                    return jnp.where(
                        bits[level],
                        pick(c, level - 1, first + (1 << level)),
                        pick(c, level - 1, first),
                    )

                for c in range(2):
                    value_ref[c, rows, :] = pick(c, 4, 0) * weights[s * 8 : (s + 1) * 8]
            return carry

        lax.fori_loop(0, steps, step, 0)
        for c in range(2):
            total = value_ref[c, 0:kept, :]
            for k in range(1, 8):
                total = total + value_ref[c, k * kept : (k + 1) * kept, :]
            rounded = total.astype(BF)
            own_ref[c] = rounded.astype(F32)
            block = jnp.concatenate([rounded.astype(F32), jnp.zeros((SROWS - kept, LANES), F32)], axis=0).astype(BF)
            for t in range(c, TILES, 2):
                out_ref[t] = block

    return pl.pallas_call(
        kernel,
        out_shape=(
            jax.ShapeDtypeStruct((TILES, SROWS, LANES), BF),
            jax.ShapeDtypeStruct((2, kept, LANES), F32),
        ),
        in_specs=[VM] * 3,
        out_specs=(VM, VM),
        scratch_shapes=[pltpu.VMEM((2, index.shape[0], LANES), F32)],
        compiler_params=pltpu.CompilerParams(vmem_limit_bytes=VMEM_LIMIT),
        name="interpolate",
    )(index, weight, table)


def correlate(place, own, other, spectrum, filt, tabx, back):
    def kernel(at_ref, own_ref, other_ref, spec_ref, filt_ref, tabx_ref, back_ref, keep_ref, send_ref, sl_s, spec_s):
        first = at_ref[1] == 0
        mine = own_ref[...].astype(F32).reshape(TILES * SROWS, LANES)
        theirs = other_ref[...].astype(F32).reshape(TILES * SROWS, LANES)
        sl_s[0] = jnp.where(first, mine, theirs)
        sl_s[1] = jnp.where(first, theirs, mine)
        for c in range(2):
            for b in range(ROWS):
                spec_s[c * ROWS + b] = spec_ref[c, :, b * LANES : (b + 1) * LANES].astype(F32)
        for b in range(ROWS):
            spec_s[2 * ROWS + b] = filt_ref[:, b * LANES : (b + 1) * LANES].astype(F32)
        real = [[None] * (ROWS * ROWS) for _ in range(2)]
        imag = [[None] * (ROWS * ROWS) for _ in range(2)]
        for j in range(ROWS):
            for b in range(ROWS):
                mr = every(spec_s.at[b], j, ROWS)
                mi = every(spec_s.at[ROWS + b], j, ROWS)
                c = every(spec_s.at[2 * ROWS + b], j, ROWS)
                for o in range(2):
                    row = o * BLOCKS + j * ROWS + b
                    cr = c * every(sl_s.at[0], row, SROWS)
                    ci = c * every(sl_s.at[1], row, SROWS)
                    real[o][j * ROWS + b] = (mr * cr + mi * ci).astype(BF)
                    imag[o][j * ROWS + b] = (mi * cr - mr * ci).astype(BF)
        cross = jnp.concatenate(
            [
                jnp.concatenate(real[o][j * ROWS : (j + 1) * ROWS] + imag[o][j * ROWS : (j + 1) * ROWS], axis=1)
                for o in range(2)
                for j in range(ROWS)
            ],
            axis=0,
        )
        cosv, sinv = tabx_ref[:, :DFT], tabx_ref[:, 2 * DFT : 3 * DFT]
        wide = jnp.concatenate(
            [jnp.concatenate([cosv, sinv], axis=1), jnp.concatenate([-sinv, cosv], axis=1)], axis=0
        )
        halfimg = lax.dot_general(cross, wide, NN, preferred_element_type=F32).astype(BF)
        table = back_ref[at_ref[0]]
        low = at_ref[0] == 0
        for o in range(2):
            rows = halfimg[o * HALF : (o + 1) * HALF]
            both = jnp.concatenate([rows[:, :DFT], rows[:, DFT:]], axis=0)
            sums = lax.dot_general(table, both, NN, preferred_element_type=F32)
            left = jnp.concatenate([sums[:HALF, :HALF], sums[HALF:, :HALF]], axis=1)
            right = jnp.concatenate([sums[:HALF, HALF:], sums[HALF:, HALF:]], axis=1)
            keep_ref[o] = jnp.where(low, left, right).astype(BF)
            send_ref[o] = jnp.where(low, right, left).astype(BF)

    shape = jax.ShapeDtypeStruct((2, HALF, DFT), BF)
    return pl.pallas_call(
        kernel,
        out_shape=(shape, shape),
        in_specs=[SM] + [VM] * 6,
        out_specs=(VM, VM),
        scratch_shapes=[
            pltpu.VMEM((2, TILES * SROWS, LANES), F32),
            pltpu.VMEM((3 * ROWS, HALF, LANES), F32),
        ],
        compiler_params=pltpu.CompilerParams(vmem_limit_bytes=VMEM_LIMIT),
        name="correlate",
    )(place, own, other, spectrum, filt, tabx, back)


def score(got, slices, tabx, taby):
    def kernel(got_ref, slice_ref, tabx_ref, taby_ref, out_ref, place_ref, got_s):
        got_s[...] = got_ref[...].astype(F32).reshape(got_s.shape)
        meta = every(got_s, 4 * BLOCKS, XROWS)
        lane = lax.broadcasted_iota(I32, (TILES, DFT), 1).astype(F32)
        count = meta[:, 20:21]
        tri_r = lax.broadcasted_iota(I32, (TILES, TILES), 0)
        tri_c = lax.broadcasted_iota(I32, (TILES, TILES), 1)
        before = jnp.where(tri_c < tri_r, 1.0, 0.0).astype(BF)
        spread = jnp.broadcast_to(count, (TILES, LANES)).astype(BF)
        offset = lax.dot_general(before, spread, NN, preferred_element_type=F32)[:, 0:1]
        hot_x, hot_y, place = [], [], []
        for i in range(SLOTS):
            y0 = meta[:, 5 * i + 1 : 5 * i + 2] * BASE + meta[:, 5 * i + 2 : 5 * i + 3]
            x0 = meta[:, 5 * i + 3 : 5 * i + 4] * BASE + meta[:, 5 * i + 4 : 5 * i + 5]
            hot_x.append(jnp.where(lane == x0, 1.0, 0.0).astype(BF))
            hot_y.append(jnp.where(lane == y0, 1.0, 0.0).astype(BF))
            seat = jnp.where(count > float(i), offset + float(i), -1.0)
            hot = jnp.where(lane[:, :256] == seat, 1.0, 0.0)
            for h in range(2):
                place_ref[h, pl.ds(i, TILES, stride=SLOTS), :] = hot[:, h * LANES : (h + 1) * LANES]
            place.append(hot.astype(BF))
        hot_x = jnp.concatenate(hot_x, axis=0)
        hot_y = jnp.concatenate(hot_y, axis=0)
        place = jnp.concatenate(place, axis=0)
        wave = lax.dot_general(hot_x, tabx_ref[...], NN, preferred_element_type=F32)
        cx = wave[:, :DFT] + wave[:, DFT : 2 * DFT]
        sx = wave[:, 2 * DFT : 3 * DFT] + wave[:, 3 * DFT :]
        tilt = lax.dot_general(hot_y, taby_ref[...], NT, preferred_element_type=F32)
        pieces = [[] for _ in range(SLOTS)]
        for j in range(ROWS):
            for b in range(ROWS):
                r = j * ROWS + b
                cols = slice(b * LANES, (b + 1) * LANES)
                mr = every(got_s, r, XROWS)
                mi = every(got_s, BLOCKS + r, XROWS)
                plain = []
                for o in range(2):
                    sr = slice_ref[0, o * BLOCKS + r : o * BLOCKS + r + 1, :]
                    si = slice_ref[1, o * BLOCKS + r : o * BLOCKS + r + 1, :]
                    plain.append(((mr * sr + mi * si).astype(BF).astype(F32), (mi * sr - mr * si).astype(BF).astype(F32)))
                for i in range(SLOTS):
                    at = slice(i * TILES, (i + 1) * TILES)
                    second = meta[:, 5 * i : 5 * i + 1] > 0.5
                    pr = jnp.where(second, plain[1][0], plain[0][0])
                    pi = jnp.where(second, plain[1][1], plain[0][1])
                    cy = tilt[at, j : j + 1] + tilt[at, 3 + j : 4 + j]
                    sy = tilt[at, 6 + j : 7 + j] + tilt[at, 9 + j : 10 + j]
                    wx, vx = cx[at, cols], sx[at, cols]
                    pieces[i].append(cy * (pr * wx - pi * vx) - sy * (pr * vx + pi * wx))
        shifted = jnp.concatenate([jnp.concatenate(p, axis=1) for p in pieces], axis=0)
        high = shifted.astype(BF)
        bin_of = lax.shift_right_logical(lax.broadcasted_iota(I32, (WIDE, DFT), 0), 2)
        group = jnp.where(bin_of == lax.broadcasted_iota(I32, (WIDE, DFT), 1), 1.0, 0.0).astype(BF)
        low = (shifted - high.astype(F32)).astype(BF)
        binned = lax.dot_general(high, group, NN, preferred_element_type=F32)
        binned = binned + lax.dot_general(low, group, NN, preferred_element_type=F32)
        binned = binned.astype(BF)[:, :BINS]
        grid = jnp.concatenate([every(got_s, 2 * BLOCKS + r, XROWS).astype(BF) for r in range(2 * BLOCKS)], axis=1)
        values = jnp.concatenate([grid[:, q * BINS : (q + 1) * BINS] for q in range(GRID)], axis=0)
        scores = lax.dot_general(values, binned, NT, preferred_element_type=F32).astype(BF)
        packed = lax.dot_general(scores, place, NN, preferred_element_type=F32)
        lanes = lax.broadcasted_iota(I32, (TILES, LANES), 1)
        extra = jnp.zeros((TILES, LANES), F32)
        for q in range(GRID):
            block = packed[q * TILES : (q + 1) * TILES]
            out_ref[:, q * LANES : (q + 1) * LANES] = block[:, :LANES].astype(BF)
            extra = jnp.where(lanes == q, block[:, LANES : LANES + 1], extra)
        out_ref[:, GRID * LANES :] = extra.astype(BF)

    return pl.pallas_call(
        kernel,
        out_shape=(
            jax.ShapeDtypeStruct((TILES, (GRID + 1) * LANES), BF),
            jax.ShapeDtypeStruct((2, SLOTS * TILES, LANES), F32),
        ),
        in_specs=[VM] * 4,
        out_specs=(VM, VM),
        scratch_shapes=[pltpu.VMEM((TILES * XROWS, LANES), F32)],
        compiler_params=pltpu.CompilerParams(vmem_limit_bytes=VMEM_LIMIT),
        name="score",
    )(got, slices, tabx, taby)


def expand(place, values, tops):
    def kernel(place_ref, value_ref, top_ref, refined_ref, best_ref):
        place = jnp.concatenate([place_ref[0], place_ref[1]], axis=1)
        top = jnp.max(top_ref[...], axis=0, keepdims=True)
        rows = jnp.concatenate([value_ref[...], jnp.broadcast_to(top, (8, top.shape[1]))], axis=0)
        out = lax.dot_general(rows, place, NT, preferred_element_type=F32, precision=lax.Precision.HIGHEST)
        refined_ref[...] = out[:GRID]
        best_ref[...] = out[GRID : GRID + 1]

    return pl.pallas_call(
        kernel,
        out_shape=(
            jax.ShapeDtypeStruct((GRID, SLOTS * TILES), F32),
            jax.ShapeDtypeStruct((1, SLOTS * TILES), F32),
        ),
        in_specs=[VM] * 3,
        out_specs=(VM, VM),
        name="expand",
    )(place, values, tops)


def finish(parts):
    def kernel(*refs):
        ins, (top_ref, mean_ref) = refs[:4], refs[4:]
        for b in range(ROWS):
            cols = slice(b * LANES, (b + 1) * LANES)
            tops = [ref[0, :, cols].astype(F32) for ref in ins]
            sums = [ref[1, :, cols].astype(F32) for ref in ins]
            top = jnp.maximum(jnp.maximum(tops[0], tops[1]), jnp.maximum(tops[2], tops[3]))
            top_ref[pl.ds(b, HALF, stride=ROWS), :] = top
            total = (sums[0] + sums[1]) + (sums[2] + sums[3])
            mean_ref[pl.ds(b, HALF, stride=ROWS), :] = total * (1.0 / ORIENTS)

    shape = jax.ShapeDtypeStruct((ROWS * HALF, LANES), F32)
    return pl.pallas_call(
        kernel,
        out_shape=(shape, shape),
        in_specs=[VM] * 4,
        out_specs=(VM, VM),
        name="finish",
    )(*parts)


def exchange(x, axis, bit):
    size = lax.axis_size(axis)
    return lax.ppermute(x, axis, [(k, k ^ bit) for k in range(size)])


def shards(
    interp_index,
    interp_weight,
    volume,
    spectrum,
    ctf_filter,
    peak_count,
    peak_orient,
    peak_row,
    peak_col,
    ctf_grid,
):
    back, tabx = [jnp.asarray(t) for t in tables()]
    nar = lax.axis_index("nar")
    tile = lax.axis_index("tile")

    taby = lax.dynamic_slice_in_dim(tabx, (nar * TILES + tile) * ROWS, ROWS, 0)
    taby = taby.reshape(ROWS, 4, DFT).transpose(1, 0, 2).reshape(4 * ROWS, DFT)
    taby = jnp.pad(taby, ((0, 16 - 4 * ROWS), (0, 0)))

    fields = jnp.stack(
        [peak_orient, peak_row // BASE, peak_row % BASE, peak_col // BASE, peak_col % BASE], axis=1
    ).reshape(1, -1)
    fields = jnp.concatenate([fields, peak_count.reshape(1, 1)], axis=1).astype(F32)
    fields = jnp.pad(fields, ((0, 0), (0, LANES - 5 * SLOTS - 1)))
    grid = ctf_grid.reshape(GRID, TILES, BINS).transpose(1, 0, 2).reshape(TILES, GRID * BINS)
    spec = spectrum.reshape(2, HALF, DFT)
    filt = ctf_filter.reshape(HALF, DFT)
    got = lax.all_to_all(prepare(spec, grid, fields), "tile", 0, 0, tiled=True)

    blocks, slices = interpolate(
        interp_index.reshape(-1, LANES),
        interp_weight.reshape(-1, LANES),
        volume.reshape(2, -1, LANES).astype(F32),
    )
    mine = lax.all_to_all(blocks, "tile", 0, 0, tiled=True)
    packed, place = score(got, slices, tabx, taby)
    other = exchange(mine, "tile", 1)
    keep, send = correlate(jnp.stack([nar, tile % 2]), mine, other, spec, filt, tabx, back)
    extra_rows = exchange(send, "nar", 1)

    sums = lax.all_to_all(packed, "tile", 0, 0, tiled=True)
    sums = jnp.sum(sums.astype(F32), axis=0)
    sums = lax.psum(sums, "nar") * (1.0 / DFT)
    last = jnp.zeros((GRID, LANES), F32).at[:, 0].set(sums[GRID * LANES : GRID * LANES + GRID])
    values = jnp.concatenate([sums[: GRID * LANES].reshape(GRID, LANES), last], axis=1)
    top = jnp.max(values, axis=0)

    corr = (keep.astype(F32) + extra_rows.astype(F32)) * (1.0 / DFT)
    stats = jnp.stack([jnp.maximum(corr[0], corr[1]), corr[0] + corr[1]]).astype(BF)
    others = [exchange(stats, "rot", bit) for bit in (1, 2, 3)]

    tops = lax.all_to_all(jnp.broadcast_to(top[None], (TILES, 2 * LANES)), "tile", 0, 0, tiled=True)
    refined, best = expand(place, values, tops)

    peak, mean = finish([stats] + others)
    return (
        peak.reshape(1, 1, -1),
        mean.reshape(1, 1, -1),
        refined.T.reshape(1, SLOTS * TILES, GRID),
        best,
    )


def solution(mesh):
    return jax.shard_map(
        shards,
        mesh=mesh,
        in_specs=(
            P(None, "rot", "nar", "tile", None),
            P(None, "rot", "nar", "tile", None),
            P(None, "nar", "tile", None),
            P(None, "tile", "nar", None, None),
            P("tile", "nar", None, None),
            P("rot", "tile"),
            P(("rot", "tile")),
            P(("rot", "tile")),
            P(("rot", "tile")),
            P("tile", "nar", None),
        ),
        out_specs=(
            P("tile", "nar", None),
            P("tile", "nar", None),
            P("rot", None, "tile"),
            P("rot", None),
        ),
        check_vma=False,
    )
```

```python
import jax
import jax.numpy as jnp
import numpy as np
from jax import lax
from jax.experimental import pallas as pl
from jax.experimental.pallas import tpu as pltpu
from jax.sharding import PartitionSpec as P

BF = jnp.bfloat16
F32 = jnp.float32
I32 = jnp.int32
LANES = 128
DFT = 384
HALF = 192
ROWS = 3
TILES = 64
SLOTS = 4
WIDE = ROWS * DFT
BINS = 288
GRID = 8
BASE = 16
BLOCKS = 9
XROWS = 40
SROWS = 24
SHARE = 16
SPAN = 5
ORIENTS = 8
REST = SHARE + 2 * BLOCKS
META = REST + 4 * BLOCKS - 2 * SHARE
VMEM_LIMIT = 48 * 1024 * 1024

VM = pl.BlockSpec(memory_space=pltpu.VMEM)
SM = pl.BlockSpec(memory_space=pltpu.SMEM)
NN = (((1,), (0,)), ((), ()))
NT = (((1,), (1,)), ((), ()))


def bf(x):
    return np.asarray(x, np.float32).astype(jnp.bfloat16)


def split(x):
    high = bf(x)
    return high, bf(np.asarray(x, np.float64) - high.astype(np.float64))


def tables():
    steps = np.arange(DFT)
    phase = (steps[:, None] * steps[None, :] % DFT) * (2.0 * np.pi / DFT)
    cosv, sinv = np.cos(phase), np.sin(phase)
    rows = np.concatenate([steps[0::2], steps[1::2]])
    order = np.array([ROWS * t + j for j in range(ROWS) for t in range(TILES)])
    back = np.zeros((2, DFT, 2 * HALF), np.float32)
    for n in range(2):
        back[n, :, :HALF] = cosv[rows][:, n * HALF + order]
        back[n, :, HALF:] = -sinv[rows][:, n * HALF + order]
    ch, cl = split(cosv)
    sh, sl = split(sinv)
    return bf(back), np.concatenate([ch, cl, sh, sl], 1)


def every(ref, row, step):
    return ref[pl.ds(row, TILES, stride=step), :]


def prepare(rot, index, weight, table, spectrum, grid, orient, row, col, count):
    def kernel(
        rot_ref, index_ref, weight_ref, table_ref, spec_ref, grid_ref, orient_ref, row_ref, col_ref, count_ref,
        out_ref, own_ref, table_s, weight_s, value_s, spec_s, all_s, out_s,
    ):
        table_s[...] = table_ref[...].astype(F32)
        for k in range(8):
            for o in range(2):
                w = weight_ref[k, o].astype(F32)
                for b in range(ROWS):
                    at = pl.ds(k * 2 * BLOCKS + o * BLOCKS + b, ROWS, stride=ROWS)
                    weight_s[at, :] = w[:, b * LANES : (b + 1) * LANES]

        def step(v, carry):
            rows = pl.ds(pl.multiple_of(v * 8, 8), 8)
            entry = index_ref[rows, :]
            low = entry & (LANES - 1)
            high = lax.shift_right_logical(entry, 7)
            bits = [(lax.shift_right_logical(high, b) & 1) == 1 for b in range(5)]

            def pick(c, level, first):
                if level < 0:
                    line = table_s[c : c + 1, first * LANES : (first + 1) * LANES]
                    return jnp.take_along_axis(jnp.broadcast_to(line, (8, LANES)), low, axis=1)
                return jnp.where(
                    bits[level],
                    pick(c, level - 1, first + (1 << level)),
                    pick(c, level - 1, first),
                )

            for c in range(2):
                value_s[c, rows, :] = pick(c, 4, 0) * weight_s[rows, :]
            return carry

        lax.fori_loop(0, 2 * BLOCKS, step, 0)
        for c in range(2):
            total = value_s[c, 0 : 2 * BLOCKS, :]
            for k in range(1, 8):
                total = total + value_s[c, k * 2 * BLOCKS : (k + 1) * 2 * BLOCKS, :]
            own_ref[c] = total.astype(BF).astype(F32)

        odd = (lax.broadcasted_iota(I32, (TILES, LANES), 0) & 1) == 1
        for r in range(2 * BLOCKS):
            row = jnp.where(odd, own_ref[1, r : r + 1, :], own_ref[0, r : r + 1, :])
            out_s[pl.ds(SHARE + r, TILES, stride=XROWS), :] = row
        for c in range(2):
            for b in range(ROWS):
                spec_s[c * ROWS + b] = spec_ref[c, :, b * LANES : (b + 1) * LANES].astype(F32)
        for c in range(2):
            for j in range(ROWS):
                for b in range(ROWS):
                    all_s[c * BLOCKS + j * ROWS + b] = spec_s[c * ROWS + b, pl.ds(j, TILES, stride=ROWS), :]
        for r in range(2 * BLOCKS):
            all_s[2 * BLOCKS + r] = grid_ref[:, r * LANES : (r + 1) * LANES].astype(F32)
        for r in range(SHARE):
            out_s[pl.ds(r, TILES, stride=XROWS), :] = all_s[(rot_ref[0] & 1) * SHARE + r]
        for r in range(META - REST):
            out_s[pl.ds(REST + r, TILES, stride=XROWS), :] = all_s[2 * SHARE + r]
        lane = lax.broadcasted_iota(I32, (1, LANES), 1)
        fields = jnp.where(lane == 5 * SLOTS, count_ref[0, 0], 0)
        for i in range(SLOTS):
            y, x = row_ref[i], col_ref[i]
            items = (orient_ref[i], y >> 4, y & (BASE - 1), x >> 4, x & (BASE - 1))
            for k, item in enumerate(items):
                fields = jnp.where(lane == 5 * i + k, item, fields)
        fields = jnp.broadcast_to(fields.astype(F32), (TILES, LANES))
        for r in range(META, XROWS):
            out_s[pl.ds(r, TILES, stride=XROWS), :] = fields
        out_ref[...] = out_s[...].astype(BF).reshape(out_ref.shape)

    return pl.pallas_call(
        kernel,
        out_shape=(
            jax.ShapeDtypeStruct((TILES, XROWS, LANES), BF),
            jax.ShapeDtypeStruct((2, 2 * BLOCKS, LANES), F32),
        ),
        in_specs=[SM] + [VM] * 5 + [SM] * 4,
        out_specs=(VM, VM),
        scratch_shapes=[
            pltpu.VMEM(table.shape, F32),
            pltpu.VMEM(index.shape, F32),
            pltpu.VMEM((2,) + index.shape, F32),
            pltpu.VMEM((2 * ROWS, HALF, LANES), F32),
            pltpu.VMEM((4 * BLOCKS, TILES, LANES), F32),
            pltpu.VMEM((TILES * XROWS, LANES), F32),
        ],
        compiler_params=pltpu.CompilerParams(vmem_limit_bytes=VMEM_LIMIT),
        name="prepare",
    )(rot, index, weight, table, spectrum, grid, orient, row, col, count)


def correlate(place, own, other, spectrum, filt, tabx, back):
    def kernel(at_ref, own_ref, other_ref, spec_ref, filt_ref, tabx_ref, back_ref, keep_ref, send_ref, sl_s, spec_s):
        sl_s[at_ref[1]] = own_ref[...].astype(F32).reshape(TILES * SROWS, LANES)
        sl_s[1 - at_ref[1]] = other_ref[...].astype(F32).reshape(TILES * SROWS, LANES)
        for c in range(2):
            for b in range(ROWS):
                spec_s[c * ROWS + b] = spec_ref[c, :, b * LANES : (b + 1) * LANES].astype(F32)
        for b in range(ROWS):
            spec_s[2 * ROWS + b] = filt_ref[:, b * LANES : (b + 1) * LANES].astype(F32)
        real = [[None] * (ROWS * ROWS) for _ in range(2)]
        imag = [[None] * (ROWS * ROWS) for _ in range(2)]
        for j in range(ROWS):
            for b in range(ROWS):
                mr = every(spec_s.at[b], j, ROWS)
                mi = every(spec_s.at[ROWS + b], j, ROWS)
                c = every(spec_s.at[2 * ROWS + b], j, ROWS)
                for o in range(2):
                    row = o * BLOCKS + j * ROWS + b
                    cr = c * every(sl_s.at[0], row, SROWS)
                    ci = c * every(sl_s.at[1], row, SROWS)
                    real[o][j * ROWS + b] = (mr * cr + mi * ci).astype(BF)
                    imag[o][j * ROWS + b] = (mi * cr - mr * ci).astype(BF)
        cross = jnp.concatenate(
            [
                jnp.concatenate(real[o][j * ROWS : (j + 1) * ROWS] + imag[o][j * ROWS : (j + 1) * ROWS], axis=1)
                for o in range(2)
                for j in range(ROWS)
            ],
            axis=0,
        )
        cosv, sinv = tabx_ref[:, :DFT], tabx_ref[:, 2 * DFT : 3 * DFT]
        wide = jnp.concatenate(
            [jnp.concatenate([cosv, sinv], axis=1), jnp.concatenate([-sinv, cosv], axis=1)], axis=0
        )
        halfimg = lax.dot_general(cross, wide, NN, preferred_element_type=F32).astype(BF)
        table = back_ref[at_ref[0]]
        low = at_ref[0] == 0
        for o in range(2):
            rows = halfimg[o * HALF : (o + 1) * HALF]
            both = jnp.concatenate([rows[:, :DFT], rows[:, DFT:]], axis=0)
            sums = lax.dot_general(table, both, NN, preferred_element_type=F32)
            left = jnp.concatenate([sums[:HALF, :HALF], sums[HALF:, :HALF]], axis=1)
            right = jnp.concatenate([sums[:HALF, HALF:], sums[HALF:, HALF:]], axis=1)
            keep_ref[o] = jnp.where(low, left, right).astype(BF)
            send_ref[o] = jnp.where(low, right, left).astype(BF)

    shape = jax.ShapeDtypeStruct((2, HALF, DFT), BF)
    return pl.pallas_call(
        kernel,
        out_shape=(shape, shape),
        in_specs=[SM] + [VM] * 6,
        out_specs=(VM, VM),
        scratch_shapes=[
            pltpu.VMEM((2, TILES * SROWS, LANES), F32),
            pltpu.VMEM((3 * ROWS, HALF, LANES), F32),
        ],
        compiler_params=pltpu.CompilerParams(vmem_limit_bytes=VMEM_LIMIT),
        name="correlate",
    )(place, own, other, spectrum, filt, tabx, back)


def score(rot, got, share, slices, tabx, taby):
    def kernel(
        rot_ref, got_ref, share_ref, slice_ref, tabx_ref, taby_ref,
        out_ref, place_ref, got_s, share_s, out_s,
    ):
        got_s[...] = got_ref[...].astype(F32).reshape(got_s.shape)
        side = rot_ref[0] & 1
        share_s[1 - side] = share_ref[...].astype(F32).reshape(TILES * SHARE, LANES)
        for r in range(SHARE):
            share_s[side, pl.ds(r, TILES, stride=SHARE), :] = every(got_s, r, XROWS)

        def sent(row):
            if row < 2 * SHARE:
                return every(share_s.at[row // SHARE], row % SHARE, SHARE)
            return every(got_s, REST + row - 2 * SHARE, XROWS)

        meta = every(got_s, META, XROWS)
        lane = lax.broadcasted_iota(I32, (TILES, DFT), 1).astype(F32)
        count = meta[:, 20:21]
        tri_r = lax.broadcasted_iota(I32, (TILES, TILES), 0)
        tri_c = lax.broadcasted_iota(I32, (TILES, TILES), 1)
        before = jnp.where(tri_c < tri_r, 1.0, 0.0).astype(BF)
        spread = jnp.broadcast_to(count, (TILES, LANES)).astype(BF)
        offset = lax.dot_general(before, spread, NN, preferred_element_type=F32)[:, 0:1]
        hot_x, hot_y, place = [], [], []
        for i in range(SLOTS):
            y0 = meta[:, 5 * i + 1 : 5 * i + 2] * BASE + meta[:, 5 * i + 2 : 5 * i + 3]
            x0 = meta[:, 5 * i + 3 : 5 * i + 4] * BASE + meta[:, 5 * i + 4 : 5 * i + 5]
            hot_x.append(jnp.where(lane == x0, 1.0, 0.0).astype(BF))
            hot_y.append(jnp.where(lane == y0, 1.0, 0.0).astype(BF))
            seat = jnp.where(count > float(i), offset + float(i), -1.0)
            hot = jnp.where(lane[:, :256] == seat, 1.0, 0.0)
            for h in range(2):
                place_ref[h, pl.ds(i, TILES, stride=SLOTS), :] = hot[:, h * LANES : (h + 1) * LANES]
            place.append(hot.astype(BF))
        hot_x = jnp.concatenate(hot_x, axis=0)
        hot_y = jnp.concatenate(hot_y, axis=0)
        place = jnp.concatenate(place, axis=0)
        wave = lax.dot_general(hot_x, tabx_ref[...], NN, preferred_element_type=F32)
        cx = wave[:, :DFT] + wave[:, DFT : 2 * DFT]
        sx = wave[:, 2 * DFT : 3 * DFT] + wave[:, 3 * DFT :]
        tilt = lax.dot_general(hot_y, taby_ref[...], NT, preferred_element_type=F32)
        pieces = [[] for _ in range(SLOTS)]
        for j in range(ROWS):
            for b in range(ROWS):
                r = j * ROWS + b
                cols = slice(b * LANES, (b + 1) * LANES)
                mr = sent(r)
                mi = sent(BLOCKS + r)
                plain = []
                for o in range(2):
                    sr = slice_ref[0, o * BLOCKS + r : o * BLOCKS + r + 1, :]
                    si = slice_ref[1, o * BLOCKS + r : o * BLOCKS + r + 1, :]
                    plain.append(((mr * sr + mi * si).astype(BF).astype(F32), (mi * sr - mr * si).astype(BF).astype(F32)))
                for i in range(SLOTS):
                    at = slice(i * TILES, (i + 1) * TILES)
                    second = meta[:, 5 * i : 5 * i + 1] > 0.5
                    pr = jnp.where(second, plain[1][0], plain[0][0])
                    pi = jnp.where(second, plain[1][1], plain[0][1])
                    cy = tilt[at, j : j + 1] + tilt[at, 3 + j : 4 + j]
                    sy = tilt[at, 6 + j : 7 + j] + tilt[at, 9 + j : 10 + j]
                    wx, vx = cx[at, cols], sx[at, cols]
                    pieces[i].append(cy * (pr * wx - pi * vx) - sy * (pr * vx + pi * wx))
        shifted = jnp.concatenate([jnp.concatenate(p, axis=1) for p in pieces], axis=0)
        high = shifted.astype(BF)
        bin_of = lax.shift_right_logical(lax.broadcasted_iota(I32, (WIDE, DFT), 0), 2)
        group = jnp.where(bin_of == lax.broadcasted_iota(I32, (WIDE, DFT), 1), 1.0, 0.0).astype(BF)
        low = (shifted - high.astype(F32)).astype(BF)
        binned = lax.dot_general(high, group, NN, preferred_element_type=F32)
        binned = binned + lax.dot_general(low, group, NN, preferred_element_type=F32)
        binned = binned.astype(BF)[:, :BINS]
        grid = jnp.concatenate([sent(2 * BLOCKS + r).astype(BF) for r in range(2 * BLOCKS)], axis=1)
        values = jnp.concatenate([grid[:, q * BINS : (q + 1) * BINS] for q in range(GRID)], axis=0)
        scores = lax.dot_general(values, binned, NT, preferred_element_type=F32).astype(BF)
        packed = lax.dot_general(scores, place, NN, preferred_element_type=F32)
        lanes = lax.broadcasted_iota(I32, (TILES, LANES), 1)
        extra = jnp.zeros((TILES, LANES), F32)
        for q in range(GRID):
            block = packed[q * TILES : (q + 1) * TILES]
            out_s[:, q // SPAN, q % SPAN * LANES : (q % SPAN + 1) * LANES] = block[:, :LANES]
            extra = jnp.where(lanes == q, block[:, LANES : LANES + 1], extra)
        out_s[:, 1, (SPAN - 2) * LANES : (SPAN - 1) * LANES] = extra
        out_s[:, 1, (SPAN - 1) * LANES :] = jnp.zeros((TILES, LANES), F32)
        out_ref[...] = out_s[...].astype(BF)

    return pl.pallas_call(
        kernel,
        out_shape=(
            jax.ShapeDtypeStruct((TILES, 2, SPAN * LANES), BF),
            jax.ShapeDtypeStruct((2, SLOTS * TILES, LANES), F32),
        ),
        in_specs=[SM] + [VM] * 5,
        out_specs=(VM, VM),
        scratch_shapes=[pltpu.VMEM((TILES * XROWS, LANES), F32), pltpu.VMEM((2, TILES * SHARE, LANES), F32), pltpu.VMEM((TILES, 2, SPAN * LANES), F32)],
        compiler_params=pltpu.CompilerParams(vmem_limit_bytes=VMEM_LIMIT),
        name="score",
    )(rot, got, share, slices, tabx, taby)


def expand(place, sums):
    def kernel(place_ref, sum_ref, refined_ref, top_ref):
        place = jnp.concatenate([place_ref[0].astype(BF), place_ref[1].astype(BF)], axis=1)
        lane = lax.broadcasted_iota(I32, (GRID, LANES), 1)
        row = lax.broadcasted_iota(I32, (GRID, LANES), 0)
        sums = [sum_ref[r // SPAN : r // SPAN + 1, r % SPAN * LANES : (r % SPAN + 1) * LANES] for r in range(GRID + 1)]
        last = jnp.broadcast_to(sums[GRID], (GRID, LANES))
        last = jnp.sum(jnp.where(lane == row, last, 0.0), axis=1, keepdims=True)
        rest = jnp.concatenate([jnp.concatenate(sums[:GRID], axis=0), jnp.where(lane == 0, last, 0.0)], axis=1) * (1.0 / DFT)
        parts = []
        for _ in range(3):
            parts.append(rest.astype(BF).astype(F32))
            rest = rest - parts[-1]
        parts = jnp.concatenate(parts, axis=0).astype(BF)
        out = lax.dot_general(parts, place, NT, preferred_element_type=F32)
        refined = (out[:GRID] + out[GRID : 2 * GRID]) + out[2 * GRID :]
        refined_ref[...] = refined
        top = jnp.max(refined, axis=0, keepdims=True)
        top_ref[...] = jnp.broadcast_to(top[None], top_ref.shape)

    return pl.pallas_call(
        kernel,
        out_shape=(
            jax.ShapeDtypeStruct((GRID, SLOTS * TILES), F32),
            jax.ShapeDtypeStruct((TILES, 1, SLOTS * TILES), F32),
        ),
        in_specs=[VM] * 2,
        out_specs=(VM, VM),
        name="expand",
    )(place, sums)


def highest(tops, scores):
    def kernel(top_ref, score_ref, best_ref, out_ref):
        best_ref[...] = jnp.max(top_ref[...], axis=0)
        out_ref[...] = score_ref[...]

    return pl.pallas_call(
        kernel,
        out_shape=(jax.ShapeDtypeStruct(tops.shape[1:], F32), jax.ShapeDtypeStruct(scores.shape, F32)),
        in_specs=[VM] * 2,
        out_specs=(VM, VM),
        name="highest",
    )(tops, scores)


def finish(parts):
    def kernel(*refs):
        ins, (top_ref, mean_ref) = refs[:4], refs[4:]
        for b in range(ROWS):
            cols = slice(b * LANES, (b + 1) * LANES)
            tops = [ref[0, :, cols].astype(F32) for ref in ins]
            sums = [ref[1, :, cols].astype(F32) for ref in ins]
            top_ref[pl.ds(b, HALF, stride=ROWS), :] = jnp.maximum(
                jnp.maximum(tops[0], tops[1]), jnp.maximum(tops[2], tops[3])
            )
            total = (sums[0] + sums[1]) + (sums[2] + sums[3])
            mean_ref[pl.ds(b, HALF, stride=ROWS), :] = total * (1.0 / ORIENTS)

    shape = jax.ShapeDtypeStruct((ROWS * HALF, LANES), F32)
    return pl.pallas_call(
        kernel,
        out_shape=(shape, shape),
        in_specs=[VM] * 4,
        out_specs=(VM, VM),
        cost_estimate=pl.CostEstimate(flops=1, transcendentals=0, bytes_accessed=1),
        name="finish",
    )(*parts)


def exchange(x, axis, bit):
    size = lax.axis_size(axis)
    return lax.ppermute(x, axis, [(k, k ^ bit) for k in range(size)])


def shards(
    interp_index,
    interp_weight,
    volume,
    spectrum,
    ctf_filter,
    peak_count,
    peak_orient,
    peak_row,
    peak_col,
    ctf_grid,
):
    back, tabx = [jnp.asarray(t) for t in tables()]
    nar = lax.axis_index("nar")
    tile = lax.axis_index("tile")

    taby = lax.dynamic_slice_in_dim(tabx, (nar * TILES + tile) * ROWS, ROWS, 0)
    taby = taby.reshape(ROWS, 4, DFT).transpose(1, 0, 2).reshape(4 * ROWS, DFT)
    taby = jnp.pad(taby, ((0, 16 - 4 * ROWS), (0, 0)))

    grid = ctf_grid.reshape(GRID, TILES, BINS).transpose(1, 0, 2).reshape(TILES, GRID * BINS)
    spec = spectrum.reshape(2, HALF, DFT)
    filt = ctf_filter.reshape(HALF, DFT)
    rot = lax.axis_index("rot").reshape(1)
    blocks, slices = prepare(
        rot,
        interp_index.reshape(-1, LANES),
        interp_weight.reshape(8, 2, ROWS, DFT),
        volume.reshape(2, -1),
        spec,
        grid,
        peak_orient,
        peak_row,
        peak_col,
        peak_count,
    )
    got = lax.all_to_all(blocks, "tile", 0, 0, tiled=True)
    share, mine = exchange(got[:, :SHARE], "rot", 1), got[:, SHARE:]
    other = exchange(mine, "tile", 1)
    keep, send = correlate(jnp.stack([nar, tile % 2]), mine, other, spec, filt, tabx, back)
    got, share, send = lax.optimization_barrier((got, share, send))
    extra_rows = exchange(send, "nar", 1)
    packed, place = score(rot, got, share, slices, tabx, taby)
    sums = lax.all_to_all(packed, "tile", 0, 0, tiled=True)

    corr = (keep.astype(F32) + extra_rows.astype(F32)) * (1.0 / DFT)
    stats = jnp.stack([jnp.maximum(corr[0], corr[1]), corr[0] + corr[1]]).astype(BF)
    others = [exchange(stats, "rot", bit) for bit in (1, 2, 3)]

    sums = jnp.sum(sums.astype(F32), axis=0)
    sums = sums + exchange(sums, "nar", 1)
    refined, tops = expand(place, sums)
    tops = lax.all_to_all(tops, "tile", 0, 0)
    peak, mean = finish([stats] + others)
    tops, peak, mean = lax.optimization_barrier((tops, peak, mean))
    best, refined = highest(tops, refined)
    return (
        peak.reshape(1, 1, -1),
        mean.reshape(1, 1, -1),
        refined.T.reshape(1, SLOTS * TILES, GRID),
        best,
    )


def solution(mesh):
    return jax.shard_map(
        shards,
        mesh=mesh,
        in_specs=(
            P(None, "rot", "nar", "tile", None),
            P(None, "rot", "nar", "tile", None),
            P(None, "nar", "tile", None),
            P(None, "tile", "nar", None, None),
            P("tile", "nar", None, None),
            P("rot", "tile"),
            P(("rot", "tile")),
            P(("rot", "tile")),
            P(("rot", "tile")),
            P("tile", "nar", None),
        ),
        out_specs=(
            P("tile", "nar", None),
            P("tile", "nar", None),
            P("rot", None, "tile"),
            P("rot", None),
        ),
        check_vma=False,
    )
```

```python
import jax
import jax.numpy as jnp
import numpy as np
from jax import lax
from jax.experimental import pallas as pl
from jax.experimental.pallas import tpu as pltpu
from jax.sharding import PartitionSpec as P

BF = jnp.bfloat16
F32 = jnp.float32
I32 = jnp.int32
LANES = 128
DFT = 384
HALF = 192
ROWS = 3
TILES = 64
SLOTS = 4
WIDE = ROWS * DFT
BINS = 288
GRID = 8
BASE = 16
BLOCKS = 9
XROWS = 40
SROWS = 24
SHARE = 16
SPAN = 5
ORIENTS = 8
REST = SHARE + 2 * BLOCKS
META = REST + 4 * BLOCKS - 2 * SHARE
VMEM_LIMIT = 48 * 1024 * 1024

VM = pl.BlockSpec(memory_space=pltpu.VMEM)
SM = pl.BlockSpec(memory_space=pltpu.SMEM)
HB = pl.BlockSpec(memory_space=pltpu.HBM)
NN = (((1,), (0,)), ((), ()))
NT = (((1,), (1,)), ((), ()))


def bf(x):
    return np.asarray(x, np.float32).astype(jnp.bfloat16)


def split(x):
    high = bf(x)
    return high, bf(np.asarray(x, np.float64) - high.astype(np.float64))


def tables():
    steps = np.arange(DFT)
    phase = (steps[:, None] * steps[None, :] % DFT) * (2.0 * np.pi / DFT)
    cosv, sinv = np.cos(phase), np.sin(phase)
    rows = np.concatenate([steps[0::2], steps[1::2]])
    order = np.array([ROWS * t + j for j in range(ROWS) for t in range(TILES)])
    back = np.zeros((2, DFT, 2 * HALF), np.float32)
    for n in range(2):
        back[n, :, :HALF] = cosv[rows][:, n * HALF + order]
        back[n, :, HALF:] = -sinv[rows][:, n * HALF + order]
    ch, cl = split(cosv)
    sh, sl = split(sinv)
    return bf(back), np.concatenate([ch, cl, sh, sl], 1)


def stay(x):
    return pltpu.with_memory_space_constraint(x, pltpu.HBM)


def every(ref, row, step):
    return ref[pl.ds(row, TILES, stride=step), :]


def prepare(rot, index, weight, table, spectrum, grid, orient, row, col, count):
    def kernel(
        rot_ref, count_ref, *refs,
    ):
        sources, (out_ref, own_ref), scratch = refs[:8], refs[8:10], refs[10:]
        targets, (sems, table_s, weight_s, value_s, spec_s, grid_s, all_s, out_s) = scratch[:8], scratch[8:]
        copies = [pltpu.make_async_copy(a, b, sems.at[i]) for i, (a, b) in enumerate(zip(sources, targets))]
        for copy in copies:
            copy.start()
        index_ref, weight_ref, table_ref, spec_ref, grid_ref, orient_ref, row_ref, col_ref = targets
        for copy in copies[:3]:
            copy.wait()
        table_s[...] = table_ref[...].astype(F32)
        for k in range(8):
            for j in range(ROWS):
                w = weight_ref[k, 0, j].astype(F32)
                for b in range(ROWS):
                    at = pl.ds(k * 2 * BLOCKS + j * ROWS + b, 2, stride=BLOCKS)
                    weight_s[at, :] = w[:, b * LANES : (b + 1) * LANES]

        def step(v, carry):
            rows = pl.ds(pl.multiple_of(v * 8, 8), 8)
            entry = index_ref[rows, :]
            low = entry & (LANES - 1)
            high = lax.shift_right_logical(entry, 7)
            bits = [(lax.shift_right_logical(high, b) & 1) == 1 for b in range(5)]

            def pick(c, level, first):
                if level < 0:
                    line = table_s[c : c + 1, first * LANES : (first + 1) * LANES]
                    return jnp.take_along_axis(jnp.broadcast_to(line, (8, LANES)), low, axis=1)
                return jnp.where(
                    bits[level],
                    pick(c, level - 1, first + (1 << level)),
                    pick(c, level - 1, first),
                )

            for c in range(2):
                value_s[c, rows, :] = pick(c, 4, 0) * weight_s[rows, :]
            return carry

        lax.fori_loop(0, 2 * BLOCKS, step, 0)
        for c in range(2):
            total = value_s[c, 0 : 2 * BLOCKS, :]
            for k in range(1, 8):
                total = total + value_s[c, k * 2 * BLOCKS : (k + 1) * 2 * BLOCKS, :]
            own_ref[c] = total.astype(BF).astype(F32)

        for copy in copies[3:]:
            copy.wait()
        odd = (lax.broadcasted_iota(I32, (TILES, LANES), 0) & 1) == 1
        for r in range(2 * BLOCKS):
            row = jnp.where(odd, own_ref[1, r : r + 1, :], own_ref[0, r : r + 1, :])
            out_s[pl.ds(SHARE + r, TILES, stride=XROWS), :] = row
        for c in range(2):
            for b in range(ROWS):
                spec_s[c * ROWS + b] = spec_ref[c, :, b * LANES : (b + 1) * LANES].astype(F32)
        for c in range(2):
            for j in range(ROWS):
                for b in range(ROWS):
                    all_s[c * BLOCKS + j * ROWS + b] = spec_s[c * ROWS + b, pl.ds(j, TILES, stride=ROWS), :]
        for k in range(TILES * BINS // LANES):
            grid_s[k * GRID : (k + 1) * GRID, :] = grid_ref[:, k * LANES : (k + 1) * LANES].astype(F32)
        for a in range(4):
            first, shift = divmod(a * BINS, LANES)
            pieces = []
            for q in range(GRID):
                blocks = [
                    grid_s[pl.ds((first + k) * GRID + q, TILES // 4, stride=BLOCKS * GRID), :] for k in range(3)
                ]
                pieces.append(jnp.concatenate(blocks, axis=1)[:, shift : shift + BINS])
            row = jnp.concatenate(pieces, axis=1)
            for r in range(2 * BLOCKS):
                all_s[2 * BLOCKS + r, pl.ds(a, TILES // 4, stride=4), :] = row[:, r * LANES : (r + 1) * LANES]
        for r in range(SHARE):
            out_s[pl.ds(r, TILES, stride=XROWS), :] = all_s[(rot_ref[0] & 1) * SHARE + r]
        for r in range(META - REST):
            out_s[pl.ds(REST + r, TILES, stride=XROWS), :] = all_s[2 * SHARE + r]
        lane = lax.broadcasted_iota(I32, (1, LANES), 1)
        fields = jnp.where(lane == 5 * SLOTS, count_ref[0, 0], 0)
        for i in range(SLOTS):
            y, x = row_ref[i], col_ref[i]
            items = (orient_ref[i], y >> 4, y & (BASE - 1), x >> 4, x & (BASE - 1))
            for k, item in enumerate(items):
                fields = jnp.where(lane == 5 * i + k, item, fields)
        fields = jnp.broadcast_to(fields.astype(F32), (TILES, LANES))
        for r in range(META, XROWS):
            out_s[pl.ds(r, TILES, stride=XROWS), :] = fields
        out_ref[...] = out_s[...].astype(BF).reshape(out_ref.shape)

    return pl.pallas_call(
        kernel,
        out_shape=(
            jax.ShapeDtypeStruct((TILES, XROWS, LANES), BF),
            jax.ShapeDtypeStruct((2, 2 * BLOCKS, LANES), F32),
        ),
        in_specs=[SM, SM] + [HB] * 8,
        out_specs=(VM, VM),
        scratch_shapes=[pltpu.VMEM(x.shape, x.dtype) for x in (index, weight, table, spectrum, grid)]
        + [pltpu.SMEM(x.shape, x.dtype) for x in (orient, row, col)]
        + [
            pltpu.SemaphoreType.DMA((8,)),
            pltpu.VMEM(table.shape, F32),
            pltpu.VMEM(index.shape, F32),
            pltpu.VMEM((2,) + index.shape, F32),
            pltpu.VMEM((2 * ROWS, HALF, LANES), F32),
            pltpu.VMEM((GRID * TILES * BINS // LANES, LANES), F32),
            pltpu.VMEM((4 * BLOCKS, TILES, LANES), F32),
            pltpu.VMEM((TILES * XROWS, LANES), F32),
        ],
        compiler_params=pltpu.CompilerParams(vmem_limit_bytes=VMEM_LIMIT),
        name="prepare",
    )(rot, count, *[stay(x) for x in (index, weight, table, spectrum, grid, orient, row, col)])


def correlate(place, own, other, spectrum, filt, tabx, back):
    def kernel(
        at_ref, own_ref, other_ref, spec_hbm, filt_hbm, tabx_ref, back_ref, keep_ref, send_ref,
        sl_s, spec_s, spec_ref, filt_ref, sems,
    ):
        copies = [
            pltpu.make_async_copy(spec_hbm, spec_ref, sems.at[0]),
            pltpu.make_async_copy(filt_hbm, filt_ref, sems.at[1]),
        ]
        for copy in copies:
            copy.start()
        sl_s[at_ref[1]] = own_ref[...].astype(F32).reshape(TILES * SROWS, LANES)
        sl_s[1 - at_ref[1]] = other_ref[...].astype(F32).reshape(TILES * SROWS, LANES)
        for copy in copies:
            copy.wait()
        for c in range(2):
            for b in range(ROWS):
                spec_s[c * ROWS + b] = spec_ref[c, :, b * LANES : (b + 1) * LANES].astype(F32)
        for b in range(ROWS):
            spec_s[2 * ROWS + b] = filt_ref[:, b * LANES : (b + 1) * LANES].astype(F32)
        real = [[None] * (ROWS * ROWS) for _ in range(2)]
        imag = [[None] * (ROWS * ROWS) for _ in range(2)]
        for j in range(ROWS):
            for b in range(ROWS):
                mr = every(spec_s.at[b], j, ROWS)
                mi = every(spec_s.at[ROWS + b], j, ROWS)
                c = every(spec_s.at[2 * ROWS + b], j, ROWS)
                for o in range(2):
                    row = o * BLOCKS + j * ROWS + b
                    cr = c * every(sl_s.at[0], row, SROWS)
                    ci = c * every(sl_s.at[1], row, SROWS)
                    real[o][j * ROWS + b] = (mr * cr + mi * ci).astype(BF)
                    imag[o][j * ROWS + b] = (mi * cr - mr * ci).astype(BF)
        cross = jnp.concatenate(
            [
                jnp.concatenate(real[o][j * ROWS : (j + 1) * ROWS] + imag[o][j * ROWS : (j + 1) * ROWS], axis=1)
                for o in range(2)
                for j in range(ROWS)
            ],
            axis=0,
        )
        cosv, sinv = tabx_ref[:, :DFT], tabx_ref[:, 2 * DFT : 3 * DFT]
        wide = jnp.concatenate(
            [jnp.concatenate([cosv, sinv], axis=1), jnp.concatenate([-sinv, cosv], axis=1)], axis=0
        )
        halfimg = lax.dot_general(cross, wide, NN, preferred_element_type=F32).astype(BF)
        table = back_ref[at_ref[0]]
        low = at_ref[0] == 0
        for o in range(2):
            rows = halfimg[o * HALF : (o + 1) * HALF]
            both = jnp.concatenate([rows[:, :DFT], rows[:, DFT:]], axis=0)
            sums = lax.dot_general(table, both, NN, preferred_element_type=F32)
            left = jnp.concatenate([sums[:HALF, :HALF], sums[HALF:, :HALF]], axis=1)
            right = jnp.concatenate([sums[:HALF, HALF:], sums[HALF:, HALF:]], axis=1)
            keep_ref[o] = jnp.where(low, left, right).astype(BF)
            send_ref[o] = jnp.where(low, right, left).astype(BF)

    shape = jax.ShapeDtypeStruct((2, HALF, DFT), BF)
    return pl.pallas_call(
        kernel,
        out_shape=(shape, shape),
        in_specs=[SM, VM, VM, HB, HB, VM, VM],
        out_specs=(VM, VM),
        scratch_shapes=[
            pltpu.VMEM((2, TILES * SROWS, LANES), F32),
            pltpu.VMEM((3 * ROWS, HALF, LANES), F32),
            pltpu.VMEM(spectrum.shape, BF),
            pltpu.VMEM(filt.shape, BF),
            pltpu.SemaphoreType.DMA((2,)),
        ],
        compiler_params=pltpu.CompilerParams(vmem_limit_bytes=VMEM_LIMIT),
        name="correlate",
    )(place, own, other, stay(spectrum), stay(filt), tabx, back)


def score(rot, got, share, slices, tabx, taby):
    def kernel(
        rot_ref, got_ref, share_ref, slice_ref, tabx_ref, taby_ref,
        out_ref, place_hbm, got_s, share_s, place_s, place_ref, sem, out_s,
    ):
        got_s[...] = got_ref[...].astype(F32).reshape(got_s.shape)
        side = rot_ref[0] & 1
        share_s[1 - side] = share_ref[...].astype(F32).reshape(TILES * SHARE, LANES)
        for r in range(SHARE):
            share_s[side, pl.ds(r, TILES, stride=SHARE), :] = every(got_s, r, XROWS)

        def sent(row):
            if row < 2 * SHARE:
                return every(share_s.at[row // SHARE], row % SHARE, SHARE)
            return every(got_s, REST + row - 2 * SHARE, XROWS)

        meta = every(got_s, META, XROWS)
        lane = lax.broadcasted_iota(I32, (TILES, DFT), 1).astype(F32)
        count = meta[:, 20:21]
        tri_r = lax.broadcasted_iota(I32, (TILES, TILES), 0)
        tri_c = lax.broadcasted_iota(I32, (TILES, TILES), 1)
        before = jnp.where(tri_c < tri_r, 1.0, 0.0).astype(BF)
        spread = jnp.broadcast_to(count, (TILES, LANES)).astype(BF)
        offset = lax.dot_general(before, spread, NN, preferred_element_type=F32)[:, 0:1]
        hot_x, hot_y, place = [], [], []
        for i in range(SLOTS):
            y0 = meta[:, 5 * i + 1 : 5 * i + 2] * BASE + meta[:, 5 * i + 2 : 5 * i + 3]
            x0 = meta[:, 5 * i + 3 : 5 * i + 4] * BASE + meta[:, 5 * i + 4 : 5 * i + 5]
            hot_x.append(jnp.where(lane == x0, 1.0, 0.0).astype(BF))
            hot_y.append(jnp.where(lane == y0, 1.0, 0.0).astype(BF))
            seat = jnp.where(count > float(i), offset + float(i), -1.0)
            hot = jnp.where(lane[:, :256] == seat, 1.0, 0.0)
            for h in range(2):
                place_s[h, pl.ds(i, TILES, stride=SLOTS), :] = hot[:, h * LANES : (h + 1) * LANES]
            place.append(hot.astype(BF))
        place_ref[...] = place_s[...].astype(BF)
        leave = pltpu.make_async_copy(place_ref, place_hbm, sem)
        leave.start()
        hot_x = jnp.concatenate(hot_x, axis=0)
        hot_y = jnp.concatenate(hot_y, axis=0)
        place = jnp.concatenate(place, axis=0)
        wave = lax.dot_general(hot_x, tabx_ref[...], NN, preferred_element_type=F32)
        cx = wave[:, :DFT] + wave[:, DFT : 2 * DFT]
        sx = wave[:, 2 * DFT : 3 * DFT] + wave[:, 3 * DFT :]
        tilt = lax.dot_general(hot_y, taby_ref[...], NT, preferred_element_type=F32)
        pieces = [[] for _ in range(SLOTS)]
        second = [jnp.broadcast_to(meta[:, 5 * i : 5 * i + 1], (TILES, LANES)) > 0.5 for i in range(SLOTS)]
        for j in range(ROWS):
            cosines = jnp.broadcast_to(tilt[:, j : j + 1] + tilt[:, 3 + j : 4 + j], (SLOTS * TILES, LANES))
            sines = jnp.broadcast_to(tilt[:, 6 + j : 7 + j] + tilt[:, 9 + j : 10 + j], (SLOTS * TILES, LANES))
            for b in range(ROWS):
                r = j * ROWS + b
                cols = slice(b * LANES, (b + 1) * LANES)
                mr = sent(r)
                mi = sent(BLOCKS + r)
                plain = []
                for o in range(2):
                    sr = slice_ref[0, o * BLOCKS + r : o * BLOCKS + r + 1, :]
                    si = slice_ref[1, o * BLOCKS + r : o * BLOCKS + r + 1, :]
                    plain.append(((mr * sr + mi * si).astype(BF).astype(F32), (mi * sr - mr * si).astype(BF).astype(F32)))
                for i in range(SLOTS):
                    at = slice(i * TILES, (i + 1) * TILES)
                    pr = jnp.where(second[i], plain[1][0], plain[0][0])
                    pi = jnp.where(second[i], plain[1][1], plain[0][1])
                    cy, sy = cosines[at], sines[at]
                    wx, vx = cx[at, cols], sx[at, cols]
                    pieces[i].append(cy * (pr * wx - pi * vx) - sy * (pr * vx + pi * wx))
        shifted = jnp.concatenate([jnp.concatenate(p, axis=1) for p in pieces], axis=0)
        high = shifted.astype(BF)
        bin_of = lax.shift_right_logical(lax.broadcasted_iota(I32, (WIDE, DFT), 0), 2)
        group = jnp.where(bin_of == lax.broadcasted_iota(I32, (WIDE, DFT), 1), 1.0, 0.0).astype(BF)
        low = (shifted - high.astype(F32)).astype(BF)
        binned = lax.dot_general(high, group, NN, preferred_element_type=F32)
        binned = binned + lax.dot_general(low, group, NN, preferred_element_type=F32)
        binned = binned.astype(BF)[:, :BINS]
        grid = jnp.concatenate([sent(2 * BLOCKS + r).astype(BF) for r in range(2 * BLOCKS)], axis=1)
        values = jnp.concatenate([grid[:, q * BINS : (q + 1) * BINS] for q in range(GRID)], axis=0)
        scores = lax.dot_general(values, binned, NT, preferred_element_type=F32).astype(BF)
        packed = lax.dot_general(scores, place, NN, preferred_element_type=F32)
        lanes = lax.broadcasted_iota(I32, (TILES, LANES), 1)
        extra = jnp.zeros((TILES, LANES), F32)
        for q in range(GRID):
            block = packed[q * TILES : (q + 1) * TILES]
            out_s[:, q // SPAN, q % SPAN * LANES : (q % SPAN + 1) * LANES] = block[:, :LANES]
            extra = jnp.where(lanes == q, block[:, LANES : LANES + 1], extra)
        out_s[:, 1, (SPAN - 2) * LANES : (SPAN - 1) * LANES] = extra
        out_s[:, 1, (SPAN - 1) * LANES :] = jnp.zeros((TILES, LANES), F32)
        out_ref[...] = out_s[...].astype(BF)
        leave.wait()

    return pl.pallas_call(
        kernel,
        out_shape=(
            jax.ShapeDtypeStruct((TILES, 2, SPAN * LANES), BF),
            jax.ShapeDtypeStruct((2, SLOTS * TILES, LANES), BF),
        ),
        in_specs=[SM] + [VM] * 5,
        out_specs=(VM, HB),
        scratch_shapes=[pltpu.VMEM((TILES * XROWS, LANES), F32), pltpu.VMEM((2, TILES * SHARE, LANES), F32), pltpu.VMEM((2, SLOTS * TILES, LANES), F32), pltpu.VMEM((2, SLOTS * TILES, LANES), BF), pltpu.SemaphoreType.DMA, pltpu.VMEM((TILES, 2, SPAN * LANES), F32)],
        compiler_params=pltpu.CompilerParams(vmem_limit_bytes=VMEM_LIMIT),
        cost_estimate=pl.CostEstimate(flops=6_000_000_000, transcendentals=0, bytes_accessed=8_000_000),
        name="score",
    )(rot, got, share, slices, tabx, taby)


def expand(place, sums):
    def kernel(place_ref, sum_ref, refined_ref, top_ref):
        place = jnp.concatenate([place_ref[0], place_ref[1]], axis=1)
        lane = lax.broadcasted_iota(I32, (GRID, LANES), 1)
        row = lax.broadcasted_iota(I32, (GRID, LANES), 0)
        sums = [sum_ref[r // SPAN : r // SPAN + 1, r % SPAN * LANES : (r % SPAN + 1) * LANES] for r in range(GRID + 1)]
        last = jnp.broadcast_to(sums[GRID], (GRID, LANES))
        last = jnp.sum(jnp.where(lane == row, last, 0.0), axis=1, keepdims=True)
        rest = jnp.concatenate([jnp.concatenate(sums[:GRID], axis=0), jnp.where(lane == 0, last, 0.0)], axis=1) * (1.0 / DFT)
        parts = []
        for _ in range(3):
            parts.append(rest.astype(BF).astype(F32))
            rest = rest - parts[-1]
        parts = jnp.concatenate(parts, axis=0).astype(BF)
        out = lax.dot_general(parts, place, NT, preferred_element_type=F32)
        refined = (out[:GRID] + out[GRID : 2 * GRID]) + out[2 * GRID :]
        refined_ref[...] = refined
        top = jnp.max(refined, axis=0, keepdims=True)
        top_ref[...] = jnp.broadcast_to(top[None], top_ref.shape)

    return pl.pallas_call(
        kernel,
        out_shape=(
            jax.ShapeDtypeStruct((GRID, SLOTS * TILES), F32),
            jax.ShapeDtypeStruct((TILES, 1, SLOTS * TILES), F32),
        ),
        in_specs=[VM] * 2,
        out_specs=(VM, VM),
        name="expand",
    )(place, sums)


def finish(parts):
    def kernel(*refs):
        ins, (top_ref, mean_ref) = refs[:4], refs[4:]
        for b in range(ROWS):
            cols = slice(b * LANES, (b + 1) * LANES)
            tops = [ref[0, :, cols].astype(F32) for ref in ins]
            sums = [ref[1, :, cols].astype(F32) for ref in ins]
            top_ref[pl.ds(b, HALF, stride=ROWS), :] = jnp.maximum(
                jnp.maximum(tops[0], tops[1]), jnp.maximum(tops[2], tops[3])
            )
            total = (sums[0] + sums[1]) + (sums[2] + sums[3])
            mean_ref[pl.ds(b, HALF, stride=ROWS), :] = total * (1.0 / ORIENTS)

    shape = jax.ShapeDtypeStruct((ROWS * HALF, LANES), F32)
    return pl.pallas_call(
        kernel,
        out_shape=(shape, shape),
        in_specs=[VM] * 4,
        out_specs=(VM, VM),
        cost_estimate=pl.CostEstimate(flops=1, transcendentals=0, bytes_accessed=1),
        name="finish",
    )(*parts)


def exchange(x, axis, bit):
    size = lax.axis_size(axis)
    return lax.ppermute(x, axis, [(k, k ^ bit) for k in range(size)])


def shards(
    interp_index,
    interp_weight,
    volume,
    spectrum,
    ctf_filter,
    peak_count,
    peak_orient,
    peak_row,
    peak_col,
    ctf_grid,
):
    back, tabx = [jnp.asarray(t) for t in tables()]
    nar = lax.axis_index("nar")
    tile = lax.axis_index("tile")

    taby = lax.dynamic_slice_in_dim(tabx, (nar * TILES + tile) * ROWS, ROWS, 0)
    taby = taby.reshape(ROWS, 4, DFT).transpose(1, 0, 2).reshape(4 * ROWS, DFT)
    taby = jnp.pad(taby, ((0, 16 - 4 * ROWS), (0, 0)))

    grid = ctf_grid.reshape(GRID, TILES * BINS)
    spec = spectrum.reshape(2, HALF, DFT)
    filt = ctf_filter.reshape(HALF, DFT)
    rot = lax.axis_index("rot").reshape(1)
    blocks, slices = prepare(
        rot,
        interp_index.reshape(-1, LANES),
        interp_weight.transpose(0, 2, 3, 1, 4),
        volume.reshape(2, -1),
        spec,
        grid,
        peak_orient,
        peak_row,
        peak_col,
        peak_count,
    )
    got = lax.all_to_all(blocks, "tile", 0, 0, tiled=True)
    share, mine = exchange(got[:, :SHARE], "rot", 1), got[:, SHARE:]
    other = exchange(mine, "tile", 1)
    keep, send = correlate(jnp.stack([nar, tile % 2]), mine, other, spec, filt, tabx, back)
    got, send = lax.optimization_barrier((got, send))
    extra_rows = exchange(send, "nar", 1)
    packed, place = score(rot, got, share, slices, tabx, taby)
    sums = lax.all_to_all(packed, "tile", 0, 0, tiled=True)

    corr = (keep.astype(F32) + extra_rows.astype(F32)) * (1.0 / DFT)
    stats = jnp.stack([jnp.maximum(corr[0], corr[1]), corr[0] + corr[1]]).astype(BF)
    others = [exchange(stats, "rot", bit) for bit in (1, 2, 3)]

    sums = jnp.sum(sums.astype(F32), axis=0)
    sums = sums + exchange(sums, "nar", 1)
    refined, tops = expand(place, sums)
    tops = lax.all_to_all(tops, "tile", 0, 0)
    peak, mean = finish([stats] + others)
    tops, peak, mean = lax.optimization_barrier((tops, peak, mean))
    best = jnp.max(tops, axis=0)
    return (
        peak.reshape(1, 1, -1),
        mean.reshape(1, 1, -1),
        refined.T.reshape(1, SLOTS * TILES, GRID),
        best,
    )


def solution(mesh):
    return jax.shard_map(
        shards,
        mesh=mesh,
        in_specs=(
            P(None, "rot", "nar", "tile", None),
            P(None, "rot", "nar", "tile", None),
            P(None, "nar", "tile", None),
            P(None, "tile", "nar", None, None),
            P("tile", "nar", None, None),
            P("rot", "tile"),
            P(("rot", "tile")),
            P(("rot", "tile")),
            P(("rot", "tile")),
            P("tile", "nar", None),
        ),
        out_specs=(
            P("tile", "nar", None),
            P("tile", "nar", None),
            P("rot", None, "tile"),
            P("rot", None),
        ),
        check_vma=False,
    )
```

```python
import jax
import jax.numpy as jnp
import numpy as np
from jax import lax
from jax.experimental import pallas as pl
from jax.experimental.pallas import tpu as pltpu
from jax.sharding import PartitionSpec as P

BF = jnp.bfloat16
F32 = jnp.float32
I32 = jnp.int32
LANES = 128
DFT = 384
HALF = 192
ROWS = 3
TILES = 64
SLOTS = 4
WIDE = ROWS * DFT
BINS = 288
GRID = 8
BASE = 16
BLOCKS = 9
XROWS = 40
SROWS = 24
SHARE = 16
SPAN = 5
ORIENTS = 8
REST = SHARE + 2 * BLOCKS
META = REST + 4 * BLOCKS - 2 * SHARE
VMEM_LIMIT = 16 * 1024 * 1024

VM = pl.BlockSpec(memory_space=pltpu.VMEM)
SM = pl.BlockSpec(memory_space=pltpu.SMEM)
HB = pl.BlockSpec(memory_space=pltpu.HBM)
NN = (((1,), (0,)), ((), ()))
NT = (((1,), (1,)), ((), ()))


def bf(x):
    return np.asarray(x, np.float32).astype(jnp.bfloat16)


def tables():
    steps = np.arange(DFT)
    phase = (steps[:, None] * steps[None, :] % DFT) * (2.0 * np.pi / DFT)
    cosv, sinv = np.cos(phase), np.sin(phase)
    rows = np.concatenate([steps[0::2], steps[1::2]])
    order = np.array([ROWS * t + j for j in range(ROWS) for t in range(TILES)])
    back = np.zeros((2, DFT, 2 * HALF), np.float32)
    for n in range(2):
        back[n, :, :HALF] = cosv[rows][:, n * HALF + order]
        back[n, :, HALF:] = -sinv[rows][:, n * HALF + order]
    return bf(back), bf(np.concatenate([cosv, sinv], 1))


def stay(x):
    return pltpu.with_memory_space_constraint(x, pltpu.HBM)


def every(ref, row, step):
    return ref[pl.ds(row, TILES, stride=step), :]


def prepare(rot, index, weight, table, spectrum, grid, orient, row, col, count):
    def kernel(
        rot_ref, count_ref, *refs,
    ):
        sources, (out_ref, own_ref), scratch = refs[:8], refs[8:10], refs[10:]
        targets, (sems, table_s, weight_s, value_s, spec_s, grid_s, all_s, out_s) = scratch[:8], scratch[8:]
        copies = [pltpu.make_async_copy(a, b, sems.at[i]) for i, (a, b) in enumerate(zip(sources, targets))]
        for copy in copies:
            copy.start()
        index_ref, weight_ref, table_ref, spec_ref, grid_ref, orient_ref, row_ref, col_ref = targets
        for copy in copies[:3]:
            copy.wait()
        table_s[...] = table_ref[...].astype(F32)
        for k in range(8):
            for j in range(ROWS):
                w = weight_ref[k, 0, j].astype(F32)
                for b in range(ROWS):
                    at = pl.ds(k * 2 * BLOCKS + j * ROWS + b, 2, stride=BLOCKS)
                    weight_s[at, :] = w[:, b * LANES : (b + 1) * LANES]

        def step(v, carry):
            rows = pl.ds(pl.multiple_of(v * 8, 8), 8)
            entry = index_ref[rows, :]
            low = entry & (LANES - 1)
            high = lax.shift_right_logical(entry, 7)
            bits = [(lax.shift_right_logical(high, b) & 1) == 1 for b in range(5)]

            def pick(c, level, first):
                if level < 0:
                    line = table_s[c : c + 1, first * LANES : (first + 1) * LANES]
                    return jnp.take_along_axis(jnp.broadcast_to(line, (8, LANES)), low, axis=1)
                return jnp.where(
                    bits[level],
                    pick(c, level - 1, first + (1 << level)),
                    pick(c, level - 1, first),
                )

            for c in range(2):
                value_s[c, rows, :] = pick(c, 4, 0) * weight_s[rows, :]
            return carry

        lax.fori_loop(0, 2 * BLOCKS, step, 0)
        for c in range(2):
            total = value_s[c, 0 : 2 * BLOCKS, :]
            for k in range(1, 8):
                total = total + value_s[c, k * 2 * BLOCKS : (k + 1) * 2 * BLOCKS, :]
            own_ref[c] = total.astype(BF).astype(F32)

        for copy in copies[3:]:
            copy.wait()
        odd = (lax.broadcasted_iota(I32, (TILES, LANES), 0) & 1) == 1
        for r in range(2 * BLOCKS):
            row = jnp.where(odd, own_ref[1, r : r + 1, :], own_ref[0, r : r + 1, :])
            out_s[pl.ds(SHARE + r, TILES, stride=XROWS), :] = row
        for c in range(2):
            for b in range(ROWS):
                spec_s[c * ROWS + b] = spec_ref[c, :, b * LANES : (b + 1) * LANES].astype(F32)
        for c in range(2):
            for j in range(ROWS):
                for b in range(ROWS):
                    all_s[c * BLOCKS + j * ROWS + b] = spec_s[c * ROWS + b, pl.ds(j, TILES, stride=ROWS), :]
        for k in range(TILES * BINS // LANES):
            grid_s[k * GRID : (k + 1) * GRID, :] = grid_ref[:, k * LANES : (k + 1) * LANES].astype(F32)
        for a in range(4):
            first, shift = divmod(a * BINS, LANES)
            pieces = []
            for q in range(GRID):
                blocks = [
                    grid_s[pl.ds((first + k) * GRID + q, TILES // 4, stride=BLOCKS * GRID), :] for k in range(3)
                ]
                pieces.append(jnp.concatenate(blocks, axis=1)[:, shift : shift + BINS])
            row = jnp.concatenate(pieces, axis=1)
            for r in range(2 * BLOCKS):
                all_s[2 * BLOCKS + r, pl.ds(a, TILES // 4, stride=4), :] = row[:, r * LANES : (r + 1) * LANES]
        for r in range(SHARE):
            out_s[pl.ds(r, TILES, stride=XROWS), :] = all_s[(rot_ref[0] & 1) * SHARE + r]
        for r in range(META - REST):
            out_s[pl.ds(REST + r, TILES, stride=XROWS), :] = all_s[2 * SHARE + r]
        lane = lax.broadcasted_iota(I32, (1, LANES), 1)
        fields = jnp.where(lane == 5 * SLOTS, count_ref[0, 0], 0)
        for i in range(SLOTS):
            y, x = row_ref[i], col_ref[i]
            items = (orient_ref[i], y >> 4, y & (BASE - 1), x >> 4, x & (BASE - 1))
            for k, item in enumerate(items):
                fields = jnp.where(lane == 5 * i + k, item, fields)
        fields = jnp.broadcast_to(fields.astype(F32), (TILES, LANES))
        for r in range(META, XROWS):
            out_s[pl.ds(r, TILES, stride=XROWS), :] = fields
        out_ref[...] = out_s[...].astype(BF).reshape(out_ref.shape)

    return pl.pallas_call(
        kernel,
        out_shape=(
            jax.ShapeDtypeStruct((TILES, XROWS, LANES), BF),
            jax.ShapeDtypeStruct((2, 2 * BLOCKS, LANES), F32),
        ),
        in_specs=[SM, SM] + [HB] * 8,
        out_specs=(VM, VM),
        scratch_shapes=[pltpu.VMEM(x.shape, x.dtype) for x in (index, weight, table, spectrum, grid)]
        + [pltpu.SMEM(x.shape, x.dtype) for x in (orient, row, col)]
        + [
            pltpu.SemaphoreType.DMA((8,)),
            pltpu.VMEM(table.shape, F32),
            pltpu.VMEM(index.shape, F32),
            pltpu.VMEM((2,) + index.shape, F32),
            pltpu.VMEM((2 * ROWS, HALF, LANES), F32),
            pltpu.VMEM((GRID * TILES * BINS // LANES, LANES), F32),
            pltpu.VMEM((4 * BLOCKS, TILES, LANES), F32),
            pltpu.VMEM((TILES * XROWS, LANES), F32),
        ],
        compiler_params=pltpu.CompilerParams(vmem_limit_bytes=VMEM_LIMIT),
        name="prepare",
    )(rot, count, *[stay(x) for x in (index, weight, table, spectrum, grid, orient, row, col)])


def arrange(spectrum, filt, tabx):
    def kernel(spec_hbm, filt_hbm, tabx_hbm, out_ref, wide_ref, spec_ref, filt_ref, tabx_ref, spec_s, sems):
        pairs = ((spec_hbm, spec_ref), (filt_hbm, filt_ref), (tabx_hbm, tabx_ref))
        copies = [pltpu.make_async_copy(a, b, sems.at[i]) for i, (a, b) in enumerate(pairs)]
        for copy in copies:
            copy.start()
        for copy in copies:
            copy.wait()
        for b in range(ROWS):
            cols = slice(b * LANES, (b + 1) * LANES)
            for c, value in enumerate((spec_ref[0, :, cols], spec_ref[1, :, cols], filt_ref[:, cols])):
                spec_s[c * ROWS + b] = value.astype(F32)
        for c in range(3):
            for j in range(ROWS):
                for b in range(ROWS):
                    out_ref[c * BLOCKS + j * ROWS + b] = every(spec_s.at[c * ROWS + b], j, ROWS)
        cosv, sinv = tabx_ref[:, :DFT], tabx_ref[:, DFT:]
        wide_ref[:DFT, :DFT] = cosv
        wide_ref[:DFT, DFT:] = sinv
        wide_ref[DFT:, :DFT] = -sinv
        wide_ref[DFT:, DFT:] = cosv

    return pl.pallas_call(
        kernel,
        out_shape=(
            jax.ShapeDtypeStruct((3 * BLOCKS, TILES, LANES), F32),
            jax.ShapeDtypeStruct((2 * DFT, 2 * DFT), BF),
        ),
        in_specs=[HB] * 3,
        out_specs=(VM, VM),
        scratch_shapes=[pltpu.VMEM(x.shape, BF) for x in (spectrum, filt, tabx)]
        + [pltpu.VMEM((3 * ROWS, HALF, LANES), F32), pltpu.SemaphoreType.DMA((3,))],
        compiler_params=pltpu.CompilerParams(vmem_limit_bytes=VMEM_LIMIT),
        name="arrange",
    )(*[stay(x) for x in (spectrum, filt, tabx)])


def correlate(place, own, other, blocks, wide, back):
    def kernel(
        at_ref, own_ref, other_ref, block_ref, wide_ref, back_hbm, keep_hbm, send_ref,
        sl_s, back_ref, keep_ref, sems,
    ):
        fetch = pltpu.make_async_copy(back_hbm.at[at_ref[0]], back_ref, sems.at[2])
        fetch.start()
        leave = [pltpu.make_async_copy(keep_ref.at[o], keep_hbm.at[o], sems.at[o]) for o in range(2)]
        sl_s[at_ref[1]] = own_ref[...].astype(F32).reshape(TILES * SROWS, LANES)
        sl_s[1 - at_ref[1]] = other_ref[...].astype(F32).reshape(TILES * SROWS, LANES)
        real = [[None] * (ROWS * ROWS) for _ in range(2)]
        imag = [[None] * (ROWS * ROWS) for _ in range(2)]
        for j in range(ROWS):
            for b in range(ROWS):
                mr, mi, c = [block_ref[k * BLOCKS + j * ROWS + b] for k in range(3)]
                for o in range(2):
                    row = o * BLOCKS + j * ROWS + b
                    cr = c * every(sl_s.at[0], row, SROWS)
                    ci = c * every(sl_s.at[1], row, SROWS)
                    real[o][j * ROWS + b] = (mr * cr + mi * ci).astype(BF)
                    imag[o][j * ROWS + b] = (mi * cr - mr * ci).astype(BF)
        cross = jnp.concatenate(
            [
                jnp.concatenate(real[o][j * ROWS : (j + 1) * ROWS] + imag[o][j * ROWS : (j + 1) * ROWS], axis=1)
                for o in range(2)
                for j in range(ROWS)
            ],
            axis=0,
        )
        halfimg = lax.dot_general(cross, wide_ref[...], NN, preferred_element_type=F32).astype(BF)
        fetch.wait()
        table = back_ref[...]
        low = at_ref[0] == 0
        for o in range(2):
            rows = halfimg[o * HALF : (o + 1) * HALF]
            both = jnp.concatenate([rows[:, :DFT], rows[:, DFT:]], axis=0)
            sums = lax.dot_general(table, both, NN, preferred_element_type=F32)
            left = jnp.concatenate([sums[:HALF, :HALF], sums[HALF:, :HALF]], axis=1)
            right = jnp.concatenate([sums[:HALF, HALF:], sums[HALF:, HALF:]], axis=1)
            keep_ref[o] = jnp.where(low, left, right).astype(BF)
            leave[o].start()
            send_ref[o] = jnp.where(low, right, left).astype(BF)
        for copy in leave:
            copy.wait()

    shape = jax.ShapeDtypeStruct((2, HALF, DFT), BF)
    return pl.pallas_call(
        kernel,
        out_shape=(shape, shape),
        in_specs=[SM] + [VM] * 4 + [HB],
        out_specs=(HB, VM),
        scratch_shapes=[
            pltpu.VMEM((2, TILES * SROWS, LANES), F32),
            pltpu.VMEM((DFT, DFT), BF),
            pltpu.VMEM((2, HALF, DFT), BF),
            pltpu.SemaphoreType.DMA((3,)),
        ],
        compiler_params=pltpu.CompilerParams(vmem_limit_bytes=VMEM_LIMIT),
        name="correlate",
    )(place, own, other, blocks, wide, stay(back))


def score(place, got, share, slices, tabx):
    def kernel(
        at_ref, got_ref, share_ref, slice_ref, tabx_ref,
        out_ref, place_hbm, got_s, share_s, place_s, place_ref, sem, out_s,
    ):
        got_s[...] = got_ref[...].astype(F32).reshape(got_s.shape)
        side = at_ref[2] & 1
        share_s[1 - side] = share_ref[...].astype(F32).reshape(TILES * SHARE, LANES)
        for r in range(SHARE):
            share_s[side, pl.ds(r, TILES, stride=SHARE), :] = every(got_s, r, XROWS)

        def sent(row):
            if row < 2 * SHARE:
                return every(share_s.at[row // SHARE], row % SHARE, SHARE)
            return every(got_s, REST + row - 2 * SHARE, XROWS)

        meta = every(got_s, META, XROWS)
        lane = lax.broadcasted_iota(I32, (TILES, DFT), 1).astype(F32)
        count = meta[:, 20:21]
        tri_r = lax.broadcasted_iota(I32, (TILES, TILES), 0)
        tri_c = lax.broadcasted_iota(I32, (TILES, TILES), 1)
        before = jnp.where(tri_c < tri_r, 1.0, 0.0).astype(BF)
        spread = jnp.broadcast_to(count, (TILES, LANES)).astype(BF)
        offset = lax.dot_general(before, spread, NN, preferred_element_type=F32)[:, 0:1]
        hot_x, hot_y, place = [], [], []
        for i in range(SLOTS):
            y0 = meta[:, 5 * i + 1 : 5 * i + 2] * BASE + meta[:, 5 * i + 2 : 5 * i + 3]
            x0 = meta[:, 5 * i + 3 : 5 * i + 4] * BASE + meta[:, 5 * i + 4 : 5 * i + 5]
            hot_x.append(jnp.where(lane == x0, 1.0, 0.0).astype(BF))
            hot_y.append(jnp.where(lane == y0, 1.0, 0.0).astype(BF))
            seat = jnp.where(count > float(i), offset + float(i), -1.0)
            hot = jnp.where(lane[:, :256] == seat, 1.0, 0.0)
            for h in range(2):
                place_s[h, pl.ds(i, TILES, stride=SLOTS), :] = hot[:, h * LANES : (h + 1) * LANES]
            place.append(hot.astype(BF))
        place_ref[...] = place_s[...].astype(BF)
        leave = pltpu.make_async_copy(place_ref, place_hbm, sem)
        leave.start()
        hot_x = jnp.concatenate(hot_x, axis=0)
        hot_y = jnp.concatenate(hot_y, axis=0)
        place = jnp.concatenate(place, axis=0)
        wave = lax.dot_general(hot_x, tabx_ref[...], NN, preferred_element_type=F32)
        cx, sx = wave[:, :DFT], wave[:, DFT:]
        line = lax.broadcasted_iota(I32, (16, DFT), 0) + at_ref[3]
        pick = jnp.where(lax.broadcasted_iota(I32, (16, DFT), 1) == line, 1.0, 0.0).astype(BF)
        taby = lax.dot_general(pick, tabx_ref[...], NN, preferred_element_type=F32).astype(BF)
        tilt_c = lax.dot_general(hot_y, taby[:, :DFT], NT, preferred_element_type=F32)
        tilt_s = lax.dot_general(hot_y, taby[:, DFT:], NT, preferred_element_type=F32)
        pieces = [[] for _ in range(SLOTS)]
        second = [jnp.broadcast_to(meta[:, 5 * i : 5 * i + 1], (TILES, LANES)) > 0.5 for i in range(SLOTS)]
        for j in range(ROWS):
            cosines = jnp.broadcast_to(tilt_c[:, j : j + 1], (SLOTS * TILES, LANES))
            sines = jnp.broadcast_to(tilt_s[:, j : j + 1], (SLOTS * TILES, LANES))
            for b in range(ROWS):
                r = j * ROWS + b
                cols = slice(b * LANES, (b + 1) * LANES)
                mr = sent(r)
                mi = sent(BLOCKS + r)
                plain = []
                for o in range(2):
                    sr = slice_ref[0, o * BLOCKS + r : o * BLOCKS + r + 1, :]
                    si = slice_ref[1, o * BLOCKS + r : o * BLOCKS + r + 1, :]
                    plain.append(((mr * sr + mi * si).astype(BF).astype(F32), (mi * sr - mr * si).astype(BF).astype(F32)))
                for i in range(SLOTS):
                    at = slice(i * TILES, (i + 1) * TILES)
                    pr = jnp.where(second[i], plain[1][0], plain[0][0])
                    pi = jnp.where(second[i], plain[1][1], plain[0][1])
                    cy, sy = cosines[at], sines[at]
                    wx, vx = cx[at, cols], sx[at, cols]
                    pieces[i].append(cy * (pr * wx - pi * vx) - sy * (pr * vx + pi * wx))
        shifted = jnp.concatenate([jnp.concatenate(p, axis=1) for p in pieces], axis=0)
        bin_of = lax.shift_right_logical(lax.broadcasted_iota(I32, (WIDE, DFT), 0), 2)
        group = jnp.where(bin_of == lax.broadcasted_iota(I32, (WIDE, DFT), 1), 1.0, 0.0).astype(BF)
        binned = lax.dot_general(shifted.astype(BF), group, NN, preferred_element_type=F32)
        binned = binned.astype(BF)[:, :BINS]
        grid = jnp.concatenate([sent(2 * BLOCKS + r).astype(BF) for r in range(2 * BLOCKS)], axis=1)
        values = jnp.concatenate([grid[:, q * BINS : (q + 1) * BINS] for q in range(GRID)], axis=0)
        scores = lax.dot_general(values, binned, NT, preferred_element_type=F32).astype(BF)
        packed = lax.dot_general(scores, place, NN, preferred_element_type=F32)
        lanes = lax.broadcasted_iota(I32, (TILES, LANES), 1)
        extra = jnp.zeros((TILES, LANES), F32)
        for q in range(GRID):
            block = packed[q * TILES : (q + 1) * TILES]
            out_s[:, q // SPAN, q % SPAN * LANES : (q % SPAN + 1) * LANES] = block[:, :LANES]
            extra = jnp.where(lanes == q, block[:, LANES : LANES + 1], extra)
        out_s[:, 1, (SPAN - 2) * LANES : (SPAN - 1) * LANES] = extra
        out_s[:, 1, (SPAN - 1) * LANES :] = jnp.zeros((TILES, LANES), F32)
        out_ref[...] = out_s[...].astype(BF)
        leave.wait()

    return pl.pallas_call(
        kernel,
        out_shape=(
            jax.ShapeDtypeStruct((TILES, 2, SPAN * LANES), BF),
            jax.ShapeDtypeStruct((2, SLOTS * TILES, LANES), BF),
        ),
        in_specs=[SM] + [VM] * 4,
        out_specs=(VM, HB),
        scratch_shapes=[pltpu.VMEM((TILES * XROWS, LANES), F32), pltpu.VMEM((2, TILES * SHARE, LANES), F32), pltpu.VMEM((2, SLOTS * TILES, LANES), F32), pltpu.VMEM((2, SLOTS * TILES, LANES), BF), pltpu.SemaphoreType.DMA, pltpu.VMEM((TILES, 2, SPAN * LANES), F32)],
        compiler_params=pltpu.CompilerParams(vmem_limit_bytes=VMEM_LIMIT),
        cost_estimate=pl.CostEstimate(flops=6_000_000_000, transcendentals=0, bytes_accessed=8_000_000),
        name="score",
    )(place, got, share, slices, tabx)


def expand(place, mine, other):
    def kernel(place_ref, mine_ref, other_ref, refined_ref, top_ref):
        both = mine_ref[...] + other_ref[...]
        place = jnp.concatenate([place_ref[0], place_ref[1]], axis=1)
        lane = lax.broadcasted_iota(I32, (GRID, LANES), 1)
        row = lax.broadcasted_iota(I32, (GRID, LANES), 0)
        sums = [both[r // SPAN : r // SPAN + 1, r % SPAN * LANES : (r % SPAN + 1) * LANES] for r in range(GRID + 1)]
        last = jnp.broadcast_to(sums[GRID], (GRID, LANES))
        last = jnp.sum(jnp.where(lane == row, last, 0.0), axis=1, keepdims=True)
        rest = jnp.concatenate([jnp.concatenate(sums[:GRID], axis=0), jnp.where(lane == 0, last, 0.0)], axis=1) * (1.0 / DFT)
        parts = []
        for _ in range(3):
            parts.append(rest.astype(BF).astype(F32))
            rest = rest - parts[-1]
        parts = jnp.concatenate(parts, axis=0).astype(BF)
        out = lax.dot_general(parts, place, NT, preferred_element_type=F32)
        refined = (out[:GRID] + out[GRID : 2 * GRID]) + out[2 * GRID :]
        refined_ref[...] = refined
        top = jnp.max(refined, axis=0, keepdims=True)
        top_ref[...] = jnp.broadcast_to(top[None], top_ref.shape)

    return pl.pallas_call(
        kernel,
        out_shape=(
            jax.ShapeDtypeStruct((GRID, SLOTS * TILES), F32),
            jax.ShapeDtypeStruct((TILES, 1, SLOTS * TILES), F32),
        ),
        in_specs=[VM] * 3,
        out_specs=(VM, VM),
        compiler_params=pltpu.CompilerParams(vmem_limit_bytes=VMEM_LIMIT),
        name="expand",
    )(place, mine, other)


def finish(parts):
    def kernel(*refs):
        ins, (top_ref, mean_ref) = refs[:4], refs[4:]
        for b in range(ROWS):
            cols = slice(b * LANES, (b + 1) * LANES)
            tops = [ref[0, :, cols].astype(F32) for ref in ins]
            sums = [ref[1, :, cols].astype(F32) for ref in ins]
            top_ref[pl.ds(b, HALF, stride=ROWS), :] = jnp.maximum(
                jnp.maximum(tops[0], tops[1]), jnp.maximum(tops[2], tops[3])
            )
            total = (sums[0] + sums[1]) + (sums[2] + sums[3])
            mean_ref[pl.ds(b, HALF, stride=ROWS), :] = total * (1.0 / ORIENTS)

    shape = jax.ShapeDtypeStruct((ROWS * HALF, LANES), F32)
    return pl.pallas_call(
        kernel,
        out_shape=(shape, shape),
        in_specs=[VM] * 4,
        out_specs=(VM, VM),
        cost_estimate=pl.CostEstimate(flops=1, transcendentals=0, bytes_accessed=1),
        compiler_params=pltpu.CompilerParams(vmem_limit_bytes=VMEM_LIMIT),
        name="finish",
    )(*parts)


def exchange(x, axis, bit):
    size = lax.axis_size(axis)
    return lax.ppermute(x, axis, [(k, k ^ bit) for k in range(size)])


def shards(
    interp_index,
    interp_weight,
    volume,
    spectrum,
    ctf_filter,
    peak_count,
    peak_orient,
    peak_row,
    peak_col,
    ctf_grid,
):
    back, tabx = [jnp.asarray(t) for t in tables()]
    nar = lax.axis_index("nar")
    tile = lax.axis_index("tile")

    grid = ctf_grid.reshape(GRID, TILES * BINS)
    spec = spectrum.reshape(2, HALF, DFT)
    filt = ctf_filter.reshape(HALF, DFT)
    rot = lax.axis_index("rot").reshape(1)
    blocks, slices = prepare(
        rot,
        interp_index.reshape(-1, LANES),
        interp_weight.transpose(0, 2, 3, 1, 4),
        volume.reshape(2, -1),
        spec,
        grid,
        peak_orient,
        peak_row,
        peak_col,
        peak_count,
    )
    slices, nar, tile = lax.optimization_barrier((slices, nar, tile))
    place_at = jnp.stack([nar, tile % 2, rot[0], (nar * TILES + tile) * ROWS])
    rows, wide = arrange(spec, filt, tabx)
    got = lax.all_to_all(blocks, "tile", 0, 0, tiled=True)
    got, rows, wide, place_at = lax.optimization_barrier((got, rows, wide, place_at))
    share, mine = exchange(got[:, :SHARE], "rot", 1), got[:, SHARE:]
    other = exchange(mine, "tile", 1)
    keep, send = correlate(place_at, mine, other, rows, wide, back)
    got, send = lax.optimization_barrier((got, send))
    extra_rows = exchange(send, "nar", 1)
    packed, place = score(place_at, got, share, slices, tabx)
    sums = lax.all_to_all(packed, "tile", 0, 0, tiled=True)

    corr = (keep.astype(F32) + extra_rows.astype(F32)) * (1.0 / DFT)
    stats = jnp.stack([jnp.maximum(corr[0], corr[1]), corr[0] + corr[1]]).astype(BF)
    others = [exchange(stats, "rot", bit) for bit in (1, 2, 3)]

    sums = jnp.sum(sums.astype(F32), axis=0)
    refined, tops = expand(place, sums, exchange(sums, "nar", 1))
    tops = lax.all_to_all(tops, "tile", 0, 0)
    peak, mean = finish([stats] + others)
    tops, peak, mean = lax.optimization_barrier((tops, peak, mean))
    best = jnp.max(tops, axis=0)
    return (
        peak.reshape(1, 1, -1),
        mean.reshape(1, 1, -1),
        refined.T.reshape(1, SLOTS * TILES, GRID),
        best,
    )


def solution(mesh):
    return jax.shard_map(
        shards,
        mesh=mesh,
        in_specs=(
            P(None, "rot", "nar", "tile", None),
            P(None, "rot", "nar", "tile", None),
            P(None, "nar", "tile", None),
            P(None, "tile", "nar", None, None),
            P("tile", "nar", None, None),
            P("rot", "tile"),
            P(("rot", "tile")),
            P(("rot", "tile")),
            P(("rot", "tile")),
            P("tile", "nar", None),
        ),
        out_specs=(
            P("tile", "nar", None),
            P("tile", "nar", None),
            P("rot", None, "tile"),
            P("rot", None),
        ),
        check_vma=False,
    )
```

```python
import jax
import jax.numpy as jnp
import numpy as np
from jax import lax
from jax.experimental import pallas as pl
from jax.experimental.pallas import tpu as pltpu
from jax.sharding import PartitionSpec as P

BF = jnp.bfloat16
F32 = jnp.float32
I32 = jnp.int32
LANES = 128
DFT = 384
HALF = 192
ROWS = 3
TILES = 64
SLOTS = 4
WIDE = ROWS * DFT
BINS = 288
GRID = 8
BASE = 16
BLOCKS = 9
XROWS = 40
SROWS = 24
SHARE = 16
SPAN = 5
ORIENTS = 8
REST = SHARE + 2 * BLOCKS
META = REST + 4 * BLOCKS - 2 * SHARE
VMEM_LIMIT = 16 * 1024 * 1024

VM = pl.BlockSpec(memory_space=pltpu.VMEM)
SM = pl.BlockSpec(memory_space=pltpu.SMEM)
HB = pl.BlockSpec(memory_space=pltpu.HBM)
NN = (((1,), (0,)), ((), ()))
NT = (((1,), (1,)), ((), ()))


def bf(x):
    return np.asarray(x, np.float32).astype(jnp.bfloat16)


def tables():
    steps = np.arange(DFT)
    phase = (steps[:, None] * steps[None, :] % DFT) * (2.0 * np.pi / DFT)
    cosv, sinv = np.cos(phase), np.sin(phase)
    rows = np.concatenate([steps[0::2], steps[1::2]])
    order = np.array([ROWS * t + j for j in range(ROWS) for t in range(TILES)])
    back = np.zeros((2, DFT, 2 * HALF), np.float32)
    for n in range(2):
        back[n, :, :HALF] = cosv[rows][:, n * HALF + order]
        back[n, :, HALF:] = -sinv[rows][:, n * HALF + order]
    return bf(back), bf(np.concatenate([cosv, sinv], 1))


def stay(x):
    return pltpu.with_memory_space_constraint(x, pltpu.HBM)


def every(ref, row, step):
    return ref[pl.ds(row, TILES, stride=step), :]


def prepare(rot, index, weight, table, spectrum, grid, orient, row, col, count):
    def kernel(
        rot_ref, count_ref, *refs,
    ):
        sources, (out_hbm, own_ref), scratch = refs[:8], refs[8:10], refs[10:]
        targets, (sems, table_s, weight_s, value_s, spec_s, grid_s, all_s, out_s, out_ref) = scratch[:8], scratch[8:]
        copies = [pltpu.make_async_copy(a, b, sems.at[i]) for i, (a, b) in enumerate(zip(sources, targets))]
        for copy in copies:
            copy.start()
        index_ref, weight_ref, table_ref, spec_ref, grid_ref, orient_ref, row_ref, col_ref = targets
        for copy in copies[:3]:
            copy.wait()
        table_s[...] = table_ref[...].astype(F32)
        for k in range(8):
            for j in range(ROWS):
                w = weight_ref[k, 0, j].astype(F32)
                for b in range(ROWS):
                    at = pl.ds(k * 2 * BLOCKS + j * ROWS + b, 2, stride=BLOCKS)
                    weight_s[at, :] = w[:, b * LANES : (b + 1) * LANES]

        def step(v, carry):
            rows = pl.ds(pl.multiple_of(v * 8, 8), 8)
            entry = index_ref[rows, :]
            low = entry & (LANES - 1)
            high = lax.shift_right_logical(entry, 7)
            bits = [(lax.shift_right_logical(high, b) & 1) == 1 for b in range(5)]

            def pick(c, level, first):
                if level < 0:
                    line = table_s[c : c + 1, first * LANES : (first + 1) * LANES]
                    return jnp.take_along_axis(jnp.broadcast_to(line, (8, LANES)), low, axis=1)
                return jnp.where(
                    bits[level],
                    pick(c, level - 1, first + (1 << level)),
                    pick(c, level - 1, first),
                )

            for c in range(2):
                value_s[c, rows, :] = pick(c, 4, 0) * weight_s[rows, :]
            return carry

        lax.fori_loop(0, 2 * BLOCKS, step, 0, unroll=3)
        for c in range(2):
            total = value_s[c, 0 : 2 * BLOCKS, :]
            for k in range(1, 8):
                total = total + value_s[c, k * 2 * BLOCKS : (k + 1) * 2 * BLOCKS, :]
            own_ref[c] = total.astype(BF).astype(F32)

        for copy in copies[3:]:
            copy.wait()
        odd = (lax.broadcasted_iota(I32, (TILES, LANES), 0) & 1) == 1
        for r in range(2 * BLOCKS):
            row = jnp.where(odd, own_ref[1, r : r + 1, :], own_ref[0, r : r + 1, :])
            out_s[pl.ds(SHARE + r, TILES, stride=XROWS), :] = row
        for c in range(2):
            for b in range(ROWS):
                spec_s[c * ROWS + b] = spec_ref[c, :, b * LANES : (b + 1) * LANES].astype(F32)
        for c in range(2):
            for j in range(ROWS):
                for b in range(ROWS):
                    all_s[c * BLOCKS + j * ROWS + b] = spec_s[c * ROWS + b, pl.ds(j, TILES, stride=ROWS), :]
        for k in range(TILES * BINS // LANES):
            grid_s[k * GRID : (k + 1) * GRID, :] = grid_ref[:, k * LANES : (k + 1) * LANES].astype(F32)
        for a in range(4):
            first, shift = divmod(a * BINS, LANES)
            pieces = []
            for q in range(GRID):
                blocks = [
                    grid_s[pl.ds((first + k) * GRID + q, TILES // 4, stride=BLOCKS * GRID), :] for k in range(3)
                ]
                pieces.append(jnp.concatenate(blocks, axis=1)[:, shift : shift + BINS])
            row = jnp.concatenate(pieces, axis=1)
            for r in range(2 * BLOCKS):
                all_s[2 * BLOCKS + r, pl.ds(a, TILES // 4, stride=4), :] = row[:, r * LANES : (r + 1) * LANES]
        for r in range(SHARE):
            out_s[pl.ds(r, TILES, stride=XROWS), :] = all_s[(rot_ref[0] & 1) * SHARE + r]
        for r in range(META - REST):
            out_s[pl.ds(REST + r, TILES, stride=XROWS), :] = all_s[2 * SHARE + r]
        lane = lax.broadcasted_iota(I32, (1, LANES), 1)
        fields = jnp.where(lane == 5 * SLOTS, count_ref[0, 0], 0)
        for i in range(SLOTS):
            y, x = row_ref[i], col_ref[i]
            items = (orient_ref[i], y >> 4, y & (BASE - 1), x >> 4, x & (BASE - 1))
            for k, item in enumerate(items):
                fields = jnp.where(lane == 5 * i + k, item, fields)
        fields = jnp.broadcast_to(fields.astype(F32), (TILES, LANES))
        for r in range(META, XROWS):
            out_s[pl.ds(r, TILES, stride=XROWS), :] = fields
        piece = TILES // 4
        leave = []
        for k in range(4):
            rows = out_s[k * piece * XROWS : (k + 1) * piece * XROWS, :]
            out_ref[k * piece : (k + 1) * piece] = rows.astype(BF).reshape(piece, XROWS, LANES)
            at = pl.ds(k * piece, piece)
            leave.append(pltpu.make_async_copy(out_ref.at[at], out_hbm.at[at], sems.at[8 + k]))
            leave[-1].start()
        for copy in leave:
            copy.wait()

    return pl.pallas_call(
        kernel,
        out_shape=(
            jax.ShapeDtypeStruct((TILES, XROWS, LANES), BF),
            jax.ShapeDtypeStruct((2, 2 * BLOCKS, LANES), F32),
        ),
        in_specs=[SM, SM] + [HB] * 8,
        out_specs=(HB, VM),
        scratch_shapes=[pltpu.VMEM(x.shape, x.dtype) for x in (index, weight, table, spectrum, grid)]
        + [pltpu.SMEM(x.shape, x.dtype) for x in (orient, row, col)]
        + [
            pltpu.SemaphoreType.DMA((12,)),
            pltpu.VMEM(table.shape, F32),
            pltpu.VMEM(index.shape, F32),
            pltpu.VMEM((2,) + index.shape, F32),
            pltpu.VMEM((2 * ROWS, HALF, LANES), F32),
            pltpu.VMEM((GRID * TILES * BINS // LANES, LANES), F32),
            pltpu.VMEM((4 * BLOCKS, TILES, LANES), F32),
            pltpu.VMEM((TILES * XROWS, LANES), F32),
            pltpu.VMEM((TILES, XROWS, LANES), BF),
        ],
        compiler_params=pltpu.CompilerParams(vmem_limit_bytes=VMEM_LIMIT),
        name="prepare",
    )(rot, count, *[stay(x) for x in (index, weight, table, spectrum, grid, orient, row, col)])


def arrange(spectrum, filt, tabx):
    def kernel(spec_hbm, filt_hbm, tabx_hbm, out_ref, wide_ref, spec_ref, filt_ref, tabx_ref, spec_s, sems):
        pairs = ((spec_hbm, spec_ref), (filt_hbm, filt_ref), (tabx_hbm, tabx_ref))
        copies = [pltpu.make_async_copy(a, b, sems.at[i]) for i, (a, b) in enumerate(pairs)]
        for copy in copies:
            copy.start()
        for copy in copies:
            copy.wait()
        for b in range(ROWS):
            cols = slice(b * LANES, (b + 1) * LANES)
            for c, value in enumerate((spec_ref[0, :, cols], spec_ref[1, :, cols], filt_ref[:, cols])):
                spec_s[c * ROWS + b] = value.astype(F32)
        for c in range(3):
            for j in range(ROWS):
                for b in range(ROWS):
                    out_ref[c * BLOCKS + j * ROWS + b] = every(spec_s.at[c * ROWS + b], j, ROWS)
        cosv, sinv = tabx_ref[:, :DFT], tabx_ref[:, DFT:]
        wide_ref[:DFT, :DFT] = cosv
        wide_ref[:DFT, DFT:] = sinv
        wide_ref[DFT:, :DFT] = -sinv
        wide_ref[DFT:, DFT:] = cosv

    return pl.pallas_call(
        kernel,
        out_shape=(
            jax.ShapeDtypeStruct((3 * BLOCKS, TILES, LANES), F32),
            jax.ShapeDtypeStruct((2 * DFT, 2 * DFT), BF),
        ),
        in_specs=[HB] * 3,
        out_specs=(VM, VM),
        scratch_shapes=[pltpu.VMEM(x.shape, BF) for x in (spectrum, filt, tabx)]
        + [pltpu.VMEM((3 * ROWS, HALF, LANES), F32), pltpu.SemaphoreType.DMA((3,))],
        compiler_params=pltpu.CompilerParams(vmem_limit_bytes=VMEM_LIMIT),
        name="arrange",
    )(*[stay(x) for x in (spectrum, filt, tabx)])


def correlate(place, own, other, blocks, wide, back):
    def kernel(
        at_ref, own_ref, other_ref, block_ref, wide_ref, back_hbm, keep_hbm, send_ref,
        sl_s, back_ref, keep_ref, sems,
    ):
        fetch = pltpu.make_async_copy(back_hbm.at[at_ref[0]], back_ref, sems.at[2])
        fetch.start()
        leave = [pltpu.make_async_copy(keep_ref.at[o], keep_hbm.at[o], sems.at[o]) for o in range(2)]
        sl_s[at_ref[1]] = own_ref[...].astype(F32).reshape(TILES * SROWS, LANES)
        sl_s[1 - at_ref[1]] = other_ref[...].astype(F32).reshape(TILES * SROWS, LANES)
        real = [[None] * (ROWS * ROWS) for _ in range(2)]
        imag = [[None] * (ROWS * ROWS) for _ in range(2)]
        for j in range(ROWS):
            for b in range(ROWS):
                mr, mi, c = [block_ref[k * BLOCKS + j * ROWS + b] for k in range(3)]
                for o in range(2):
                    row = o * BLOCKS + j * ROWS + b
                    cr = c * every(sl_s.at[0], row, SROWS)
                    ci = c * every(sl_s.at[1], row, SROWS)
                    real[o][j * ROWS + b] = (mr * cr + mi * ci).astype(BF)
                    imag[o][j * ROWS + b] = (mi * cr - mr * ci).astype(BF)
        cross = jnp.concatenate(
            [
                jnp.concatenate(real[o][j * ROWS : (j + 1) * ROWS] + imag[o][j * ROWS : (j + 1) * ROWS], axis=1)
                for o in range(2)
                for j in range(ROWS)
            ],
            axis=0,
        )
        halfimg = lax.dot_general(cross, wide_ref[...], NN, preferred_element_type=F32).astype(BF)
        fetch.wait()
        table = back_ref[...]
        low = at_ref[0] == 0
        for o in range(2):
            rows = halfimg[o * HALF : (o + 1) * HALF]
            both = jnp.concatenate([rows[:, :DFT], rows[:, DFT:]], axis=0)
            sums = lax.dot_general(table, both, NN, preferred_element_type=F32)
            left = jnp.concatenate([sums[:HALF, :HALF], sums[HALF:, :HALF]], axis=1)
            right = jnp.concatenate([sums[:HALF, HALF:], sums[HALF:, HALF:]], axis=1)
            keep_ref[o] = jnp.where(low, left, right).astype(BF)
            leave[o].start()
            send_ref[o] = jnp.where(low, right, left).astype(BF)
        for copy in leave:
            copy.wait()

    shape = jax.ShapeDtypeStruct((2, HALF, DFT), BF)
    return pl.pallas_call(
        kernel,
        out_shape=(shape, shape),
        in_specs=[SM] + [VM] * 4 + [HB],
        out_specs=(HB, VM),
        scratch_shapes=[
            pltpu.VMEM((2, TILES * SROWS, LANES), F32),
            pltpu.VMEM((DFT, DFT), BF),
            pltpu.VMEM((2, HALF, DFT), BF),
            pltpu.SemaphoreType.DMA((3,)),
        ],
        compiler_params=pltpu.CompilerParams(vmem_limit_bytes=VMEM_LIMIT),
        name="correlate",
    )(place, own, other, blocks, wide, stay(back))


def score(place, got, share, slices, tabx):
    def kernel(
        at_ref, got_ref, share_ref, slice_ref, tabx_ref,
        out_ref, place_hbm, got_s, share_s, place_s, place_ref, sem, out_s,
    ):
        got_s[...] = got_ref[...].astype(F32).reshape(got_s.shape)
        side = at_ref[2] & 1
        share_s[1 - side] = share_ref[...].astype(F32).reshape(TILES * SHARE, LANES)
        for r in range(SHARE):
            share_s[side, pl.ds(r, TILES, stride=SHARE), :] = every(got_s, r, XROWS)

        def sent(row):
            if row < 2 * SHARE:
                return every(share_s.at[row // SHARE], row % SHARE, SHARE)
            return every(got_s, REST + row - 2 * SHARE, XROWS)

        meta = every(got_s, META, XROWS)
        lane = lax.broadcasted_iota(I32, (TILES, DFT), 1).astype(F32)
        count = meta[:, 20:21]
        tri_r = lax.broadcasted_iota(I32, (TILES, TILES), 0)
        tri_c = lax.broadcasted_iota(I32, (TILES, TILES), 1)
        before = jnp.where(tri_c < tri_r, 1.0, 0.0).astype(BF)
        spread = jnp.broadcast_to(count, (TILES, LANES)).astype(BF)
        offset = lax.dot_general(before, spread, NN, preferred_element_type=F32)[:, 0:1]
        hot_x, hot_y, place = [], [], []
        for i in range(SLOTS):
            y0 = meta[:, 5 * i + 1 : 5 * i + 2] * BASE + meta[:, 5 * i + 2 : 5 * i + 3]
            x0 = meta[:, 5 * i + 3 : 5 * i + 4] * BASE + meta[:, 5 * i + 4 : 5 * i + 5]
            hot_x.append(jnp.where(lane == x0, 1.0, 0.0).astype(BF))
            hot_y.append(jnp.where(lane == y0, 1.0, 0.0).astype(BF))
            seat = jnp.where(count > float(i), offset + float(i), -1.0)
            hot = jnp.where(lane[:, :256] == seat, 1.0, 0.0)
            for h in range(2):
                place_s[h, pl.ds(i, TILES, stride=SLOTS), :] = hot[:, h * LANES : (h + 1) * LANES]
            place.append(hot.astype(BF))
        place_ref[...] = place_s[...].astype(BF)
        leave = pltpu.make_async_copy(place_ref, place_hbm, sem)
        leave.start()
        hot_x = jnp.concatenate(hot_x, axis=0)
        hot_y = jnp.concatenate(hot_y, axis=0)
        place = jnp.concatenate(place, axis=0)
        wave = lax.dot_general(hot_x, tabx_ref[...], NN, preferred_element_type=F32)
        cx, sx = wave[:, :DFT], wave[:, DFT:]
        line = lax.broadcasted_iota(I32, (16, DFT), 0) + at_ref[3]
        pick = jnp.where(lax.broadcasted_iota(I32, (16, DFT), 1) == line, 1.0, 0.0).astype(BF)
        taby = lax.dot_general(pick, tabx_ref[...], NN, preferred_element_type=F32).astype(BF)
        tilt_c = lax.dot_general(hot_y, taby[:, :DFT], NT, preferred_element_type=F32)
        tilt_s = lax.dot_general(hot_y, taby[:, DFT:], NT, preferred_element_type=F32)
        pieces = [[] for _ in range(SLOTS)]
        second = [jnp.broadcast_to(meta[:, 5 * i : 5 * i + 1], (TILES, LANES)) > 0.5 for i in range(SLOTS)]
        for j in range(ROWS):
            cosines = jnp.broadcast_to(tilt_c[:, j : j + 1], (SLOTS * TILES, LANES))
            sines = jnp.broadcast_to(tilt_s[:, j : j + 1], (SLOTS * TILES, LANES))
            for b in range(ROWS):
                r = j * ROWS + b
                cols = slice(b * LANES, (b + 1) * LANES)
                mr = sent(r)
                mi = sent(BLOCKS + r)
                plain = []
                for o in range(2):
                    sr = slice_ref[0, o * BLOCKS + r : o * BLOCKS + r + 1, :]
                    si = slice_ref[1, o * BLOCKS + r : o * BLOCKS + r + 1, :]
                    plain.append(((mr * sr + mi * si).astype(BF).astype(F32), (mi * sr - mr * si).astype(BF).astype(F32)))
                for i in range(SLOTS):
                    at = slice(i * TILES, (i + 1) * TILES)
                    pr = jnp.where(second[i], plain[1][0], plain[0][0])
                    pi = jnp.where(second[i], plain[1][1], plain[0][1])
                    cy, sy = cosines[at], sines[at]
                    wx, vx = cx[at, cols], sx[at, cols]
                    pieces[i].append(cy * (pr * wx - pi * vx) - sy * (pr * vx + pi * wx))
        shifted = jnp.concatenate([jnp.concatenate(p, axis=1) for p in pieces], axis=0)
        bin_of = lax.shift_right_logical(lax.broadcasted_iota(I32, (WIDE, DFT), 0), 2)
        group = jnp.where(bin_of == lax.broadcasted_iota(I32, (WIDE, DFT), 1), 1.0, 0.0).astype(BF)
        binned = lax.dot_general(shifted.astype(BF), group, NN, preferred_element_type=F32)
        binned = binned.astype(BF)[:, :BINS]
        grid = jnp.concatenate([sent(2 * BLOCKS + r).astype(BF) for r in range(2 * BLOCKS)], axis=1)
        values = jnp.concatenate([grid[:, q * BINS : (q + 1) * BINS] for q in range(GRID)], axis=0)
        scores = lax.dot_general(values, binned, NT, preferred_element_type=F32).astype(BF)
        packed = lax.dot_general(scores, place, NN, preferred_element_type=F32)
        lanes = lax.broadcasted_iota(I32, (TILES, LANES), 1)
        extra = jnp.zeros((TILES, LANES), F32)
        for q in range(GRID):
            block = packed[q * TILES : (q + 1) * TILES]
            out_s[:, q // SPAN, q % SPAN * LANES : (q % SPAN + 1) * LANES] = block[:, :LANES]
            extra = jnp.where(lanes == q, block[:, LANES : LANES + 1], extra)
        out_s[:, 1, (SPAN - 2) * LANES : (SPAN - 1) * LANES] = extra
        out_s[:, 1, (SPAN - 1) * LANES :] = jnp.zeros((TILES, LANES), F32)
        out_ref[...] = out_s[...].astype(BF)
        leave.wait()

    return pl.pallas_call(
        kernel,
        out_shape=(
            jax.ShapeDtypeStruct((TILES, 2, SPAN * LANES), BF),
            jax.ShapeDtypeStruct((2, SLOTS * TILES, LANES), BF),
        ),
        in_specs=[SM] + [VM] * 4,
        out_specs=(VM, HB),
        scratch_shapes=[pltpu.VMEM((TILES * XROWS, LANES), F32), pltpu.VMEM((2, TILES * SHARE, LANES), F32), pltpu.VMEM((2, SLOTS * TILES, LANES), F32), pltpu.VMEM((2, SLOTS * TILES, LANES), BF), pltpu.SemaphoreType.DMA, pltpu.VMEM((TILES, 2, SPAN * LANES), F32)],
        compiler_params=pltpu.CompilerParams(vmem_limit_bytes=VMEM_LIMIT),
        cost_estimate=pl.CostEstimate(flops=6_000_000_000, transcendentals=0, bytes_accessed=8_000_000),
        name="score",
    )(place, got, share, slices, tabx)


def expand(place, mine, other):
    def kernel(place_ref, mine_ref, other_ref, refined_ref, top_ref):
        both = mine_ref[...] + other_ref[...]
        place = jnp.concatenate([place_ref[0], place_ref[1]], axis=1)
        lane = lax.broadcasted_iota(I32, (GRID, LANES), 1)
        row = lax.broadcasted_iota(I32, (GRID, LANES), 0)
        sums = [both[r // SPAN : r // SPAN + 1, r % SPAN * LANES : (r % SPAN + 1) * LANES] for r in range(GRID + 1)]
        last = jnp.broadcast_to(sums[GRID], (GRID, LANES))
        last = jnp.sum(jnp.where(lane == row, last, 0.0), axis=1, keepdims=True)
        rest = jnp.concatenate([jnp.concatenate(sums[:GRID], axis=0), jnp.where(lane == 0, last, 0.0)], axis=1) * (1.0 / DFT)
        parts = []
        for _ in range(3):
            parts.append(rest.astype(BF).astype(F32))
            rest = rest - parts[-1]
        parts = jnp.concatenate(parts, axis=0).astype(BF)
        out = lax.dot_general(parts, place, NT, preferred_element_type=F32)
        refined = (out[:GRID] + out[GRID : 2 * GRID]) + out[2 * GRID :]
        refined_ref[...] = refined
        top = jnp.max(refined, axis=0, keepdims=True)
        top_ref[...] = jnp.broadcast_to(top[None], top_ref.shape)

    return pl.pallas_call(
        kernel,
        out_shape=(
            jax.ShapeDtypeStruct((GRID, SLOTS * TILES), F32),
            jax.ShapeDtypeStruct((TILES, 1, SLOTS * TILES), F32),
        ),
        in_specs=[VM] * 3,
        out_specs=(VM, VM),
        compiler_params=pltpu.CompilerParams(vmem_limit_bytes=VMEM_LIMIT),
        name="expand",
    )(place, mine, other)


def finish(parts):
    def kernel(*refs):
        ins, (top_ref, mean_ref) = refs[:4], refs[4:]
        for b in range(ROWS):
            cols = slice(b * LANES, (b + 1) * LANES)
            tops = [ref[0, :, cols].astype(F32) for ref in ins]
            sums = [ref[1, :, cols].astype(F32) for ref in ins]
            top_ref[pl.ds(b, HALF, stride=ROWS), :] = jnp.maximum(
                jnp.maximum(tops[0], tops[1]), jnp.maximum(tops[2], tops[3])
            )
            total = (sums[0] + sums[1]) + (sums[2] + sums[3])
            mean_ref[pl.ds(b, HALF, stride=ROWS), :] = total * (1.0 / ORIENTS)

    shape = jax.ShapeDtypeStruct((ROWS * HALF, LANES), F32)
    return pl.pallas_call(
        kernel,
        out_shape=(shape, shape),
        in_specs=[VM] * 4,
        out_specs=(VM, VM),
        cost_estimate=pl.CostEstimate(flops=1, transcendentals=0, bytes_accessed=1),
        compiler_params=pltpu.CompilerParams(vmem_limit_bytes=VMEM_LIMIT),
        name="finish",
    )(*parts)


def exchange(x, axis, bit):
    size = lax.axis_size(axis)
    return lax.ppermute(x, axis, [(k, k ^ bit) for k in range(size)])


def shards(
    interp_index,
    interp_weight,
    volume,
    spectrum,
    ctf_filter,
    peak_count,
    peak_orient,
    peak_row,
    peak_col,
    ctf_grid,
):
    back, tabx = [jnp.asarray(t) for t in tables()]
    nar = lax.axis_index("nar")
    tile = lax.axis_index("tile")

    grid = ctf_grid.reshape(GRID, TILES * BINS)
    spec = spectrum.reshape(2, HALF, DFT)
    filt = ctf_filter.reshape(HALF, DFT)
    rot = lax.axis_index("rot").reshape(1)
    blocks, slices = prepare(
        rot,
        interp_index.reshape(-1, LANES),
        interp_weight.transpose(0, 2, 3, 1, 4),
        volume.reshape(2, -1),
        spec,
        grid,
        peak_orient,
        peak_row,
        peak_col,
        peak_count,
    )
    slices, nar, tile = lax.optimization_barrier((slices, nar, tile))
    place_at = jnp.stack([nar, tile % 2, rot[0], (nar * TILES + tile) * ROWS])
    rows, wide = arrange(spec, filt, tabx)
    got = lax.all_to_all(blocks, "tile", 0, 0, tiled=True)
    got, rows, wide, place_at = lax.optimization_barrier((got, rows, wide, place_at))
    share, mine = exchange(got[:, :SHARE], "rot", 1), got[:, SHARE:]
    other = exchange(mine, "tile", 1)
    keep, send = correlate(place_at, mine, other, rows, wide, back)
    got, send = lax.optimization_barrier((got, send))
    extra_rows = exchange(send, "nar", 1)
    packed, place = score(place_at, got, share, slices, tabx)
    sums = lax.all_to_all(packed, "tile", 0, 0, tiled=True)

    corr = (keep.astype(F32) + extra_rows.astype(F32)) * (1.0 / DFT)
    stats = jnp.stack([jnp.maximum(corr[0], corr[1]), corr[0] + corr[1]]).astype(BF)
    others = [exchange(stats, "rot", bit) for bit in (1, 2, 3)]

    sums = jnp.sum(sums.astype(F32), axis=0)
    refined, tops = expand(place, sums, exchange(sums, "nar", 1))
    tops = lax.all_to_all(tops, "tile", 0, 0)
    peak, mean = finish([stats] + others)
    tops, peak, mean = lax.optimization_barrier((tops, peak, mean))
    best = jnp.max(tops, axis=0)
    return (
        peak.reshape(1, 1, -1),
        mean.reshape(1, 1, -1),
        refined.T.reshape(1, SLOTS * TILES, GRID),
        best,
    )


def solution(mesh):
    return jax.shard_map(
        shards,
        mesh=mesh,
        in_specs=(
            P(None, "rot", "nar", "tile", None),
            P(None, "rot", "nar", "tile", None),
            P(None, "nar", "tile", None),
            P(None, "tile", "nar", None, None),
            P("tile", "nar", None, None),
            P("rot", "tile"),
            P(("rot", "tile")),
            P(("rot", "tile")),
            P(("rot", "tile")),
            P("tile", "nar", None),
        ),
        out_specs=(
            P("tile", "nar", None),
            P("tile", "nar", None),
            P("rot", None, "tile"),
            P("rot", None),
        ),
        check_vma=False,
    )
```

```python
import jax
import jax.numpy as jnp
import numpy as np
from jax import lax
from jax.experimental import pallas as pl
from jax.experimental.pallas import tpu as pltpu
from jax.sharding import PartitionSpec as P

BF = jnp.bfloat16
F32 = jnp.float32
I32 = jnp.int32
LANES = 128
DFT = 384
HALF = 192
ROWS = 3
TILES = 64
SLOTS = 4
WIDE = ROWS * DFT
BINS = 288
GRID = 8
BASE = 16
BLOCKS = 9
XROWS = 40
SROWS = 24
SHARE = 16
SPAN = 5
ORIENTS = 8
REST = SHARE + 2 * BLOCKS
META = REST + 4 * BLOCKS - 2 * SHARE
VMEM_LIMIT = 16 * 1024 * 1024

VM = pl.BlockSpec(memory_space=pltpu.VMEM)
SM = pl.BlockSpec(memory_space=pltpu.SMEM)
HB = pl.BlockSpec(memory_space=pltpu.HBM)
NN = (((1,), (0,)), ((), ()))
NT = (((1,), (1,)), ((), ()))


def bf(x):
    return np.asarray(x, np.float32).astype(jnp.bfloat16)


def tables():
    steps = np.arange(DFT)
    phase = (steps[:, None] * steps[None, :] % DFT) * (2.0 * np.pi / DFT)
    cosv, sinv = np.cos(phase), np.sin(phase)
    rows = np.concatenate([steps[0::2], steps[1::2]])
    order = np.array([ROWS * t + j for j in range(ROWS) for t in range(TILES)])
    back = np.zeros((2, DFT, 2 * HALF), np.float32)
    for n in range(2):
        back[n, :, :HALF] = cosv[rows][:, n * HALF + order]
        back[n, :, HALF:] = -sinv[rows][:, n * HALF + order]
    return bf(back), bf(np.concatenate([cosv, sinv], 1))


def stay(x):
    return pltpu.with_memory_space_constraint(x, pltpu.HBM)


def every(ref, row, step):
    return ref[pl.ds(row, TILES, stride=step), :]


def prepare(rot, index, weight, table, spectrum, grid, orient, row, col, count):
    def kernel(
        rot_ref, count_ref, *refs,
    ):
        sources, (out_hbm, own_ref), scratch = refs[:8], refs[8:10], refs[10:]
        targets, (sems, table_s, weight_s, value_s, spec_s, grid_s, all_s, out_s, out_ref) = scratch[:8], scratch[8:]
        copies = [pltpu.make_async_copy(a, b, sems.at[i]) for i, (a, b) in enumerate(zip(sources, targets))]
        for copy in copies:
            copy.start()
        index_ref, weight_ref, table_ref, spec_ref, grid_ref, orient_ref, row_ref, col_ref = targets
        for copy in copies[:3]:
            copy.wait()
        table_s[...] = table_ref[...].astype(F32)
        for k in range(8):
            for j in range(ROWS):
                w = weight_ref[k, 0, j].astype(F32)
                for b in range(ROWS):
                    at = pl.ds(k * 2 * BLOCKS + j * ROWS + b, 2, stride=BLOCKS)
                    weight_s[at, :] = w[:, b * LANES : (b + 1) * LANES]

        def step(v, carry):
            rows = pl.ds(pl.multiple_of(v * 8, 8), 8)
            entry = index_ref[rows, :]
            low = entry & (LANES - 1)
            high = lax.shift_right_logical(entry, 7)
            bits = [(lax.shift_right_logical(high, b) & 1) == 1 for b in range(5)]

            def pick(c, level, first):
                if level < 0:
                    line = table_s[c : c + 1, first * LANES : (first + 1) * LANES]
                    return jnp.take_along_axis(jnp.broadcast_to(line, (8, LANES)), low, axis=1)
                return jnp.where(
                    bits[level],
                    pick(c, level - 1, first + (1 << level)),
                    pick(c, level - 1, first),
                )

            for c in range(2):
                value_s[c, rows, :] = pick(c, 4, 0) * weight_s[rows, :]
            return carry

        lax.fori_loop(0, 2 * BLOCKS, step, 0, unroll=6)
        for c in range(2):
            total = value_s[c, 0 : 2 * BLOCKS, :]
            for k in range(1, 8):
                total = total + value_s[c, k * 2 * BLOCKS : (k + 1) * 2 * BLOCKS, :]
            own_ref[c] = total.astype(BF).astype(F32)

        for copy in copies[3:]:
            copy.wait()
        odd = (lax.broadcasted_iota(I32, (TILES, LANES), 0) & 1) == 1
        for r in range(2 * BLOCKS):
            row = jnp.where(odd, own_ref[1, r : r + 1, :], own_ref[0, r : r + 1, :])
            out_s[pl.ds(SHARE + r, TILES, stride=XROWS), :] = row
        for c in range(2):
            for b in range(ROWS):
                spec_s[c * ROWS + b] = spec_ref[c, :, b * LANES : (b + 1) * LANES].astype(F32)
        for c in range(2):
            for j in range(ROWS):
                for b in range(ROWS):
                    all_s[c * BLOCKS + j * ROWS + b] = spec_s[c * ROWS + b, pl.ds(j, TILES, stride=ROWS), :]
        for k in range(TILES * BINS // LANES):
            grid_s[k * GRID : (k + 1) * GRID, :] = grid_ref[:, k * LANES : (k + 1) * LANES].astype(F32)
        for a in range(4):
            first, shift = divmod(a * BINS, LANES)
            pieces = []
            for q in range(GRID):
                blocks = [
                    grid_s[pl.ds((first + k) * GRID + q, TILES // 4, stride=BLOCKS * GRID), :] for k in range(3)
                ]
                pieces.append(jnp.concatenate(blocks, axis=1)[:, shift : shift + BINS])
            row = jnp.concatenate(pieces, axis=1)
            for r in range(2 * BLOCKS):
                all_s[2 * BLOCKS + r, pl.ds(a, TILES // 4, stride=4), :] = row[:, r * LANES : (r + 1) * LANES]
        for r in range(SHARE):
            out_s[pl.ds(r, TILES, stride=XROWS), :] = all_s[(rot_ref[0] & 1) * SHARE + r]
        for r in range(META - REST):
            out_s[pl.ds(REST + r, TILES, stride=XROWS), :] = all_s[2 * SHARE + r]
        lane = lax.broadcasted_iota(I32, (1, LANES), 1)
        fields = jnp.where(lane == 5 * SLOTS, count_ref[0, 0], 0)
        for i in range(SLOTS):
            y, x = row_ref[i], col_ref[i]
            items = (orient_ref[i], y >> 4, y & (BASE - 1), x >> 4, x & (BASE - 1))
            for k, item in enumerate(items):
                fields = jnp.where(lane == 5 * i + k, item, fields)
        fields = jnp.broadcast_to(fields.astype(F32), (TILES, LANES))
        for r in range(META, XROWS):
            out_s[pl.ds(r, TILES, stride=XROWS), :] = fields
        piece = TILES // 4
        leave = []
        for k in range(4):
            rows = out_s[k * piece * XROWS : (k + 1) * piece * XROWS, :]
            out_ref[k * piece : (k + 1) * piece] = rows.astype(BF).reshape(piece, XROWS, LANES)
            at = pl.ds(k * piece, piece)
            leave.append(pltpu.make_async_copy(out_ref.at[at], out_hbm.at[at], sems.at[8 + k]))
            leave[-1].start()
        for copy in leave:
            copy.wait()

    return pl.pallas_call(
        kernel,
        out_shape=(
            jax.ShapeDtypeStruct((TILES, XROWS, LANES), BF),
            jax.ShapeDtypeStruct((2, 2 * BLOCKS, LANES), F32),
        ),
        in_specs=[SM, SM] + [HB] * 8,
        out_specs=(HB, VM),
        scratch_shapes=[pltpu.VMEM(x.shape, x.dtype) for x in (index, weight, table, spectrum, grid)]
        + [pltpu.SMEM(x.shape, x.dtype) for x in (orient, row, col)]
        + [
            pltpu.SemaphoreType.DMA((12,)),
            pltpu.VMEM(table.shape, F32),
            pltpu.VMEM(index.shape, F32),
            pltpu.VMEM((2,) + index.shape, F32),
            pltpu.VMEM((2 * ROWS, HALF, LANES), F32),
            pltpu.VMEM((GRID * TILES * BINS // LANES, LANES), F32),
            pltpu.VMEM((4 * BLOCKS, TILES, LANES), F32),
            pltpu.VMEM((TILES * XROWS, LANES), F32),
            pltpu.VMEM((TILES, XROWS, LANES), BF),
        ],
        compiler_params=pltpu.CompilerParams(vmem_limit_bytes=VMEM_LIMIT),
        name="prepare",
    )(rot, count, *[stay(x) for x in (index, weight, table, spectrum, grid, orient, row, col)])


def arrange(spectrum, filt, tabx):
    def kernel(spec_hbm, filt_hbm, tabx_hbm, out_ref, wide_ref, spec_ref, filt_ref, tabx_ref, spec_s, sems):
        pairs = ((spec_hbm, spec_ref), (filt_hbm, filt_ref), (tabx_hbm, tabx_ref))
        copies = [pltpu.make_async_copy(a, b, sems.at[i]) for i, (a, b) in enumerate(pairs)]
        for copy in copies:
            copy.start()
        for copy in copies:
            copy.wait()
        for b in range(ROWS):
            cols = slice(b * LANES, (b + 1) * LANES)
            for c, value in enumerate((spec_ref[0, :, cols], spec_ref[1, :, cols], filt_ref[:, cols])):
                spec_s[c * ROWS + b] = value.astype(F32)
        for c in range(3):
            for j in range(ROWS):
                for b in range(ROWS):
                    out_ref[c * BLOCKS + j * ROWS + b] = every(spec_s.at[c * ROWS + b], j, ROWS)
        cosv, sinv = tabx_ref[:, :DFT], tabx_ref[:, DFT:]
        wide_ref[:DFT, :DFT] = cosv
        wide_ref[:DFT, DFT:] = sinv
        wide_ref[DFT:, :DFT] = -sinv
        wide_ref[DFT:, DFT:] = cosv

    return pl.pallas_call(
        kernel,
        out_shape=(
            jax.ShapeDtypeStruct((3 * BLOCKS, TILES, LANES), F32),
            jax.ShapeDtypeStruct((2 * DFT, 2 * DFT), BF),
        ),
        in_specs=[HB] * 3,
        out_specs=(VM, VM),
        scratch_shapes=[pltpu.VMEM(x.shape, BF) for x in (spectrum, filt, tabx)]
        + [pltpu.VMEM((3 * ROWS, HALF, LANES), F32), pltpu.SemaphoreType.DMA((3,))],
        compiler_params=pltpu.CompilerParams(vmem_limit_bytes=VMEM_LIMIT),
        name="arrange",
    )(*[stay(x) for x in (spectrum, filt, tabx)])


def correlate(place, own, other, blocks, wide, back):
    def kernel(
        at_ref, own_ref, other_ref, block_ref, wide_ref, back_hbm, keep_hbm, send_ref,
        sl_s, back_ref, keep_ref, sems,
    ):
        fetch = pltpu.make_async_copy(back_hbm.at[at_ref[0]], back_ref, sems.at[2])
        fetch.start()
        leave = [pltpu.make_async_copy(keep_ref.at[o], keep_hbm.at[o], sems.at[o]) for o in range(2)]
        sl_s[at_ref[1]] = own_ref[...].astype(F32).reshape(TILES * SROWS, LANES)
        sl_s[1 - at_ref[1]] = other_ref[...].astype(F32).reshape(TILES * SROWS, LANES)
        real = [[None] * (ROWS * ROWS) for _ in range(2)]
        imag = [[None] * (ROWS * ROWS) for _ in range(2)]
        for j in range(ROWS):
            for b in range(ROWS):
                mr, mi, c = [block_ref[k * BLOCKS + j * ROWS + b] for k in range(3)]
                for o in range(2):
                    row = o * BLOCKS + j * ROWS + b
                    cr = c * every(sl_s.at[0], row, SROWS)
                    ci = c * every(sl_s.at[1], row, SROWS)
                    real[o][j * ROWS + b] = (mr * cr + mi * ci).astype(BF)
                    imag[o][j * ROWS + b] = (mi * cr - mr * ci).astype(BF)
        cross = jnp.concatenate(
            [
                jnp.concatenate(real[o][j * ROWS : (j + 1) * ROWS] + imag[o][j * ROWS : (j + 1) * ROWS], axis=1)
                for o in range(2)
                for j in range(ROWS)
            ],
            axis=0,
        )
        halfimg = lax.dot_general(cross, wide_ref[...], NN, preferred_element_type=F32).astype(BF)
        fetch.wait()
        table = back_ref[...]
        low = at_ref[0] == 0
        for o in range(2):
            rows = halfimg[o * HALF : (o + 1) * HALF]
            both = jnp.concatenate([rows[:, :DFT], rows[:, DFT:]], axis=0)
            sums = lax.dot_general(table, both, NN, preferred_element_type=F32)
            left = jnp.concatenate([sums[:HALF, :HALF], sums[HALF:, :HALF]], axis=1)
            right = jnp.concatenate([sums[:HALF, HALF:], sums[HALF:, HALF:]], axis=1)
            keep_ref[o] = jnp.where(low, left, right).astype(BF)
            leave[o].start()
            send_ref[o] = jnp.where(low, right, left).astype(BF)
        for copy in leave:
            copy.wait()

    shape = jax.ShapeDtypeStruct((2, HALF, DFT), BF)
    return pl.pallas_call(
        kernel,
        out_shape=(shape, shape),
        in_specs=[SM] + [VM] * 4 + [HB],
        out_specs=(HB, VM),
        scratch_shapes=[
            pltpu.VMEM((2, TILES * SROWS, LANES), F32),
            pltpu.VMEM((DFT, DFT), BF),
            pltpu.VMEM((2, HALF, DFT), BF),
            pltpu.SemaphoreType.DMA((3,)),
        ],
        compiler_params=pltpu.CompilerParams(vmem_limit_bytes=VMEM_LIMIT),
        name="correlate",
    )(place, own, other, blocks, wide, stay(back))


def score(place, got, share, slices, tabx):
    def kernel(
        at_ref, got_ref, share_ref, slice_ref, tabx_ref,
        out_ref, place_hbm, got_s, share_s, place_s, place_ref, sem, out_s,
    ):
        got_s[...] = got_ref[...].astype(F32).reshape(got_s.shape)
        side = at_ref[2] & 1
        share_s[1 - side] = share_ref[...].astype(F32).reshape(TILES * SHARE, LANES)
        for r in range(SHARE):
            share_s[side, pl.ds(r, TILES, stride=SHARE), :] = every(got_s, r, XROWS)

        def sent(row):
            if row < 2 * SHARE:
                return every(share_s.at[row // SHARE], row % SHARE, SHARE)
            return every(got_s, REST + row - 2 * SHARE, XROWS)

        meta = every(got_s, META, XROWS)
        lane = lax.broadcasted_iota(I32, (TILES, DFT), 1).astype(F32)
        count = meta[:, 20:21]
        tri_r = lax.broadcasted_iota(I32, (TILES, TILES), 0)
        tri_c = lax.broadcasted_iota(I32, (TILES, TILES), 1)
        before = jnp.where(tri_c < tri_r, 1.0, 0.0).astype(BF)
        spread = jnp.broadcast_to(count, (TILES, LANES)).astype(BF)
        offset = lax.dot_general(before, spread, NN, preferred_element_type=F32)[:, 0:1]
        hot_x, hot_y, place = [], [], []
        for i in range(SLOTS):
            y0 = meta[:, 5 * i + 1 : 5 * i + 2] * BASE + meta[:, 5 * i + 2 : 5 * i + 3]
            x0 = meta[:, 5 * i + 3 : 5 * i + 4] * BASE + meta[:, 5 * i + 4 : 5 * i + 5]
            hot_x.append(jnp.where(lane == x0, 1.0, 0.0).astype(BF))
            hot_y.append(jnp.where(lane == y0, 1.0, 0.0).astype(BF))
            seat = jnp.where(count > float(i), offset + float(i), -1.0)
            hot = jnp.where(lane[:, :256] == seat, 1.0, 0.0)
            for h in range(2):
                place_s[h, pl.ds(i, TILES, stride=SLOTS), :] = hot[:, h * LANES : (h + 1) * LANES]
            place.append(hot.astype(BF))
        place_ref[...] = place_s[...].astype(BF)
        leave = pltpu.make_async_copy(place_ref, place_hbm, sem)
        leave.start()
        hot_x = jnp.concatenate(hot_x, axis=0)
        hot_y = jnp.concatenate(hot_y, axis=0)
        place = jnp.concatenate(place, axis=0)
        wave = lax.dot_general(hot_x, tabx_ref[...], NN, preferred_element_type=F32)
        cx, sx = wave[:, :DFT], wave[:, DFT:]
        line = lax.broadcasted_iota(I32, (16, DFT), 0) + at_ref[3]
        pick = jnp.where(lax.broadcasted_iota(I32, (16, DFT), 1) == line, 1.0, 0.0).astype(BF)
        taby = lax.dot_general(pick, tabx_ref[...], NN, preferred_element_type=F32).astype(BF)
        tilt_c = lax.dot_general(hot_y, taby[:, :DFT], NT, preferred_element_type=F32)
        tilt_s = lax.dot_general(hot_y, taby[:, DFT:], NT, preferred_element_type=F32)
        pieces = [[] for _ in range(SLOTS)]
        second = [jnp.broadcast_to(meta[:, 5 * i : 5 * i + 1], (TILES, LANES)) > 0.5 for i in range(SLOTS)]
        for j in range(ROWS):
            cosines = jnp.broadcast_to(tilt_c[:, j : j + 1], (SLOTS * TILES, LANES))
            sines = jnp.broadcast_to(tilt_s[:, j : j + 1], (SLOTS * TILES, LANES))
            for b in range(ROWS):
                r = j * ROWS + b
                cols = slice(b * LANES, (b + 1) * LANES)
                mr = sent(r)
                mi = sent(BLOCKS + r)
                plain = []
                for o in range(2):
                    sr = slice_ref[0, o * BLOCKS + r : o * BLOCKS + r + 1, :]
                    si = slice_ref[1, o * BLOCKS + r : o * BLOCKS + r + 1, :]
                    plain.append(((mr * sr + mi * si).astype(BF).astype(F32), (mi * sr - mr * si).astype(BF).astype(F32)))
                for i in range(SLOTS):
                    at = slice(i * TILES, (i + 1) * TILES)
                    pr = jnp.where(second[i], plain[1][0], plain[0][0])
                    pi = jnp.where(second[i], plain[1][1], plain[0][1])
                    cy, sy = cosines[at], sines[at]
                    wx, vx = cx[at, cols], sx[at, cols]
                    pieces[i].append(cy * (pr * wx - pi * vx) - sy * (pr * vx + pi * wx))
        shifted = jnp.concatenate(
            [
                jnp.concatenate(pieces[i][j * ROWS : (j + 1) * ROWS], axis=1).astype(BF)
                for j in range(ROWS)
                for i in range(SLOTS)
            ],
            axis=0,
        )
        bin_of = lax.shift_right_logical(lax.broadcasted_iota(I32, (DFT, LANES), 0), 2)
        group = jnp.where(bin_of == lax.broadcasted_iota(I32, (DFT, LANES), 1), 1.0, 0.0).astype(BF)
        sums = lax.dot_general(shifted, group, NN, preferred_element_type=F32)
        count_rows = SLOTS * TILES
        binned = jnp.concatenate(
            [sums[j * count_rows : (j + 1) * count_rows, : DFT // 4] for j in range(ROWS)], axis=1
        ).astype(BF)
        grid = jnp.concatenate([sent(2 * BLOCKS + r).astype(BF) for r in range(2 * BLOCKS)], axis=1)
        values = jnp.concatenate([grid[:, q * BINS : (q + 1) * BINS] for q in range(GRID)], axis=0)
        scores = lax.dot_general(values, binned, NT, preferred_element_type=F32).astype(BF)
        packed = lax.dot_general(scores, place, NN, preferred_element_type=F32)
        lanes = lax.broadcasted_iota(I32, (TILES, LANES), 1)
        extra = jnp.zeros((TILES, LANES), F32)
        for q in range(GRID):
            block = packed[q * TILES : (q + 1) * TILES]
            out_s[:, q // SPAN, q % SPAN * LANES : (q % SPAN + 1) * LANES] = block[:, :LANES]
            extra = jnp.where(lanes == q, block[:, LANES : LANES + 1], extra)
        out_s[:, 1, (SPAN - 2) * LANES : (SPAN - 1) * LANES] = extra
        out_s[:, 1, (SPAN - 1) * LANES :] = jnp.zeros((TILES, LANES), F32)
        out_ref[...] = out_s[...].astype(BF)
        leave.wait()

    return pl.pallas_call(
        kernel,
        out_shape=(
            jax.ShapeDtypeStruct((TILES, 2, SPAN * LANES), BF),
            jax.ShapeDtypeStruct((2, SLOTS * TILES, LANES), BF),
        ),
        in_specs=[SM] + [VM] * 4,
        out_specs=(VM, HB),
        scratch_shapes=[pltpu.VMEM((TILES * XROWS, LANES), F32), pltpu.VMEM((2, TILES * SHARE, LANES), F32), pltpu.VMEM((2, SLOTS * TILES, LANES), F32), pltpu.VMEM((2, SLOTS * TILES, LANES), BF), pltpu.SemaphoreType.DMA, pltpu.VMEM((TILES, 2, SPAN * LANES), F32)],
        compiler_params=pltpu.CompilerParams(vmem_limit_bytes=VMEM_LIMIT),
        cost_estimate=pl.CostEstimate(flops=6_000_000_000, transcendentals=0, bytes_accessed=8_000_000),
        name="score",
    )(place, got, share, slices, tabx)


def expand(place, mine, other):
    def kernel(place_ref, mine_ref, other_ref, refined_ref, top_ref):
        both = mine_ref[...] + other_ref[...]
        place = jnp.concatenate([place_ref[0], place_ref[1]], axis=1)
        lane = lax.broadcasted_iota(I32, (GRID, LANES), 1)
        row = lax.broadcasted_iota(I32, (GRID, LANES), 0)
        sums = [both[r // SPAN : r // SPAN + 1, r % SPAN * LANES : (r % SPAN + 1) * LANES] for r in range(GRID + 1)]
        last = jnp.broadcast_to(sums[GRID], (GRID, LANES))
        last = jnp.sum(jnp.where(lane == row, last, 0.0), axis=1, keepdims=True)
        rest = jnp.concatenate([jnp.concatenate(sums[:GRID], axis=0), jnp.where(lane == 0, last, 0.0)], axis=1) * (1.0 / DFT)
        parts = []
        for _ in range(3):
            parts.append(rest.astype(BF).astype(F32))
            rest = rest - parts[-1]
        parts = jnp.concatenate(parts, axis=0).astype(BF)
        out = lax.dot_general(parts, place, NT, preferred_element_type=F32)
        refined = (out[:GRID] + out[GRID : 2 * GRID]) + out[2 * GRID :]
        refined_ref[...] = refined
        top = jnp.max(refined, axis=0, keepdims=True)
        top_ref[...] = jnp.broadcast_to(top[None], top_ref.shape)

    return pl.pallas_call(
        kernel,
        out_shape=(
            jax.ShapeDtypeStruct((GRID, SLOTS * TILES), F32),
            jax.ShapeDtypeStruct((TILES, 1, SLOTS * TILES), F32),
        ),
        in_specs=[VM] * 3,
        out_specs=(VM, VM),
        compiler_params=pltpu.CompilerParams(vmem_limit_bytes=VMEM_LIMIT),
        name="expand",
    )(place, mine, other)


def finish(parts):
    def kernel(*refs):
        ins, (top_ref, mean_ref) = refs[:4], refs[4:]
        for b in range(ROWS):
            cols = slice(b * LANES, (b + 1) * LANES)
            tops = [ref[0, :, cols].astype(F32) for ref in ins]
            sums = [ref[1, :, cols].astype(F32) for ref in ins]
            top_ref[pl.ds(b, HALF, stride=ROWS), :] = jnp.maximum(
                jnp.maximum(tops[0], tops[1]), jnp.maximum(tops[2], tops[3])
            )
            total = (sums[0] + sums[1]) + (sums[2] + sums[3])
            mean_ref[pl.ds(b, HALF, stride=ROWS), :] = total * (1.0 / ORIENTS)

    shape = jax.ShapeDtypeStruct((ROWS * HALF, LANES), F32)
    return pl.pallas_call(
        kernel,
        out_shape=(shape, shape),
        in_specs=[VM] * 4,
        out_specs=(VM, VM),
        cost_estimate=pl.CostEstimate(flops=1, transcendentals=0, bytes_accessed=1),
        compiler_params=pltpu.CompilerParams(vmem_limit_bytes=VMEM_LIMIT),
        name="finish",
    )(*parts)


def exchange(x, axis, bit):
    size = lax.axis_size(axis)
    return lax.ppermute(x, axis, [(k, k ^ bit) for k in range(size)])


def shards(
    interp_index,
    interp_weight,
    volume,
    spectrum,
    ctf_filter,
    peak_count,
    peak_orient,
    peak_row,
    peak_col,
    ctf_grid,
):
    back, tabx = [jnp.asarray(t) for t in tables()]
    nar = lax.axis_index("nar")
    tile = lax.axis_index("tile")

    grid = ctf_grid.reshape(GRID, TILES * BINS)
    spec = spectrum.reshape(2, HALF, DFT)
    filt = ctf_filter.reshape(HALF, DFT)
    rot = lax.axis_index("rot").reshape(1)
    blocks, slices = prepare(
        rot,
        interp_index.reshape(-1, LANES),
        interp_weight.transpose(0, 2, 3, 1, 4),
        volume.reshape(2, -1),
        spec,
        grid,
        peak_orient,
        peak_row,
        peak_col,
        peak_count,
    )
    slices, nar, tile = lax.optimization_barrier((slices, nar, tile))
    place_at = jnp.stack([nar, tile % 2, rot[0], (nar * TILES + tile) * ROWS])
    rows, wide = arrange(spec, filt, tabx)
    got = lax.all_to_all(blocks, "tile", 0, 0, tiled=True)
    got, rows, wide, place_at = lax.optimization_barrier((got, rows, wide, place_at))
    share, mine = exchange(got[:, :SHARE], "rot", 1), got[:, SHARE:]
    other = exchange(mine, "tile", 1)
    keep, send = correlate(place_at, mine, other, rows, wide, back)
    got, send = lax.optimization_barrier((got, send))
    extra_rows = exchange(send, "nar", 1)
    packed, place = score(place_at, got, share, slices, tabx)
    sums = lax.all_to_all(packed, "tile", 0, 0, tiled=True)

    corr = (keep.astype(F32) + extra_rows.astype(F32)) * (1.0 / DFT)
    stats = jnp.stack([jnp.maximum(corr[0], corr[1]), corr[0] + corr[1]]).astype(BF)
    others = [exchange(stats, "rot", bit) for bit in (1, 2, 3)]

    sums = jnp.sum(sums.astype(F32), axis=0)
    refined, tops = expand(place, sums, exchange(sums, "nar", 1))
    tops = lax.all_to_all(tops, "tile", 0, 0)
    peak, mean = finish([stats] + others)
    tops, peak, mean = lax.optimization_barrier((tops, peak, mean))
    best = jnp.max(tops, axis=0)
    return (
        peak.reshape(1, 1, -1),
        mean.reshape(1, 1, -1),
        refined.T.reshape(1, SLOTS * TILES, GRID),
        best,
    )


def solution(mesh):
    return jax.shard_map(
        shards,
        mesh=mesh,
        in_specs=(
            P(None, "rot", "nar", "tile", None),
            P(None, "rot", "nar", "tile", None),
            P(None, "nar", "tile", None),
            P(None, "tile", "nar", None, None),
            P("tile", "nar", None, None),
            P("rot", "tile"),
            P(("rot", "tile")),
            P(("rot", "tile")),
            P(("rot", "tile")),
            P("tile", "nar", None),
        ),
        out_specs=(
            P("tile", "nar", None),
            P("tile", "nar", None),
            P("rot", None, "tile"),
            P("rot", None),
        ),
        check_vma=False,
    )
```

```python
import jax
import jax.numpy as jnp
import numpy as np
from jax import lax
from jax.experimental import pallas as pl
from jax.experimental.pallas import tpu as pltpu
from jax.sharding import PartitionSpec as P

BF = jnp.bfloat16
F32 = jnp.float32
I32 = jnp.int32
LANES = 128
DFT = 384
HALF = 192
ROWS = 3
TILES = 64
SLOTS = 4
WIDE = ROWS * DFT
BINS = 288
GRID = 8
BASE = 16
BLOCKS = 9
XROWS = 40
SROWS = 24
SHARE = 16
SPAN = 5
ORIENTS = 8
REST = SHARE + 2 * BLOCKS
META = REST + 4 * BLOCKS - 2 * SHARE
VMEM_LIMIT = 16 * 1024 * 1024

VM = pl.BlockSpec(memory_space=pltpu.VMEM)
SM = pl.BlockSpec(memory_space=pltpu.SMEM)
HB = pl.BlockSpec(memory_space=pltpu.HBM)
NN = (((1,), (0,)), ((), ()))
NT = (((1,), (1,)), ((), ()))


def bf(x):
    return np.asarray(x, np.float32).astype(jnp.bfloat16)


def tables():
    steps = np.arange(DFT)
    phase = (steps[:, None] * steps[None, :] % DFT) * (2.0 * np.pi / DFT)
    cosv, sinv = np.cos(phase), np.sin(phase)
    rows = np.concatenate([steps[0::2], steps[1::2]])
    order = np.array([ROWS * t + j for j in range(ROWS) for t in range(TILES)])
    back = np.zeros((2, DFT, 2 * HALF), np.float32)
    for n in range(2):
        back[n, :, :HALF] = cosv[rows][:, n * HALF + order]
        back[n, :, HALF:] = -sinv[rows][:, n * HALF + order]
    return bf(back), bf(np.concatenate([cosv, sinv], 1))


def stay(x):
    return pltpu.with_memory_space_constraint(x, pltpu.HBM)


def every(ref, row, step):
    return ref[pl.ds(row, TILES, stride=step), :]


def prepare(rot, index, weight, table, spectrum, grid, orient, row, col, count):
    def kernel(
        rot_ref, count_ref, *refs,
    ):
        sources, (out_hbm, own_ref), scratch = refs[:8], refs[8:10], refs[10:]
        targets, (sems, table_s, weight_s, value_s, spec_s, grid_s, all_s, out_s, out_ref) = scratch[:8], scratch[8:]
        copies = [pltpu.make_async_copy(a, b, sems.at[i]) for i, (a, b) in enumerate(zip(sources, targets))]
        for copy in copies:
            copy.start()
        index_ref, weight_ref, table_ref, spec_ref, grid_ref, orient_ref, row_ref, col_ref = targets
        for copy in copies[:3]:
            copy.wait()
        table_s[...] = table_ref[...].astype(F32)
        for k in range(8):
            for j in range(ROWS):
                w = weight_ref[k, 0, j].astype(F32)
                for b in range(ROWS):
                    at = pl.ds(k * 2 * BLOCKS + j * ROWS + b, 2, stride=BLOCKS)
                    weight_s[at, :] = w[:, b * LANES : (b + 1) * LANES]

        def step(v, carry):
            rows = pl.ds(pl.multiple_of(v * 8, 8), 8)
            entry = index_ref[rows, :]
            low = entry & (LANES - 1)
            high = lax.shift_right_logical(entry, 7)
            bits = [(lax.shift_right_logical(high, b) & 1) == 1 for b in range(5)]

            def pick(c, level, first):
                if level < 0:
                    line = table_s[c : c + 1, first * LANES : (first + 1) * LANES]
                    return jnp.take_along_axis(jnp.broadcast_to(line, (8, LANES)), low, axis=1)
                return jnp.where(
                    bits[level],
                    pick(c, level - 1, first + (1 << level)),
                    pick(c, level - 1, first),
                )

            for c in range(2):
                value_s[c, rows, :] = pick(c, 4, 0) * weight_s[rows, :]
            return carry

        lax.fori_loop(0, 2 * BLOCKS, step, 0, unroll=9)
        for c in range(2):
            total = value_s[c, 0 : 2 * BLOCKS, :]
            for k in range(1, 8):
                total = total + value_s[c, k * 2 * BLOCKS : (k + 1) * 2 * BLOCKS, :]
            own_ref[c] = total.astype(BF).astype(F32)

        for copy in copies[3:]:
            copy.wait()
        odd = (lax.broadcasted_iota(I32, (TILES, LANES), 0) & 1) == 1
        for r in range(2 * BLOCKS):
            row = jnp.where(odd, own_ref[1, r : r + 1, :], own_ref[0, r : r + 1, :])
            out_s[pl.ds(SHARE + r, TILES, stride=XROWS), :] = row
        for c in range(2):
            for b in range(ROWS):
                spec_s[c * ROWS + b] = spec_ref[c, :, b * LANES : (b + 1) * LANES].astype(F32)
        for c in range(2):
            for j in range(ROWS):
                for b in range(ROWS):
                    all_s[c * BLOCKS + j * ROWS + b] = spec_s[c * ROWS + b, pl.ds(j, TILES, stride=ROWS), :]
        for k in range(TILES * BINS // LANES):
            grid_s[k * GRID : (k + 1) * GRID, :] = grid_ref[:, k * LANES : (k + 1) * LANES].astype(F32)
        for a in range(4):
            first, shift = divmod(a * BINS, LANES)
            pieces = []
            for q in range(GRID):
                blocks = [
                    grid_s[pl.ds((first + k) * GRID + q, TILES // 4, stride=BLOCKS * GRID), :] for k in range(3)
                ]
                pieces.append(jnp.concatenate(blocks, axis=1)[:, shift : shift + BINS])
            row = jnp.concatenate(pieces, axis=1)
            for r in range(2 * BLOCKS):
                all_s[2 * BLOCKS + r, pl.ds(a, TILES // 4, stride=4), :] = row[:, r * LANES : (r + 1) * LANES]
        for r in range(SHARE):
            out_s[pl.ds(r, TILES, stride=XROWS), :] = all_s[(rot_ref[0] & 1) * SHARE + r]
        for r in range(META - REST):
            out_s[pl.ds(REST + r, TILES, stride=XROWS), :] = all_s[2 * SHARE + r]
        lane = lax.broadcasted_iota(I32, (1, LANES), 1)
        fields = jnp.where(lane == 5 * SLOTS, count_ref[0, 0], 0)
        for i in range(SLOTS):
            y, x = row_ref[i], col_ref[i]
            items = (orient_ref[i], y >> 4, y & (BASE - 1), x >> 4, x & (BASE - 1))
            for k, item in enumerate(items):
                fields = jnp.where(lane == 5 * i + k, item, fields)
        fields = jnp.broadcast_to(fields.astype(F32), (TILES, LANES))
        for r in range(META, XROWS):
            out_s[pl.ds(r, TILES, stride=XROWS), :] = fields
        piece = TILES // 4
        leave = []
        for k in range(4):
            rows = out_s[k * piece * XROWS : (k + 1) * piece * XROWS, :]
            out_ref[k * piece : (k + 1) * piece] = rows.astype(BF).reshape(piece, XROWS, LANES)
            at = pl.ds(k * piece, piece)
            leave.append(pltpu.make_async_copy(out_ref.at[at], out_hbm.at[at], sems.at[8 + k]))
            leave[-1].start()
        for copy in leave:
            copy.wait()

    return pl.pallas_call(
        kernel,
        out_shape=(
            jax.ShapeDtypeStruct((TILES, XROWS, LANES), BF),
            jax.ShapeDtypeStruct((2, 2 * BLOCKS, LANES), F32),
        ),
        in_specs=[SM, SM] + [HB] * 8,
        out_specs=(HB, VM),
        scratch_shapes=[pltpu.VMEM(x.shape, x.dtype) for x in (index, weight, table, spectrum, grid)]
        + [pltpu.SMEM(x.shape, x.dtype) for x in (orient, row, col)]
        + [
            pltpu.SemaphoreType.DMA((12,)),
            pltpu.VMEM(table.shape, F32),
            pltpu.VMEM(index.shape, F32),
            pltpu.VMEM((2,) + index.shape, F32),
            pltpu.VMEM((2 * ROWS, HALF, LANES), F32),
            pltpu.VMEM((GRID * TILES * BINS // LANES, LANES), F32),
            pltpu.VMEM((4 * BLOCKS, TILES, LANES), F32),
            pltpu.VMEM((TILES * XROWS, LANES), F32),
            pltpu.VMEM((TILES, XROWS, LANES), BF),
        ],
        compiler_params=pltpu.CompilerParams(vmem_limit_bytes=VMEM_LIMIT),
        name="prepare",
    )(rot, count, *[stay(x) for x in (index, weight, table, spectrum, grid, orient, row, col)])


def arrange(spectrum, filt, tabx):
    def kernel(spec_hbm, filt_hbm, tabx_hbm, out_ref, wide_ref, spec_ref, filt_ref, tabx_ref, spec_s, sems):
        pairs = ((spec_hbm, spec_ref), (filt_hbm, filt_ref), (tabx_hbm, tabx_ref))
        copies = [pltpu.make_async_copy(a, b, sems.at[i]) for i, (a, b) in enumerate(pairs)]
        for copy in copies:
            copy.start()
        for copy in copies:
            copy.wait()
        for b in range(ROWS):
            cols = slice(b * LANES, (b + 1) * LANES)
            for c, value in enumerate((spec_ref[0, :, cols], spec_ref[1, :, cols], filt_ref[:, cols])):
                spec_s[c * ROWS + b] = value.astype(F32)
        for c in range(3):
            for j in range(ROWS):
                for b in range(ROWS):
                    out_ref[c * BLOCKS + j * ROWS + b] = every(spec_s.at[c * ROWS + b], j, ROWS)
        cosv, sinv = tabx_ref[:, :DFT], tabx_ref[:, DFT:]
        wide_ref[:DFT, :DFT] = cosv
        wide_ref[:DFT, DFT:] = sinv
        wide_ref[DFT:, :DFT] = -sinv
        wide_ref[DFT:, DFT:] = cosv

    return pl.pallas_call(
        kernel,
        out_shape=(
            jax.ShapeDtypeStruct((3 * BLOCKS, TILES, LANES), F32),
            jax.ShapeDtypeStruct((2 * DFT, 2 * DFT), BF),
        ),
        in_specs=[HB] * 3,
        out_specs=(VM, VM),
        scratch_shapes=[pltpu.VMEM(x.shape, BF) for x in (spectrum, filt, tabx)]
        + [pltpu.VMEM((3 * ROWS, HALF, LANES), F32), pltpu.SemaphoreType.DMA((3,))],
        compiler_params=pltpu.CompilerParams(vmem_limit_bytes=VMEM_LIMIT),
        name="arrange",
    )(*[stay(x) for x in (spectrum, filt, tabx)])


def correlate(place, own, other, blocks, wide, back):
    def kernel(
        at_ref, own_ref, other_ref, block_ref, wide_ref, back_hbm, keep_hbm, send_ref,
        sl_s, back_ref, keep_ref, sems,
    ):
        fetch = pltpu.make_async_copy(back_hbm.at[at_ref[0]], back_ref, sems.at[2])
        fetch.start()
        leave = [pltpu.make_async_copy(keep_ref.at[o], keep_hbm.at[o], sems.at[o]) for o in range(2)]
        sl_s[at_ref[1]] = own_ref[...].astype(F32).reshape(TILES * SROWS, LANES)
        sl_s[1 - at_ref[1]] = other_ref[...].astype(F32).reshape(TILES * SROWS, LANES)
        real = [[None] * (ROWS * ROWS) for _ in range(2)]
        imag = [[None] * (ROWS * ROWS) for _ in range(2)]
        for j in range(ROWS):
            for b in range(ROWS):
                mr, mi, c = [block_ref[k * BLOCKS + j * ROWS + b] for k in range(3)]
                for o in range(2):
                    row = o * BLOCKS + j * ROWS + b
                    cr = c * every(sl_s.at[0], row, SROWS)
                    ci = c * every(sl_s.at[1], row, SROWS)
                    real[o][j * ROWS + b] = (mr * cr + mi * ci).astype(BF)
                    imag[o][j * ROWS + b] = (mi * cr - mr * ci).astype(BF)
        cross = jnp.concatenate(
            [
                jnp.concatenate(real[o][j * ROWS : (j + 1) * ROWS] + imag[o][j * ROWS : (j + 1) * ROWS], axis=1)
                for o in range(2)
                for j in range(ROWS)
            ],
            axis=0,
        )
        halfimg = lax.dot_general(cross, wide_ref[...], NN, preferred_element_type=F32).astype(BF)
        fetch.wait()
        table = back_ref[...]
        low = at_ref[0] == 0
        for o in range(2):
            rows = halfimg[o * HALF : (o + 1) * HALF]
            both = jnp.concatenate([rows[:, :DFT], rows[:, DFT:]], axis=0)
            sums = lax.dot_general(table, both, NN, preferred_element_type=F32)
            left = jnp.concatenate([sums[:HALF, :HALF], sums[HALF:, :HALF]], axis=1)
            right = jnp.concatenate([sums[:HALF, HALF:], sums[HALF:, HALF:]], axis=1)
            keep_ref[o] = jnp.where(low, left, right).astype(BF)
            leave[o].start()
            send_ref[o] = jnp.where(low, right, left).astype(BF)
        for copy in leave:
            copy.wait()

    shape = jax.ShapeDtypeStruct((2, HALF, DFT), BF)
    return pl.pallas_call(
        kernel,
        out_shape=(shape, shape),
        in_specs=[SM] + [VM] * 4 + [HB],
        out_specs=(HB, VM),
        scratch_shapes=[
            pltpu.VMEM((2, TILES * SROWS, LANES), F32),
            pltpu.VMEM((DFT, DFT), BF),
            pltpu.VMEM((2, HALF, DFT), BF),
            pltpu.SemaphoreType.DMA((3,)),
        ],
        compiler_params=pltpu.CompilerParams(vmem_limit_bytes=VMEM_LIMIT),
        name="correlate",
    )(place, own, other, blocks, wide, stay(back))


def score(place, got, share, slices, tabx):
    def kernel(
        at_ref, got_ref, share_ref, slice_ref, tabx_ref,
        out_hbm, place_hbm, got_s, share_s, place_s, place_ref, sems, out_s, out_ref,
    ):
        got_s[...] = got_ref[...].astype(F32).reshape(got_s.shape)
        side = at_ref[2] & 1
        share_s[1 - side] = share_ref[...].astype(F32).reshape(TILES * SHARE, LANES)
        for r in range(SHARE):
            share_s[side, pl.ds(r, TILES, stride=SHARE), :] = every(got_s, r, XROWS)

        def sent(row):
            if row < 2 * SHARE:
                return every(share_s.at[row // SHARE], row % SHARE, SHARE)
            return every(got_s, REST + row - 2 * SHARE, XROWS)

        meta = every(got_s, META, XROWS)
        lane = lax.broadcasted_iota(I32, (TILES, DFT), 1).astype(F32)
        count = meta[:, 20:21]
        tri_r = lax.broadcasted_iota(I32, (TILES, TILES), 0)
        tri_c = lax.broadcasted_iota(I32, (TILES, TILES), 1)
        before = jnp.where(tri_c < tri_r, 1.0, 0.0).astype(BF)
        spread = jnp.broadcast_to(count, (TILES, LANES)).astype(BF)
        offset = lax.dot_general(before, spread, NN, preferred_element_type=F32)[:, 0:1]
        hot_x, hot_y, place = [], [], []
        for i in range(SLOTS):
            y0 = meta[:, 5 * i + 1 : 5 * i + 2] * BASE + meta[:, 5 * i + 2 : 5 * i + 3]
            x0 = meta[:, 5 * i + 3 : 5 * i + 4] * BASE + meta[:, 5 * i + 4 : 5 * i + 5]
            hot_x.append(jnp.where(lane == x0, 1.0, 0.0).astype(BF))
            hot_y.append(jnp.where(lane == y0, 1.0, 0.0).astype(BF))
            seat = jnp.where(count > float(i), offset + float(i), -1.0)
            hot = jnp.where(lane[:, :256] == seat, 1.0, 0.0)
            for h in range(2):
                place_s[h, pl.ds(i, TILES, stride=SLOTS), :] = hot[:, h * LANES : (h + 1) * LANES]
            place.append(hot.astype(BF))
        place_ref[...] = place_s[...].astype(BF)
        leave = [pltpu.make_async_copy(place_ref, place_hbm, sems.at[0])]
        leave[0].start()
        hot_x = jnp.concatenate(hot_x, axis=0)
        hot_y = jnp.concatenate(hot_y, axis=0)
        place = jnp.concatenate(place, axis=0)
        wave = lax.dot_general(hot_x, tabx_ref[...], NN, preferred_element_type=F32)
        cx, sx = wave[:, :DFT], wave[:, DFT:]
        line = lax.broadcasted_iota(I32, (16, DFT), 0) + at_ref[3]
        pick = jnp.where(lax.broadcasted_iota(I32, (16, DFT), 1) == line, 1.0, 0.0).astype(BF)
        taby = lax.dot_general(pick, tabx_ref[...], NN, preferred_element_type=F32).astype(BF)
        tilt_c = lax.dot_general(hot_y, taby[:, :DFT], NT, preferred_element_type=F32)
        tilt_s = lax.dot_general(hot_y, taby[:, DFT:], NT, preferred_element_type=F32)
        pieces = [[] for _ in range(SLOTS)]
        second = [jnp.broadcast_to(meta[:, 5 * i : 5 * i + 1], (TILES, LANES)) > 0.5 for i in range(SLOTS)]
        for j in range(ROWS):
            cosines = jnp.broadcast_to(tilt_c[:, j : j + 1], (SLOTS * TILES, LANES))
            sines = jnp.broadcast_to(tilt_s[:, j : j + 1], (SLOTS * TILES, LANES))
            for b in range(ROWS):
                r = j * ROWS + b
                cols = slice(b * LANES, (b + 1) * LANES)
                mr = sent(r)
                mi = sent(BLOCKS + r)
                plain = []
                for o in range(2):
                    sr = slice_ref[0, o * BLOCKS + r : o * BLOCKS + r + 1, :]
                    si = slice_ref[1, o * BLOCKS + r : o * BLOCKS + r + 1, :]
                    plain.append(((mr * sr + mi * si).astype(BF).astype(F32), (mi * sr - mr * si).astype(BF).astype(F32)))
                for i in range(SLOTS):
                    at = slice(i * TILES, (i + 1) * TILES)
                    pr = jnp.where(second[i], plain[1][0], plain[0][0])
                    pi = jnp.where(second[i], plain[1][1], plain[0][1])
                    cy, sy = cosines[at], sines[at]
                    wx, vx = cx[at, cols], sx[at, cols]
                    pieces[i].append(cy * (pr * wx - pi * vx) - sy * (pr * vx + pi * wx))
        shifted = jnp.concatenate(
            [
                jnp.concatenate(pieces[i][j * ROWS : (j + 1) * ROWS], axis=1).astype(BF)
                for j in range(ROWS)
                for i in range(SLOTS)
            ],
            axis=0,
        )
        bin_of = lax.shift_right_logical(lax.broadcasted_iota(I32, (DFT, LANES), 0), 2)
        group = jnp.where(bin_of == lax.broadcasted_iota(I32, (DFT, LANES), 1), 1.0, 0.0).astype(BF)
        sums = lax.dot_general(shifted, group, NN, preferred_element_type=F32)
        count_rows = SLOTS * TILES
        binned = jnp.concatenate(
            [sums[j * count_rows : (j + 1) * count_rows, : DFT // 4] for j in range(ROWS)], axis=1
        ).astype(BF)
        grid = jnp.concatenate([sent(2 * BLOCKS + r).astype(BF) for r in range(2 * BLOCKS)], axis=1)
        values = jnp.concatenate([grid[:, q * BINS : (q + 1) * BINS] for q in range(GRID)], axis=0)
        scores = lax.dot_general(values, binned, NT, preferred_element_type=F32).astype(BF)
        packed = lax.dot_general(scores, place, NN, preferred_element_type=F32)
        lanes = lax.broadcasted_iota(I32, (TILES, LANES), 1)
        extra = jnp.zeros((TILES, LANES), F32)
        for q in range(GRID):
            block = packed[q * TILES : (q + 1) * TILES]
            out_s[:, q // SPAN, q % SPAN * LANES : (q % SPAN + 1) * LANES] = block[:, :LANES]
            extra = jnp.where(lanes == q, block[:, LANES : LANES + 1], extra)
        out_s[:, 1, (SPAN - 2) * LANES : (SPAN - 1) * LANES] = extra
        out_s[:, 1, (SPAN - 1) * LANES :] = jnp.zeros((TILES, LANES), F32)
        piece = TILES // 4
        for k in range(4):
            at = pl.ds(k * piece, piece)
            out_ref[k * piece : (k + 1) * piece] = out_s[k * piece : (k + 1) * piece].astype(BF)
            leave.append(pltpu.make_async_copy(out_ref.at[at], out_hbm.at[at], sems.at[1 + k]))
            leave[-1].start()
        for copy in leave:
            copy.wait()

    return pl.pallas_call(
        kernel,
        out_shape=(
            jax.ShapeDtypeStruct((TILES, 2, SPAN * LANES), BF),
            jax.ShapeDtypeStruct((2, SLOTS * TILES, LANES), BF),
        ),
        in_specs=[SM] + [VM] * 4,
        out_specs=(HB, HB),
        scratch_shapes=[pltpu.VMEM((TILES * XROWS, LANES), F32), pltpu.VMEM((2, TILES * SHARE, LANES), F32), pltpu.VMEM((2, SLOTS * TILES, LANES), F32), pltpu.VMEM((2, SLOTS * TILES, LANES), BF), pltpu.SemaphoreType.DMA((5,)), pltpu.VMEM((TILES, 2, SPAN * LANES), F32), pltpu.VMEM((TILES, 2, SPAN * LANES), BF)],
        compiler_params=pltpu.CompilerParams(vmem_limit_bytes=VMEM_LIMIT),
        cost_estimate=pl.CostEstimate(flops=6_000_000_000, transcendentals=0, bytes_accessed=8_000_000),
        name="score",
    )(place, got, share, slices, tabx)


def expand(place, mine, other):
    def kernel(place_ref, mine_ref, other_ref, refined_ref, top_ref):
        both = mine_ref[...] + other_ref[...]
        place = jnp.concatenate([place_ref[0], place_ref[1]], axis=1)
        lane = lax.broadcasted_iota(I32, (GRID, LANES), 1)
        row = lax.broadcasted_iota(I32, (GRID, LANES), 0)
        sums = [both[r // SPAN : r // SPAN + 1, r % SPAN * LANES : (r % SPAN + 1) * LANES] for r in range(GRID + 1)]
        last = jnp.broadcast_to(sums[GRID], (GRID, LANES))
        last = jnp.sum(jnp.where(lane == row, last, 0.0), axis=1, keepdims=True)
        rest = jnp.concatenate([jnp.concatenate(sums[:GRID], axis=0), jnp.where(lane == 0, last, 0.0)], axis=1) * (1.0 / DFT)
        parts = []
        for _ in range(3):
            parts.append(rest.astype(BF).astype(F32))
            rest = rest - parts[-1]
        parts = jnp.concatenate(parts, axis=0).astype(BF)
        out = lax.dot_general(parts, place, NT, preferred_element_type=F32)
        refined = (out[:GRID] + out[GRID : 2 * GRID]) + out[2 * GRID :]
        refined_ref[...] = refined
        top = jnp.max(refined, axis=0, keepdims=True)
        top_ref[...] = jnp.broadcast_to(top[None], top_ref.shape)

    return pl.pallas_call(
        kernel,
        out_shape=(
            jax.ShapeDtypeStruct((GRID, SLOTS * TILES), F32),
            jax.ShapeDtypeStruct((TILES, 1, SLOTS * TILES), F32),
        ),
        in_specs=[VM] * 3,
        out_specs=(VM, VM),
        compiler_params=pltpu.CompilerParams(vmem_limit_bytes=VMEM_LIMIT),
        name="expand",
    )(place, mine, other)


def finish(parts):
    def kernel(*refs):
        ins, (top_ref, mean_ref) = refs[:4], refs[4:]
        for b in range(ROWS):
            cols = slice(b * LANES, (b + 1) * LANES)
            tops = [ref[0, :, cols].astype(F32) for ref in ins]
            sums = [ref[1, :, cols].astype(F32) for ref in ins]
            top_ref[pl.ds(b, HALF, stride=ROWS), :] = jnp.maximum(
                jnp.maximum(tops[0], tops[1]), jnp.maximum(tops[2], tops[3])
            )
            total = (sums[0] + sums[1]) + (sums[2] + sums[3])
            mean_ref[pl.ds(b, HALF, stride=ROWS), :] = total * (1.0 / ORIENTS)

    shape = jax.ShapeDtypeStruct((ROWS * HALF, LANES), F32)
    return pl.pallas_call(
        kernel,
        out_shape=(shape, shape),
        in_specs=[VM] * 4,
        out_specs=(VM, VM),
        cost_estimate=pl.CostEstimate(flops=1, transcendentals=0, bytes_accessed=1),
        compiler_params=pltpu.CompilerParams(vmem_limit_bytes=VMEM_LIMIT),
        name="finish",
    )(*parts)


def exchange(x, axis, bit):
    size = lax.axis_size(axis)
    return lax.ppermute(x, axis, [(k, k ^ bit) for k in range(size)])


def shards(
    interp_index,
    interp_weight,
    volume,
    spectrum,
    ctf_filter,
    peak_count,
    peak_orient,
    peak_row,
    peak_col,
    ctf_grid,
):
    back, tabx = [jnp.asarray(t) for t in tables()]
    nar = lax.axis_index("nar")
    tile = lax.axis_index("tile")

    grid = ctf_grid.reshape(GRID, TILES * BINS)
    spec = spectrum.reshape(2, HALF, DFT)
    filt = ctf_filter.reshape(HALF, DFT)
    rot = lax.axis_index("rot").reshape(1)
    blocks, slices = prepare(
        rot,
        interp_index.reshape(-1, LANES),
        interp_weight.transpose(0, 2, 3, 1, 4),
        volume.reshape(2, -1),
        spec,
        grid,
        peak_orient,
        peak_row,
        peak_col,
        peak_count,
    )
    slices, nar, tile = lax.optimization_barrier((slices, nar, tile))
    place_at = jnp.stack([nar, tile % 2, rot[0], (nar * TILES + tile) * ROWS])
    rows, wide = arrange(spec, filt, tabx)
    got = lax.all_to_all(blocks, "tile", 0, 0, tiled=True)
    got, rows, wide, place_at = lax.optimization_barrier((got, rows, wide, place_at))
    share, mine = exchange(got[:, :SHARE], "rot", 1), got[:, SHARE:]
    other = exchange(mine, "tile", 1)
    keep, send = correlate(place_at, mine, other, rows, wide, back)
    got, send = lax.optimization_barrier((got, send))
    extra_rows = exchange(send, "nar", 1)
    packed, place = score(place_at, got, share, slices, tabx)
    sums = lax.all_to_all(packed, "tile", 0, 0, tiled=True)

    corr = (keep.astype(F32) + extra_rows.astype(F32)) * (1.0 / DFT)
    stats = jnp.stack([jnp.maximum(corr[0], corr[1]), corr[0] + corr[1]]).astype(BF)
    others = [exchange(stats, "rot", bit) for bit in (1, 2, 3)]

    sums = jnp.sum(sums.astype(F32), axis=0)
    refined, tops = expand(place, sums, exchange(sums, "nar", 1))
    tops = lax.all_to_all(tops, "tile", 0, 0)
    peak, mean = finish([stats] + others)
    tops, peak, mean = lax.optimization_barrier((tops, peak, mean))
    best = jnp.max(tops, axis=0)
    return (
        peak.reshape(1, 1, -1),
        mean.reshape(1, 1, -1),
        refined.T.reshape(1, SLOTS * TILES, GRID),
        best,
    )


def solution(mesh):
    return jax.shard_map(
        shards,
        mesh=mesh,
        in_specs=(
            P(None, "rot", "nar", "tile", None),
            P(None, "rot", "nar", "tile", None),
            P(None, "nar", "tile", None),
            P(None, "tile", "nar", None, None),
            P("tile", "nar", None, None),
            P("rot", "tile"),
            P(("rot", "tile")),
            P(("rot", "tile")),
            P(("rot", "tile")),
            P("tile", "nar", None),
        ),
        out_specs=(
            P("tile", "nar", None),
            P("tile", "nar", None),
            P("rot", None, "tile"),
            P("rot", None),
        ),
        check_vma=False,
    )
```
